128 devices in a mesh: ctx: 32 (over x, y, core), tp: 4 (over z).
Axes of the slice: x: 4, y: 4, z: 4, core: 2. Of those that a mesh axis runs over, the one named last changes fastest.
Arguments:
- query_proj: bfloat16 [8192, 8192], P('ctx', 'tp'), may hold values from -6 to 6
- key_proj: bfloat16 [8192, 8192], P('ctx', 'tp'), may hold values from -6 to 6
- value_proj: bfloat16 [8192, 8192], P('ctx', 'tp'), may hold values from -6 to 6
- short_filter: float32 [3, 7, 8192], P(None, None, 'tp'), may hold values from -2 to 2
- residues: float32 [16, 8192], P(None, 'tp'), may hold values from -3 to 3
- decay_rate: float32 [16, 8192], P(None, 'tp'), may hold values from 3.6621094e-05 to 0.0333333333
- skip_gain: float32 [8192], P('tp'), may hold values from 0.5 to 1.5
- doc_lengths: int32 [8], replicated, may hold values from 1 to 4096, 8192 in all
Outputs:
- mixed: bfloat16 [8192, 8192], P('ctx', 'tp')
The draws below stay inside these ranges and needn't reach their ends.
Inputs may be any that keep to these rules, and one draw needn't show every extreme that they name: `doc_lengths`: the lengths sum to 8192, and the longest is exactly 4096.
All inputs are finite; a program needn't handle non-finite values.
Results may differ from the reference program's by a relative error of at most 0.008.
Values may be sent and summed in bfloat16 or wider, within the bound.
A program may use at most 128 MiB of HBM per device.

```python
import math
import jax
import jax.numpy as jnp
import numpy as np
from jax import lax

WIDTH = 8192
MODES = 16
TAPS = 7
DOCS = 8
TOKENS = 8192


def draw_decay_rate(key, part):
    shape = (MODES, WIDTH)
    position = jax.random.uniform(jax.random.fold_in(key, 11), shape, jnp.float32)
    low_rate = math.log(0.3 / TOKENS)
    high_rate = math.log(1.0 / 30.0)
    rate = jnp.exp(low_rate + (high_rate - low_rate) * position)
    return jnp.clip(rate, 0.3 / TOKENS, 1.0 / 30.0).astype(jnp.float32)


def steps_of(stream_key, shape, split, smallest, largest):
    gain = 1.0
    for dim, blocks in split:
        draws = jax.random.uniform(jax.random.fold_in(jax.random.fold_in(stream_key, 6), dim), (blocks,), jnp.float32, smallest / len(split), largest / len(split))
        gain = gain * jnp.repeat(jnp.exp(draws), shape[dim] // blocks).reshape((-1,) + (1,) * (len(shape) - 1 - dim))
    return gain


def split_up(amount, total, limit, slope):
    portions = [(1 << 20) // math.isqrt(standing ** slope) + 1 for standing in range(2, amount + 1)]
    rest, given = total - limit - (amount - 1), [1] * (amount - 1)
    while rest > 0:
        candidates = [i for i in range(amount - 1) if given[i] < limit]
        whole, budget = sum([portions[i] for i in candidates]), rest
        for i in candidates:
            addition = min(limit - given[i], max(1, budget * portions[i] // whole), rest)
            given[i] = given[i] + addition
            rest = rest - addition
    return np.array([limit] + given)


def ragged(own_key, count, total, bound, slope):
    if count == 2:
        one = jax.random.randint(own_key, (), max(1, total - bound), min(bound, total - 1) + 1)
        return jnp.stack([one, total - one])
    lengths = jnp.asarray(split_up(count, total, bound, slope), jnp.int32)
    couples = (count - 1) // 2
    giver, taker = lengths[1:1 + 2 * couples:2], lengths[2:2 + 2 * couples:2]
    room = jnp.minimum(giver - 1, bound - taker)
    passed = jax.random.randint(jax.random.fold_in(own_key, 1), (couples,), 0, 1 << 20) % (room + 1)
    lengths = lengths.at[1:1 + 2 * couples:2].set(giver - passed).at[2:2 + 2 * couples:2].set(taker + passed)
    return lengths[jax.random.permutation(jax.random.fold_in(own_key, 2), count)]


def normal_values(key, shape, scale, reach, pieces=(), kind=jnp.bfloat16):
    level = steps_of(key, shape, pieces, -0.22, 0.18) if pieces else 1.0
    entries = jax.random.normal(key, shape, jnp.float32) * scale * level
    return jnp.minimum(jnp.maximum(entries, -reach), reach).astype(kind)


def setup_inputs(seed: int = 0) -> dict:
    key_list = jax.random.split(jax.random.key(seed), 9)
    query_proj = normal_values(key_list[0], (TOKENS, WIDTH), 1.0, 6.0, ((0, 32), (1, 4)))
    key_proj = normal_values(key_list[1], (TOKENS, WIDTH), 1.0, 6.0, ((0, 32), (1, 4)))
    value_proj = normal_values(key_list[2], (TOKENS, WIDTH), 1.0, 6.0, ((0, 32), (1, 4)))
    short_filter = normal_values(key_list[3], (3, TAPS, WIDTH), TAPS ** -0.5, 2.0, ((2, 4),), jnp.float32)
    residues = normal_values(key_list[4], (MODES, WIDTH), 0.5, 3.0, ((1, 4),), jnp.float32)
    decay_rate = draw_decay_rate(jax.random.fold_in(key_list[8], 71), 0)
    skip_gain = jnp.clip(0.5 + 1.0 * jax.random.uniform(key_list[6], (WIDTH,), jnp.float32) ** steps_of(key_list[6], (WIDTH,), ((0, 4),), -0.2, 0.2), 0.5, 1.5)
    doc_lengths = ragged(key_list[7], DOCS, TOKENS, TOKENS // 2, 2).astype(jnp.int32)
    return dict(query_proj=query_proj, key_proj=key_proj, value_proj=value_proj, short_filter=short_filter, residues=residues, decay_rate=decay_rate, skip_gain=skip_gain, doc_lengths=doc_lengths)


block_rows = 64
highest = lax.Precision.HIGHEST

def mix_channels(query_cols, key_cols, value_cols, taps_cols, resid_cols, rate_cols, skip_cols, row_start):
    positions = jnp.arange(TOKENS, dtype=jnp.int32)
    filtered = []
    branch_index = 0
    for source in (query_cols, key_cols, value_cols):
        values = source.astype(jnp.float32)
        summed = jnp.zeros(values.shape, jnp.float32)
        for lag_step in range(TAPS):
            shifted = jnp.concatenate([jnp.zeros((lag_step, values.shape[1]), jnp.float32), values[:TOKENS - lag_step]], axis=0)
            inside = (positions - lag_step >= row_start)[:, None]
            summed = summed + jnp.where(inside, taps_cols[branch_index, lag_step][None, :] * shifted, 0.0)
        filtered.append(summed)
        branch_index = branch_index + 1
    gated = (filtered[1] * filtered[2]).astype(jnp.bfloat16)
    gated_float = gated.astype(jnp.float32)
    log_decay = jnp.log1p(-rate_cols)
    scaled = resid_cols * jnp.sqrt(rate_cols * (2.0 - rate_cols))
    offsets = jnp.arange(block_rows, dtype=jnp.int32)
    offset_float = offsets.astype(jnp.float32)
    short_kernel = lax.optimization_barrier(jnp.sum(scaled[None] * jnp.exp(offset_float[:, None, None] * log_decay[None]), axis=1))
    lag_table = offsets[:, None] - offsets[None, :]
    kernel = short_kernel[jnp.maximum(lag_table, 0)]
    carry_decay = jnp.exp((offset_float + 1.0)[:, None, None] * log_decay[None])
    tail_power = jnp.exp((block_rows - 1.0 - offset_float)[:, None, None] * log_decay[None])
    block_decay = jnp.exp(float(block_rows) * log_decay)
    block_count = TOKENS // block_rows
    channel_count = query_cols.shape[1]

    def advance(state, inputs):
        block_z, block_start, block_first = inputs
        rows_here = block_first + offsets
        valid = (lag_table >= 0) & (rows_here[None, :] >= block_start[:, None])
        weights = jnp.where(valid[:, :, None], kernel, 0.0)
        inner = jnp.einsum('tsc,sc->tc', weights, block_z, precision=highest)
        continuing = (block_start < block_first)[:, None]
        from_state = lax.optimization_barrier(jnp.sum(scaled[None] * carry_decay * state[None], axis=1))
        output = inner + jnp.where(continuing, from_state, 0.0)
        last_start = block_start[block_rows - 1]
        keep_old = (last_start < block_first).astype(jnp.float32)
        in_doc = (rows_here >= last_start).astype(jnp.float32)
        new_state = lax.optimization_barrier(jnp.sum(tail_power * (in_doc[:, None] * block_z)[:, None, :], axis=0)) + keep_old * block_decay * state
        return (new_state, output)
    firsts = jnp.arange(block_count, dtype=jnp.int32) * block_rows
    initial = jnp.zeros((MODES, channel_count), jnp.float32)
    unused, outputs = lax.scan(advance, initial, (gated_float.reshape(block_count, block_rows, channel_count), row_start.reshape(block_count, block_rows), firsts))
    conv = outputs.reshape(TOKENS, channel_count)
    return (filtered[0] * (conv + skip_cols[None, :] * gated_float)).astype(jnp.bfloat16)

def reference(query_proj, key_proj, value_proj, short_filter, residues, decay_rate, skip_gain, doc_lengths):
    doc_starts = (jnp.cumsum(doc_lengths) - doc_lengths).astype(jnp.int32)
    positions = jnp.arange(TOKENS, dtype=jnp.int32)
    row_start = lax.optimization_barrier(jnp.max(jnp.where(doc_starts[None, :] <= positions[:, None], doc_starts[None, :], 0), axis=1)).astype(jnp.int32)
    columns = math.gcd(WIDTH, 512)
    groups = WIDTH // columns

    def split_rows(array):
        return array.reshape(TOKENS, groups, columns).transpose(1, 0, 2)
    packed = (split_rows(query_proj), split_rows(key_proj), split_rows(value_proj), short_filter.reshape(3, TAPS, groups, columns).transpose(2, 0, 1, 3), residues.reshape(MODES, groups, columns).transpose(1, 0, 2), decay_rate.reshape(MODES, groups, columns).transpose(1, 0, 2), skip_gain.reshape(groups, columns))

    def apply_group(arrays):
        return mix_channels(arrays[0], arrays[1], arrays[2], arrays[3], arrays[4], arrays[5], arrays[6], row_start)
    results = lax.map(apply_group, packed)
    return results.transpose(1, 0, 2).reshape(TOKENS, WIDTH)
```

```python
import jax
import jax.numpy as jnp
from jax import lax
from jax.sharding import PartitionSpec as P

MODES = 16
TAPS = 7


block_rows = 32
highest = lax.Precision.HIGHEST


def from_behind(value, axis, steps):
    count = lax.axis_size(axis)
    first, last = (max(0, -steps), min(count, count - steps))
    return lax.ppermute(value, axis, [(source, source + steps) for source in range(first, last)])


def body(
    query_proj, key_proj, value_proj, short_filter, residues, decay_rate, skip_gain, doc_lengths
):
    row_count, channels = query_proj.shape
    ctx_count = lax.axis_size("ctx")
    my_index = lax.axis_index("ctx")
    first_row = my_index * row_count
    local_rows = jnp.arange(row_count, dtype=jnp.int32)
    positions = first_row + local_rows
    doc_starts = jnp.cumsum(doc_lengths) - doc_lengths
    row_start = jnp.max(
        jnp.where(doc_starts[None, :] <= positions[:, None], doc_starts[None, :], 0), axis=1
    )
    stacked = jnp.stack([query_proj, key_proj, value_proj])
    upper_rim = from_behind(stacked[:, row_count - TAPS + 1 :, :], "ctx", 1)
    extended = jnp.concatenate([upper_rim, stacked], axis=1)
    filtered = jnp.zeros(stacked.shape, jnp.float32)
    for lag_step in range(TAPS):
        inside = (positions - lag_step >= row_start)[None, :, None]
        window = extended[:, TAPS - 1 - lag_step : TAPS - 1 - lag_step + row_count, :].astype(
            jnp.float32
        )
        filtered = filtered + jnp.where(
            inside, short_filter[:, lag_step, :][:, None, :] * window, 0.0
        )
    query_short = filtered[0]
    gated = (filtered[1] * filtered[2]).astype(jnp.bfloat16)
    gated_float = gated.astype(jnp.float32)
    log_decay = jnp.log1p(-decay_rate)
    scaled = residues * jnp.sqrt(decay_rate * (2.0 - decay_rate))
    offsets = jnp.arange(block_rows, dtype=jnp.int32)
    offset_float = offsets.astype(jnp.float32)
    short_kernel = jnp.sum(
        scaled[None] * jnp.exp(offset_float[:, None, None] * log_decay[None]), axis=1
    )
    lag_table = offsets[:, None] - offsets[None, :]
    kernel = short_kernel[jnp.maximum(lag_table, 0)]
    carry_decay = jnp.exp((offset_float + 1.0)[:, None, None] * log_decay[None])
    tail_power = jnp.exp((block_rows - 1.0 - offset_float)[:, None, None] * log_decay[None])
    block_decay = jnp.exp(float(block_rows) * log_decay)
    block_count = row_count // block_rows
    firsts = first_row + jnp.arange(block_count, dtype=jnp.int32) * block_rows
    blocks_z = gated_float.reshape(block_count, block_rows, channels)
    blocks_start = row_start.reshape(block_count, block_rows)

    def next_state(state, block_z, block_start, block_first):
        rows_here = block_first + offsets
        last_start = block_start[block_rows - 1]
        keep_old = (last_start < block_first).astype(jnp.float32)
        in_doc = (rows_here >= last_start).astype(jnp.float32)
        return (
            jnp.sum(tail_power * (in_doc[:, None] * block_z)[:, None, :], axis=0)
            + keep_old * block_decay * state
        )

    def fold_state(state, inputs):
        block_z, block_start, block_first = inputs
        return (next_state(state, block_z, block_start, block_first), None)

    zero_state = jnp.zeros((MODES, channels), jnp.float32)
    own_state, unused = lax.scan(fold_state, zero_state, (blocks_z, blocks_start, firsts))
    rows_total = row_count

    def starts_between(low_device, high_device):
        low_row = jnp.maximum(low_device, 0) * row_count
        high_row = (high_device + 1) * row_count
        return jnp.any((doc_starts >= low_row) & (doc_starts < high_row)).astype(jnp.float32)

    summary = own_state
    span = 1
    while 2 * span < ctx_count:
        behind = from_behind(summary, "ctx", span)
        open_path = 1.0 - starts_between(my_index - span + 1, my_index)
        summary = summary + open_path * jnp.exp(float(span * rows_total) * log_decay) * behind
        span *= 2
    near = from_behind(summary, "ctx", 1)
    far = from_behind(summary, "ctx", 1 + span)
    open_path = 1.0 - starts_between(my_index - span, my_index - 1)
    incoming = near + open_path * jnp.exp(float(span * rows_total) * log_decay) * far

    def advance(state, inputs):
        block_z, block_start, block_first = inputs
        rows_here = block_first + offsets
        valid = (lag_table >= 0) & (rows_here[None, :] >= block_start[:, None])
        weights = jnp.where(valid[:, :, None], kernel, 0.0)
        inner = jnp.einsum("tsc,sc->tc", weights, block_z, precision=highest)
        continuing = (block_start < block_first)[:, None]
        from_state = jnp.sum(scaled[None] * carry_decay * state[None], axis=1)
        output = inner + jnp.where(continuing, from_state, 0.0)
        return (next_state(state, block_z, block_start, block_first), output)

    unused_state, outputs = lax.scan(advance, incoming, (blocks_z, blocks_start, firsts))
    conv = outputs.reshape(row_count, channels)
    return (query_short * (conv + skip_gain[None, :] * gated_float)).astype(jnp.bfloat16)


def solution(mesh):
    in_specs = (
        P("ctx", "tp"),
        P("ctx", "tp"),
        P("ctx", "tp"),
        P(None, None, "tp"),
        P(None, "tp"),
        P(None, "tp"),
        P("tp"),
        P(),
    )
    out_specs = P("ctx", "tp")
    return jax.shard_map(body, mesh=mesh, in_specs=in_specs, out_specs=out_specs, check_vma=False)
```

```python
import functools

import jax
import jax.numpy as jnp
from jax import lax
from jax.experimental import pallas as pl
from jax.experimental.pallas import tpu as pltpu
from jax.sharding import PartitionSpec as P

MODES = 16
TAPS = 7
LANES = 128
SEGMENTS = 8
INTERPRET = False


def from_behind(value, axis, steps):
    count = lax.axis_size(axis)
    first, last = (max(0, -steps), min(count, count - steps))
    return lax.ppermute(value, axis, [(source, source + steps) for source in range(first, last)])


def local_kernel(q_ref, k_ref, v_ref, rim_ref, filt_ref, amp_ref, lam_ref, skip_ref, since_ref, keep_ref,
                 segkeep_ref, acc_ref, qs_ref, cl_ref, ext_ref, g_ref):
    rows = q_ref.shape[0]
    seg_rows = rows // SEGMENTS
    since = since_ref[...]
    filtered = []
    for branch, src in enumerate((q_ref, k_ref, v_ref)):
        ext_ref[0:8, :] = rim_ref[branch].astype(jnp.float32)
        ext_ref[8:8 + rows, :] = src[...].astype(jnp.float32)
        total = jnp.zeros((rows, LANES), jnp.float32)
        for lag in range(TAPS):
            window = ext_ref[8 - lag:8 - lag + rows, :]
            tap = filt_ref[branch, lag:lag + 1, :]
            total = total + jnp.where(since >= float(lag), tap * window, 0.0)
        filtered.append(total)
    qs_ref[...] = filtered[0]
    g_ref[...] = (filtered[1] * filtered[2]).astype(jnp.bfloat16).astype(jnp.float32)
    lam = [jnp.broadcast_to(lam_ref[m:m + 1, :], (SEGMENTS, LANES)) for m in range(MODES)]
    amp = [jnp.broadcast_to(amp_ref[m:m + 1, :], (SEGMENTS, LANES)) for m in range(MODES)]
    skip = jnp.broadcast_to(skip_ref[...], (SEGMENTS, LANES))

    def step(j, states):
        x = g_ref[pl.ds(j, SEGMENTS, stride=seg_rows), :]
        keep = keep_ref[pl.ds(j, SEGMENTS, stride=seg_rows), :]
        new_states = []
        y = skip * x
        for m in range(MODES):
            h = lam[m] * (keep * states[m]) + x
            new_states.append(h)
            y = y + amp[m] * h
        acc_ref[pl.ds(j, SEGMENTS, stride=seg_rows), :] = y
        return tuple(new_states)

    zero = jnp.zeros((SEGMENTS, LANES), jnp.float32)
    ends = lax.fori_loop(0, seg_rows, step, tuple([zero] * MODES))
    segkeep = segkeep_ref[...]
    for m in range(MODES):
        seg_decay = jnp.exp(float(seg_rows) * jnp.log(lam_ref[m:m + 1, :]))
        carried = jnp.zeros((1, LANES), jnp.float32)
        cl_ref[m, 0:1, :] = carried
        for p in range(SEGMENTS):
            carried = ends[m][p:p + 1, :] + segkeep[p:p + 1, :] * seg_decay * carried
            cl_ref[m, p + 1:p + 2, :] = carried
        cl_ref[m, SEGMENTS + 1:, :] = jnp.zeros((16 - SEGMENTS - 1, LANES), jnp.float32)


def fix_kernel(acc_ref, qs_ref, cl_ref, hin_ref, amp_ref, logl_ref, cont_ref, open_ref, out_ref):
    rows = acc_ref.shape[0]
    seg_rows = rows // SEGMENTS
    seg_index = lax.broadcasted_iota(jnp.int32, (SEGMENTS, LANES), 0).astype(jnp.float32)
    lag_index = lax.broadcasted_iota(jnp.int32, (seg_rows, LANES), 0).astype(jnp.float32) + 1.0
    opened = open_ref[...]
    starts = []
    powers = []
    for m in range(MODES):
        logl = logl_ref[m:m + 1, :]
        start = cl_ref[m, 0:SEGMENTS, :] + opened * jnp.exp(seg_index * (float(seg_rows) * logl)) * hin_ref[m:m + 1, :]
        starts.append(start)
        powers.append(amp_ref[m:m + 1, :] * jnp.exp(lag_index * logl))
    for p in range(SEGMENTS):
        lo = p * seg_rows
        corr = jnp.zeros((seg_rows, LANES), jnp.float32)
        for m in range(MODES):
            corr = corr + powers[m] * starts[m][p:p + 1, :]
        conv = acc_ref[lo:lo + seg_rows, :] + cont_ref[lo:lo + seg_rows, :] * corr
        out_ref[lo:lo + seg_rows, :] = (qs_ref[lo:lo + seg_rows, :] * conv).astype(out_ref.dtype)


def body(query_proj, key_proj, value_proj, short_filter, residues, decay_rate, skip_gain, doc_lengths):
    row_count, channels = query_proj.shape
    ctx_count = lax.axis_size("ctx")
    my_index = lax.axis_index("ctx")
    first_row = my_index * row_count
    seg_rows = row_count // SEGMENTS
    local_rows = jnp.arange(row_count, dtype=jnp.int32)
    positions = first_row + local_rows
    doc_starts = jnp.cumsum(doc_lengths) - doc_lengths
    row_start = jnp.max(
        jnp.where(doc_starts[None, :] <= positions[:, None], doc_starts[None, :], 0), axis=1
    )
    since = (positions - row_start).astype(jnp.float32)
    keep = (positions != row_start).astype(jnp.float32)
    seg_first = first_row + (local_rows // seg_rows) * seg_rows
    cont = (row_start < seg_first).astype(jnp.float32)
    seg_ids = jnp.arange(SEGMENTS, dtype=jnp.int32)
    seg_lo = first_row + seg_ids * seg_rows
    in_seg = (doc_starts[None, :] >= seg_lo[:, None]) & (doc_starts[None, :] < seg_lo[:, None] + seg_rows)
    segkeep = 1.0 - jnp.any(in_seg, axis=1).astype(jnp.float32)
    before = (doc_starts[None, :] >= first_row) & (doc_starts[None, :] < seg_lo[:, None])
    opened = 1.0 - jnp.any(before, axis=1).astype(jnp.float32)

    def lanes(column):
        return jnp.broadcast_to(column[:, None], (column.shape[0], LANES))

    stacked = jnp.stack([query_proj, key_proj, value_proj])
    rim = from_behind(stacked[:, row_count - TAPS + 1:, :], "ctx", 1)
    rim = jnp.concatenate([jnp.zeros((3, 8 - TAPS + 1, channels), rim.dtype), rim], axis=1)
    log_decay = jnp.log1p(-decay_rate)
    lam = jnp.exp(log_decay)
    amp = residues * jnp.sqrt(decay_rate * (2.0 - decay_rate))
    tiles = channels // LANES
    col = lambda *lead: pl.BlockSpec(tuple(lead) + (LANES,), lambda c: (0,) * len(lead) + (c,))
    fixed = lambda *shape: pl.BlockSpec(shape, lambda c: (0,) * len(shape))
    f32 = jnp.float32
    acc, q_short, cl = pl.pallas_call(
        local_kernel,
        grid=(tiles,),
        in_specs=[col(row_count), col(row_count), col(row_count), col(3, 8), col(3, TAPS), col(MODES), col(MODES),
                  col(1), fixed(row_count, LANES), fixed(row_count, LANES), fixed(SEGMENTS, LANES)],
        out_specs=[col(row_count), col(row_count), col(MODES, 16)],
        out_shape=[jax.ShapeDtypeStruct((row_count, channels), f32), jax.ShapeDtypeStruct((row_count, channels), f32),
                   jax.ShapeDtypeStruct((MODES, 16, channels), f32)],
        scratch_shapes=[pltpu.VMEM((row_count + 8, LANES), f32), pltpu.VMEM((row_count, LANES), f32)],
        interpret=INTERPRET,
    )(query_proj, key_proj, value_proj, rim, short_filter, amp, lam, skip_gain[None, :], lanes(since), lanes(keep),
      lanes(segkeep))
    own_state = cl[:, SEGMENTS, :]

    def starts_between(low_device, high_device):
        low_row = jnp.maximum(low_device, 0) * row_count
        high_row = (high_device + 1) * row_count
        return jnp.any((doc_starts >= low_row) & (doc_starts < high_row)).astype(jnp.float32)

    summary = own_state
    span = 1
    while 2 * span < ctx_count:
        behind = from_behind(summary, "ctx", span)
        open_path = 1.0 - starts_between(my_index - span + 1, my_index)
        summary = summary + open_path * jnp.exp(float(span * row_count) * log_decay) * behind
        span *= 2
    near = from_behind(summary, "ctx", 1)
    far = from_behind(summary, "ctx", 1 + span)
    open_path = 1.0 - starts_between(my_index - span, my_index - 1)
    incoming = near + open_path * jnp.exp(float(span * row_count) * log_decay) * far

    return pl.pallas_call(
        fix_kernel,
        grid=(tiles,),
        in_specs=[col(row_count), col(row_count), col(MODES, 16), col(MODES), col(MODES), col(MODES),
                  fixed(row_count, LANES), fixed(SEGMENTS, LANES)],
        out_specs=col(row_count),
        out_shape=jax.ShapeDtypeStruct((row_count, channels), jnp.bfloat16),
        interpret=INTERPRET,
    )(acc, q_short, cl, incoming, amp, log_decay, lanes(cont), lanes(opened))


def solution(mesh):
    in_specs = (
        P("ctx", "tp"),
        P("ctx", "tp"),
        P("ctx", "tp"),
        P(None, None, "tp"),
        P(None, "tp"),
        P(None, "tp"),
        P("tp"),
        P(),
    )
    out_specs = P("ctx", "tp")
    return jax.shard_map(body, mesh=mesh, in_specs=in_specs, out_specs=out_specs, check_vma=False)
```

```python
import functools

import jax
import jax.numpy as jnp
from jax import lax
from jax.experimental import pallas as pl
from jax.experimental.pallas import tpu as pltpu
from jax.sharding import PartitionSpec as P

MODES = 16
TAPS = 7
LANES = 128
SEGMENTS = 8
INTERPRET = False


def from_behind(value, axis, steps):
    count = lax.axis_size(axis)
    first, last = (max(0, -steps), min(count, count - steps))
    return lax.ppermute(value, axis, [(source, source + steps) for source in range(first, last)])


def local_kernel(q_ref, k_ref, v_ref, rim_ref, filt_ref, amp_ref, lam_ref, skip_ref, since_ref, keep_ref,
                 segkeep_ref, acc_ref, qs_ref, cl_ref, end_ref, ext_ref, g_ref):
    rows = q_ref.shape[0]
    seg_rows = rows // SEGMENTS
    since = since_ref[...]
    filtered = []
    for branch, src in enumerate((q_ref, k_ref, v_ref)):
        ext_ref[0:8, :] = rim_ref[branch].astype(jnp.float32)
        ext_ref[8:8 + rows, :] = src[...].astype(jnp.float32)
        total = jnp.zeros((rows, LANES), jnp.float32)
        for lag in range(TAPS):
            window = ext_ref[8 - lag:8 - lag + rows, :]
            tap = filt_ref[branch, lag:lag + 1, :]
            total = total + jnp.where(since >= float(lag), tap * window, 0.0)
        filtered.append(total)
    qs_ref[...] = filtered[0]
    g_ref[...] = (filtered[1] * filtered[2]).astype(jnp.bfloat16).astype(jnp.float32)
    lam = [jnp.broadcast_to(lam_ref[m:m + 1, :], (SEGMENTS, LANES)) for m in range(MODES)]
    amp = [jnp.broadcast_to(amp_ref[m:m + 1, :], (SEGMENTS, LANES)) for m in range(MODES)]
    skip = jnp.broadcast_to(skip_ref[...], (SEGMENTS, LANES))

    def step(j, states):
        x = g_ref[pl.ds(j, SEGMENTS, stride=seg_rows), :]
        keep = keep_ref[pl.ds(j, SEGMENTS, stride=seg_rows), :]
        new_states = []
        y = skip * x
        for m in range(MODES):
            h = lam[m] * (keep * states[m]) + x
            new_states.append(h)
            y = y + amp[m] * h
        acc_ref[pl.ds(j, SEGMENTS, stride=seg_rows), :] = y
        return tuple(new_states)

    zero = jnp.zeros((SEGMENTS, LANES), jnp.float32)
    ends = lax.fori_loop(0, seg_rows, step, tuple([zero] * MODES))
    segkeep = segkeep_ref[...]
    for m in range(MODES):
        seg_decay = jnp.exp(float(seg_rows) * jnp.log(lam_ref[m:m + 1, :]))
        carried = jnp.zeros((1, LANES), jnp.float32)
        cl_ref[m, 0:1, :] = carried
        for p in range(SEGMENTS):
            carried = ends[m][p:p + 1, :] + segkeep[p:p + 1, :] * seg_decay * carried
            cl_ref[m, p + 1:p + 2, :] = carried
        cl_ref[m, SEGMENTS + 1:, :] = jnp.zeros((16 - SEGMENTS - 1, LANES), jnp.float32)
        end_ref[m:m + 1, :] = carried


def fix_kernel(acc_ref, qs_ref, cl_ref, hin_ref, amp_ref, logl_ref, cont_ref, open_ref, out_ref):
    rows = acc_ref.shape[0]
    seg_rows = rows // SEGMENTS
    seg_index = lax.broadcasted_iota(jnp.int32, (SEGMENTS, LANES), 0).astype(jnp.float32)
    lag_index = lax.broadcasted_iota(jnp.int32, (seg_rows, LANES), 0).astype(jnp.float32) + 1.0
    opened = open_ref[...]
    starts = []
    powers = []
    for m in range(MODES):
        logl = logl_ref[m:m + 1, :]
        start = cl_ref[m, 0:SEGMENTS, :] + opened * jnp.exp(seg_index * (float(seg_rows) * logl)) * hin_ref[m:m + 1, :]
        starts.append(start)
        powers.append(amp_ref[m:m + 1, :] * jnp.exp(lag_index * logl))
    for p in range(SEGMENTS):
        lo = p * seg_rows
        corr = jnp.zeros((seg_rows, LANES), jnp.float32)
        for m in range(MODES):
            corr = corr + powers[m] * starts[m][p:p + 1, :]
        conv = acc_ref[lo:lo + seg_rows, :] + cont_ref[lo:lo + seg_rows, :] * corr
        out_ref[lo:lo + seg_rows, :] = (qs_ref[lo:lo + seg_rows, :] * conv).astype(out_ref.dtype)


def scan_kernel(count, spans, own_ref, fac_ref, out_ref, sums, slots, send_sems, recv_sems):
    me = lax.axis_index("ctx")
    lane = lax.axis_index("tp")
    last = spans[-1] * 2 if spans else 1
    offsets = sorted(set(spans) | {1, 1 + last})
    barrier = pltpu.get_barrier_semaphore()
    for d in offsets:
        for other in (me - d, me + d):
            @pl.when((other >= 0) & (other < count))
            def _():
                pl.semaphore_signal(barrier, inc=1, device_id=(other, lane), device_id_type=pl.DeviceIdType.MESH)
    partners = 0
    for d in offsets:
        partners = partners + (me + count - d) // count + (2 * count - 1 - me - d) // count
    pl.semaphore_wait(barrier, partners)

    def transfer(src, slot, target):
        return pltpu.make_async_remote_copy(
            src_ref=src, dst_ref=slots.at[slot], send_sem=send_sems.at[slot], recv_sem=recv_sems.at[slot],
            device_id=(target, lane), device_id_type=pl.DeviceIdType.MESH)

    def exchange(src, sends):
        for slot, d in sends:
            @pl.when(me + d < count)
            def _():
                transfer(src, slot, me + d).start()

    def settle(src, sends):
        for slot, d in sends:
            @pl.when(me + d < count)
            def _():
                transfer(src, slot, me + d).wait_send()

    current = own_ref
    for r, d in enumerate(spans):
        exchange(current, [(r, d)])
        @pl.when(me - d >= 0)
        def _():
            transfer(current, r, me - d).wait_recv()
            sums[r] = current[...] + fac_ref[r] * slots[r]

        @pl.when(me - d < 0)
        def _():
            sums[r] = current[...]
        settle(current, [(r, d)])
        current = sums.at[r]
    near, far = len(spans), len(spans) + 1
    final = [(near, 1), (far, 1 + last)]
    exchange(current, final)
    out_ref[...] = jnp.zeros(out_ref.shape, out_ref.dtype)

    @pl.when(me - 1 >= 0)
    def _():
        transfer(current, near, me - 1).wait_recv()
        out_ref[...] = slots[near]

    @pl.when(me - 1 - last >= 0)
    def _():
        transfer(current, far, me - 1 - last).wait_recv()
        out_ref[...] = out_ref[...] + fac_ref[len(spans)] * slots[far]
    settle(current, final)


def body(query_proj, key_proj, value_proj, short_filter, residues, decay_rate, skip_gain, doc_lengths):
    row_count, channels = query_proj.shape
    ctx_count = lax.axis_size("ctx")
    my_index = lax.axis_index("ctx")
    first_row = my_index * row_count
    seg_rows = row_count // SEGMENTS
    local_rows = jnp.arange(row_count, dtype=jnp.int32)
    positions = first_row + local_rows
    doc_starts = jnp.cumsum(doc_lengths) - doc_lengths
    row_start = jnp.max(
        jnp.where(doc_starts[None, :] <= positions[:, None], doc_starts[None, :], 0), axis=1
    )
    since = (positions - row_start).astype(jnp.float32)
    keep = (positions != row_start).astype(jnp.float32)
    seg_first = first_row + (local_rows // seg_rows) * seg_rows
    cont = (row_start < seg_first).astype(jnp.float32)
    seg_ids = jnp.arange(SEGMENTS, dtype=jnp.int32)
    seg_lo = first_row + seg_ids * seg_rows
    in_seg = (doc_starts[None, :] >= seg_lo[:, None]) & (doc_starts[None, :] < seg_lo[:, None] + seg_rows)
    segkeep = 1.0 - jnp.any(in_seg, axis=1).astype(jnp.float32)
    before = (doc_starts[None, :] >= first_row) & (doc_starts[None, :] < seg_lo[:, None])
    opened = 1.0 - jnp.any(before, axis=1).astype(jnp.float32)

    def lanes(column):
        return jnp.broadcast_to(column[:, None], (column.shape[0], LANES))

    stacked = jnp.stack([query_proj, key_proj, value_proj])
    rim = from_behind(stacked[:, row_count - TAPS + 1:, :], "ctx", 1)
    rim = jnp.concatenate([jnp.zeros((3, 8 - TAPS + 1, channels), rim.dtype), rim], axis=1)
    log_decay = jnp.log1p(-decay_rate)
    lam = jnp.exp(log_decay)
    amp = residues * jnp.sqrt(decay_rate * (2.0 - decay_rate))
    tiles = channels // LANES
    col = lambda *lead: pl.BlockSpec(tuple(lead) + (LANES,), lambda c: (0,) * len(lead) + (c,))
    fixed = lambda *shape: pl.BlockSpec(shape, lambda c: (0,) * len(shape))
    f32 = jnp.float32
    acc, q_short, cl, own_state = pl.pallas_call(
        local_kernel,
        grid=(tiles,),
        in_specs=[col(row_count), col(row_count), col(row_count), col(3, 8), col(3, TAPS), col(MODES), col(MODES),
                  col(1), fixed(row_count, LANES), fixed(row_count, LANES), fixed(SEGMENTS, LANES)],
        out_specs=[col(row_count), col(row_count), col(MODES, 16), col(MODES)],
        out_shape=[jax.ShapeDtypeStruct((row_count, channels), f32), jax.ShapeDtypeStruct((row_count, channels), f32),
                   jax.ShapeDtypeStruct((MODES, 16, channels), f32), jax.ShapeDtypeStruct((MODES, channels), f32)],
        scratch_shapes=[pltpu.VMEM((row_count + 8, LANES), f32), pltpu.VMEM((row_count, LANES), f32)],
        interpret=INTERPRET,
    )(query_proj, key_proj, value_proj, rim, short_filter, amp, lam, skip_gain[None, :], lanes(since), lanes(keep),
      lanes(segkeep))

    def starts_between(low_device, high_device):
        low_row = jnp.maximum(low_device, 0) * row_count
        high_row = (high_device + 1) * row_count
        return jnp.any((doc_starts >= low_row) & (doc_starts < high_row)).astype(jnp.float32)

    spans = []
    span = 1
    while 2 * span < ctx_count:
        spans.append(span)
        span *= 2
    factors = []
    for d in spans:
        open_path = 1.0 - starts_between(my_index - d + 1, my_index)
        factors.append(open_path * jnp.exp(float(d * row_count) * log_decay))
    open_path = 1.0 - starts_between(my_index - span, my_index - 1)
    factors.append(open_path * jnp.exp(float(span * row_count) * log_decay))
    factors = jnp.stack(factors)
    vmem = pl.BlockSpec(memory_space=pltpu.VMEM)
    incoming = pl.pallas_call(
        functools.partial(scan_kernel, ctx_count, tuple(spans)),
        out_shape=jax.ShapeDtypeStruct((MODES, channels), f32),
        in_specs=[vmem, vmem],
        out_specs=vmem,
        scratch_shapes=[
            pltpu.VMEM((len(spans), MODES, channels), f32),
            pltpu.VMEM((len(spans) + 2, MODES, channels), f32),
            pltpu.SemaphoreType.DMA((len(spans) + 2,)),
            pltpu.SemaphoreType.DMA((len(spans) + 2,)),
        ],
        compiler_params=pltpu.CompilerParams(collective_id=0, has_side_effects=True),
        interpret=INTERPRET,
    )(own_state, factors)

    return pl.pallas_call(
        fix_kernel,
        grid=(tiles,),
        in_specs=[col(row_count), col(row_count), col(MODES, 16), col(MODES), col(MODES), col(MODES),
                  fixed(row_count, LANES), fixed(SEGMENTS, LANES)],
        out_specs=col(row_count),
        out_shape=jax.ShapeDtypeStruct((row_count, channels), jnp.bfloat16),
        interpret=INTERPRET,
    )(acc, q_short, cl, incoming, amp, log_decay, lanes(cont), lanes(opened))


def solution(mesh):
    in_specs = (
        P("ctx", "tp"),
        P("ctx", "tp"),
        P("ctx", "tp"),
        P(None, None, "tp"),
        P(None, "tp"),
        P(None, "tp"),
        P("tp"),
        P(),
    )
    out_specs = P("ctx", "tp")
    return jax.shard_map(body, mesh=mesh, in_specs=in_specs, out_specs=out_specs, check_vma=False)
```

```python
import functools

import jax
import jax.numpy as jnp
from jax import lax
from jax.experimental import pallas as pl
from jax.experimental.pallas import tpu as pltpu
from jax.sharding import PartitionSpec as P

MODES = 16
TAPS = 7
LANES = 128
LANES_FIX = 256
SEGMENTS = 8
INTERPRET = False


def from_behind(value, axis, steps):
    count = lax.axis_size(axis)
    first, last = (max(0, -steps), min(count, count - steps))
    return lax.ppermute(value, axis, [(source, source + steps) for source in range(first, last)])


def local_kernel(q_ref, k_ref, v_ref, rim_ref, filt_ref, amp_ref, lam_ref, skip_ref, mask_ref,
                 acc_ref, qs_ref, cl_ref, end_ref, ext_ref, g_ref):
    since_ref, keep_ref = mask_ref.at[0], mask_ref.at[1]
    rows = q_ref.shape[0]
    seg_rows = rows // SEGMENTS
    since = since_ref[...]
    filtered = []
    for branch, src in enumerate((q_ref, k_ref, v_ref)):
        ext_ref[8 - TAPS + 1:8, :] = rim_ref[branch].astype(jnp.float32)
        ext_ref[8:8 + rows, :] = src[...].astype(jnp.float32)
        total = jnp.zeros((rows, LANES), jnp.float32)
        for lag in range(TAPS):
            window = ext_ref[8 - lag:8 - lag + rows, :]
            tap = filt_ref[branch, lag:lag + 1, :]
            total = total + jnp.where(since >= float(lag), tap * window, 0.0)
        filtered.append(total)
    qs_ref[...] = filtered[0]
    g_ref[...] = (filtered[1] * filtered[2]).astype(jnp.bfloat16).astype(jnp.float32)
    lam = [jnp.broadcast_to(lam_ref[m:m + 1, :], (SEGMENTS, LANES)) for m in range(MODES)]
    amp = [jnp.broadcast_to(amp_ref[m:m + 1, :], (SEGMENTS, LANES)) for m in range(MODES)]
    skip = jnp.broadcast_to(skip_ref[...], (SEGMENTS, LANES))

    def step(j, states):
        x = g_ref[pl.ds(j, SEGMENTS, stride=seg_rows), :]
        keep = keep_ref[pl.ds(j, SEGMENTS, stride=seg_rows), :]
        new_states = []
        y = skip * x
        for m in range(MODES):
            h = lam[m] * (keep * states[m]) + x
            new_states.append(h)
            y = y + amp[m] * h
        acc_ref[pl.ds(j, SEGMENTS, stride=seg_rows), :] = y
        return tuple(new_states)

    zero = jnp.zeros((SEGMENTS, LANES), jnp.float32)
    ends = lax.fori_loop(0, seg_rows, step, tuple([zero] * MODES))
    segkeep = mask_ref[3, 0:SEGMENTS, :]
    for m in range(MODES):
        seg_decay = jnp.exp(float(seg_rows) * jnp.log(lam_ref[m:m + 1, :]))
        carried = jnp.zeros((1, LANES), jnp.float32)
        cl_ref[m, 0:1, :] = carried
        for p in range(SEGMENTS):
            carried = ends[m][p:p + 1, :] + segkeep[p:p + 1, :] * seg_decay * carried
            cl_ref[m, p + 1:p + 2, :] = carried
        cl_ref[m, SEGMENTS + 1:, :] = jnp.zeros((16 - SEGMENTS - 1, LANES), jnp.float32)
        end_ref[m:m + 1, :] = carried


def fix_kernel(acc_ref, qs_ref, cl_ref, hin_ref, amp_ref, logl_ref, mask_ref, out_ref):
    rows, width = acc_ref.shape
    seg_rows = rows // SEGMENTS
    copies = width // LANES
    widen = lambda part: jnp.concatenate([part] * copies, axis=1) if copies > 1 else part
    seg_index = lax.broadcasted_iota(jnp.int32, (SEGMENTS, width), 0).astype(jnp.float32)
    lag_index = lax.broadcasted_iota(jnp.int32, (seg_rows, width), 0).astype(jnp.float32) + 1.0
    opened = widen(mask_ref[3, 8:8 + SEGMENTS, :])
    starts = []
    powers = []
    for m in range(MODES):
        logl = logl_ref[m:m + 1, :]
        start = cl_ref[m, 0:SEGMENTS, :] + opened * jnp.exp(seg_index * (float(seg_rows) * logl)) * hin_ref[m:m + 1, :]
        starts.append(start)
        powers.append(amp_ref[m:m + 1, :] * jnp.exp(lag_index * logl))
    for p in range(SEGMENTS):
        lo = p * seg_rows
        corr = jnp.zeros((seg_rows, width), jnp.float32)
        for m in range(MODES):
            corr = corr + powers[m] * starts[m][p:p + 1, :]
        conv = acc_ref[lo:lo + seg_rows, :] + widen(mask_ref[2, lo:lo + seg_rows, :]) * corr
        out_ref[lo:lo + seg_rows, :] = (qs_ref[lo:lo + seg_rows, :] * conv).astype(out_ref.dtype)


def scan_kernel(count, spans, own_ref, fac_ref, out_ref, sums, slots, send_sems, recv_sems):
    me = lax.axis_index("ctx")
    lane = lax.axis_index("tp")
    last = spans[-1] * 2 if spans else 1
    offsets = sorted(set(spans) | {1, 1 + last})
    barrier = pltpu.get_barrier_semaphore()
    for d in offsets:
        for other in (me - d, me + d):
            @pl.when((other >= 0) & (other < count))
            def _():
                pl.semaphore_signal(barrier, inc=1, device_id=(other, lane), device_id_type=pl.DeviceIdType.MESH)
    partners = 0
    for d in offsets:
        partners = partners + (me + count - d) // count + (2 * count - 1 - me - d) // count
    pl.semaphore_wait(barrier, partners)

    def transfer(src, slot, target):
        return pltpu.make_async_remote_copy(
            src_ref=src, dst_ref=slots.at[slot], send_sem=send_sems.at[slot], recv_sem=recv_sems.at[slot],
            device_id=(target, lane), device_id_type=pl.DeviceIdType.MESH)

    def exchange(src, sends):
        for slot, d in sends:
            @pl.when(me + d < count)
            def _():
                transfer(src, slot, me + d).start()

    def settle(src, sends):
        for slot, d in sends:
            @pl.when(me + d < count)
            def _():
                transfer(src, slot, me + d).wait_send()

    current = own_ref
    for r, d in enumerate(spans):
        exchange(current, [(r, d)])
        @pl.when(me - d >= 0)
        def _():
            transfer(current, r, me - d).wait_recv()
            sums[r] = current[...] + fac_ref[r] * slots[r]

        @pl.when(me - d < 0)
        def _():
            sums[r] = current[...]
        settle(current, [(r, d)])
        current = sums.at[r]
    near, far = len(spans), len(spans) + 1
    final = [(near, 1), (far, 1 + last)]
    exchange(current, final)
    out_ref[...] = jnp.zeros(out_ref.shape, out_ref.dtype)

    @pl.when(me - 1 >= 0)
    def _():
        transfer(current, near, me - 1).wait_recv()
        out_ref[...] = slots[near]

    @pl.when(me - 1 - last >= 0)
    def _():
        transfer(current, far, me - 1 - last).wait_recv()
        out_ref[...] = out_ref[...] + fac_ref[len(spans)] * slots[far]
    settle(current, final)


def body(query_proj, key_proj, value_proj, short_filter, residues, decay_rate, skip_gain, doc_lengths):
    row_count, channels = query_proj.shape
    ctx_count = lax.axis_size("ctx")
    my_index = lax.axis_index("ctx")
    first_row = my_index * row_count
    seg_rows = row_count // SEGMENTS
    local_rows = jnp.arange(row_count, dtype=jnp.int32)
    positions = first_row + local_rows
    doc_starts = jnp.cumsum(doc_lengths) - doc_lengths
    row_start = jnp.max(
        jnp.where(doc_starts[None, :] <= positions[:, None], doc_starts[None, :], 0), axis=1
    )
    since = (positions - row_start).astype(jnp.float32)
    keep = (positions != row_start).astype(jnp.float32)
    seg_first = first_row + (local_rows // seg_rows) * seg_rows
    cont = (row_start < seg_first).astype(jnp.float32)
    seg_ids = jnp.arange(SEGMENTS, dtype=jnp.int32)
    seg_lo = first_row + seg_ids * seg_rows
    in_seg = (doc_starts[None, :] >= seg_lo[:, None]) & (doc_starts[None, :] < seg_lo[:, None] + seg_rows)
    segkeep = 1.0 - jnp.any(in_seg, axis=1).astype(jnp.float32)
    before = (doc_starts[None, :] >= first_row) & (doc_starts[None, :] < seg_lo[:, None])
    opened = 1.0 - jnp.any(before, axis=1).astype(jnp.float32)

    small = jnp.zeros((row_count,), jnp.float32).at[0:SEGMENTS].set(segkeep).at[8:8 + SEGMENTS].set(opened)
    masks = jnp.broadcast_to(jnp.stack([since, keep, cont, small])[:, :, None], (4, row_count, LANES))

    stacked = jnp.stack([query_proj, key_proj, value_proj])
    rim = from_behind(stacked[:, row_count - TAPS + 1:, :], "ctx", 1)
    log_decay = jnp.log1p(-decay_rate)
    lam = jnp.exp(log_decay)
    amp = residues * jnp.sqrt(decay_rate * (2.0 - decay_rate))
    tiles = channels // LANES
    col = lambda *lead: pl.BlockSpec(tuple(lead) + (LANES,), lambda c: (0,) * len(lead) + (c,))
    fixed = lambda *shape: pl.BlockSpec(shape, lambda c: (0,) * len(shape))
    f32 = jnp.float32
    acc, q_short, cl, own_state = pl.pallas_call(
        local_kernel,
        grid=(tiles,),
        in_specs=[col(row_count), col(row_count), col(row_count), col(3, TAPS - 1), col(3, TAPS), col(MODES), col(MODES),
                  col(1), fixed(4, row_count, LANES)],
        out_specs=[col(row_count), col(row_count), col(MODES, 16), col(MODES)],
        out_shape=[jax.ShapeDtypeStruct((row_count, channels), f32), jax.ShapeDtypeStruct((row_count, channels), f32),
                   jax.ShapeDtypeStruct((MODES, 16, channels), f32), jax.ShapeDtypeStruct((MODES, channels), f32)],
        scratch_shapes=[pltpu.VMEM((row_count + 8, LANES), f32), pltpu.VMEM((row_count, LANES), f32)],
        interpret=INTERPRET,
    )(query_proj, key_proj, value_proj, rim, short_filter, amp, lam, skip_gain[None, :], masks)

    def starts_between(low_device, high_device):
        low_row = jnp.maximum(low_device, 0) * row_count
        high_row = (high_device + 1) * row_count
        return jnp.any((doc_starts >= low_row) & (doc_starts < high_row)).astype(jnp.float32)

    spans = []
    span = 1
    while 2 * span < ctx_count:
        spans.append(span)
        span *= 2
    factors = []
    for d in spans:
        open_path = 1.0 - starts_between(my_index - d + 1, my_index)
        factors.append(open_path * jnp.exp(float(d * row_count) * log_decay))
    open_path = 1.0 - starts_between(my_index - span, my_index - 1)
    factors.append(open_path * jnp.exp(float(span * row_count) * log_decay))
    factors = jnp.stack(factors)
    vmem = pl.BlockSpec(memory_space=pltpu.VMEM)
    incoming = pl.pallas_call(
        functools.partial(scan_kernel, ctx_count, tuple(spans)),
        out_shape=jax.ShapeDtypeStruct((MODES, channels), f32),
        in_specs=[vmem, vmem],
        out_specs=vmem,
        scratch_shapes=[
            pltpu.VMEM((len(spans), MODES, channels), f32),
            pltpu.VMEM((len(spans) + 2, MODES, channels), f32),
            pltpu.SemaphoreType.DMA((len(spans) + 2,)),
            pltpu.SemaphoreType.DMA((len(spans) + 2,)),
        ],
        compiler_params=pltpu.CompilerParams(collective_id=0, has_side_effects=True),
        interpret=INTERPRET,
    )(own_state, factors)

    wide = lambda *lead: pl.BlockSpec(tuple(lead) + (LANES_FIX,), lambda c: (0,) * len(lead) + (c,))
    return pl.pallas_call(
        fix_kernel,
        grid=(channels // LANES_FIX,),
        in_specs=[wide(row_count), wide(row_count), wide(MODES, 16), wide(MODES), wide(MODES), wide(MODES),
                  fixed(4, row_count, LANES)],
        out_specs=wide(row_count),
        out_shape=jax.ShapeDtypeStruct((row_count, channels), jnp.bfloat16),
        interpret=INTERPRET,
    )(acc, q_short, cl, incoming, amp, log_decay, masks)


def solution(mesh):
    in_specs = (
        P("ctx", "tp"),
        P("ctx", "tp"),
        P("ctx", "tp"),
        P(None, None, "tp"),
        P(None, "tp"),
        P(None, "tp"),
        P("tp"),
        P(),
    )
    out_specs = P("ctx", "tp")
    return jax.shard_map(body, mesh=mesh, in_specs=in_specs, out_specs=out_specs, check_vma=False)
```

```python
import functools

import jax
import jax.numpy as jnp
from jax import lax
from jax.experimental import pallas as pl
from jax.experimental.pallas import tpu as pltpu
from jax.sharding import PartitionSpec as P

MODES = 16
TAPS = 7
LANES = 128
LANES_FIX = 256
SEGMENTS = 8
INTERPRET = False


def from_behind(value, axis, steps):
    count = lax.axis_size(axis)
    first, last = (max(0, -steps), min(count, count - steps))
    return lax.ppermute(value, axis, [(source, source + steps) for source in range(first, last)])


def local_kernel(q_ref, k_ref, v_ref, rim_ref, filt_ref, amp_ref, lam_ref, skip_ref, mask_ref,
                 acc_ref, qs_ref, cl_ref, end_ref, ext_ref, g_ref):
    since_ref, keep_ref = mask_ref.at[0], mask_ref.at[1]
    rows = q_ref.shape[0]
    seg_rows = rows // SEGMENTS
    since = since_ref[...]
    filtered = []
    for branch, src in enumerate((q_ref, k_ref, v_ref)):
        ext_ref[8 - TAPS + 1:8, :] = rim_ref[branch].astype(jnp.float32)
        ext_ref[8:8 + rows, :] = src[...].astype(jnp.float32)
        total = jnp.zeros((rows, LANES), jnp.float32)
        for lag in range(TAPS):
            window = ext_ref[8 - lag:8 - lag + rows, :]
            tap = filt_ref[branch, lag:lag + 1, :]
            total = total + jnp.where(since >= float(lag), tap * window, 0.0)
        filtered.append(total)
    qs_ref[...] = filtered[0]
    g_ref[...] = (filtered[1] * filtered[2]).astype(jnp.bfloat16).astype(jnp.float32)
    lam = [jnp.broadcast_to(lam_ref[m:m + 1, :], (SEGMENTS, LANES)) for m in range(MODES)]
    amp = [jnp.broadcast_to(amp_ref[m:m + 1, :], (SEGMENTS, LANES)) for m in range(MODES)]
    skip = jnp.broadcast_to(skip_ref[...], (SEGMENTS, LANES))

    def step(j, states):
        x = g_ref[pl.ds(j, SEGMENTS, stride=seg_rows), :]
        keep = keep_ref[pl.ds(j, SEGMENTS, stride=seg_rows), :]
        new_states = []
        y = skip * x
        for m in range(MODES):
            h = lam[m] * (keep * states[m]) + x
            new_states.append(h)
            y = y + amp[m] * h
        acc_ref[pl.ds(j, SEGMENTS, stride=seg_rows), :] = y
        return tuple(new_states)

    zero = jnp.zeros((SEGMENTS, LANES), jnp.float32)
    ends = lax.fori_loop(0, seg_rows, step, tuple([zero] * MODES))
    segkeep = mask_ref[3, 0:SEGMENTS, :]
    for m in range(MODES):
        seg_decay = jnp.exp(float(seg_rows) * jnp.log(lam_ref[m:m + 1, :]))
        carried = jnp.zeros((1, LANES), jnp.float32)
        cl_ref[m, 0:1, :] = carried
        for p in range(SEGMENTS):
            carried = ends[m][p:p + 1, :] + segkeep[p:p + 1, :] * seg_decay * carried
            cl_ref[m, p + 1:p + 2, :] = carried
        cl_ref[m, SEGMENTS + 1:, :] = jnp.zeros((16 - SEGMENTS - 1, LANES), jnp.float32)
        end_ref[m:m + 1, :] = carried


def fix_kernel(acc_ref, qs_ref, cl_ref, hin_ref, amp_ref, logl_ref, mask_ref, out_ref):
    rows, width = acc_ref.shape
    seg_rows = rows // SEGMENTS
    copies = width // LANES
    widen = lambda part: jnp.concatenate([part] * copies, axis=1) if copies > 1 else part
    seg_index = lax.broadcasted_iota(jnp.int32, (SEGMENTS, width), 0).astype(jnp.float32)
    lag_index = lax.broadcasted_iota(jnp.int32, (seg_rows, width), 0).astype(jnp.float32) + 1.0
    opened = widen(mask_ref[3, 8:8 + SEGMENTS, :])
    starts = []
    powers = []
    for m in range(MODES):
        logl = logl_ref[m:m + 1, :]
        start = cl_ref[m, 0:SEGMENTS, :] + opened * jnp.exp(seg_index * (float(seg_rows) * logl)) * hin_ref[m:m + 1, :]
        starts.append(start)
        powers.append(amp_ref[m:m + 1, :] * jnp.exp(lag_index * logl))
    for p in range(SEGMENTS):
        lo = p * seg_rows
        corr = jnp.zeros((seg_rows, width), jnp.float32)
        for m in range(MODES):
            corr = corr + powers[m] * starts[m][p:p + 1, :]
        conv = acc_ref[lo:lo + seg_rows, :] + widen(mask_ref[2, lo:lo + seg_rows, :]) * corr
        out_ref[lo:lo + seg_rows, :] = (qs_ref[lo:lo + seg_rows, :] * conv).astype(out_ref.dtype)


def scan_kernel(count, rounds, span, own_ref, fac_ref, out_ref, sums, slots, send_sems, recv_sems):
    me = lax.axis_index("ctx")
    lane = lax.axis_index("tp")
    offsets = sorted({k * d for d, radix in rounds for k in range(1, radix)} | {1, 1 + span})
    barrier = pltpu.get_barrier_semaphore()
    for d in offsets:
        for other in (me - d, me + d):
            @pl.when((other >= 0) & (other < count))
            def _():
                pl.semaphore_signal(barrier, inc=1, device_id=(other, lane), device_id_type=pl.DeviceIdType.MESH)
    partners = 0
    for d in offsets:
        partners = partners + (me + count - d) // count + (2 * count - 1 - me - d) // count
    pl.semaphore_wait(barrier, partners)

    def transfer(src, slot, target):
        return pltpu.make_async_remote_copy(
            src_ref=src, dst_ref=slots.at[slot], send_sem=send_sems.at[slot], recv_sem=recv_sems.at[slot],
            device_id=(target, lane), device_id_type=pl.DeviceIdType.MESH)

    def exchange(src, sends):
        for slot, d in sends:
            @pl.when(me + d < count)
            def _():
                transfer(src, slot, me + d).start()

    def settle(src, sends):
        for slot, d in sends:
            @pl.when(me + d < count)
            def _():
                transfer(src, slot, me + d).wait_send()

    def gather(src, dst, sends, first):
        for slot, d in sends:
            @pl.when(me - d >= 0)
            def _():
                transfer(src, slot, me - d).wait_recv()
                dst[...] = dst[...] + fac_ref[slot] * slots[slot]

    current = own_ref
    slot = 0
    for r, (d, radix) in enumerate(rounds):
        sends = [(slot + k - 1, k * d) for k in range(1, radix)]
        slot += radix - 1
        exchange(current, sends)
        sums[r] = current[...]
        gather(current, sums.at[r], sends, True)
        settle(current, sends)
        current = sums.at[r]
    final = [(slot, 1), (slot + 1, 1 + span)]
    exchange(current, final)
    out_ref[...] = jnp.zeros(out_ref.shape, out_ref.dtype)
    gather(current, out_ref, final, False)
    settle(current, final)


def body(query_proj, key_proj, value_proj, short_filter, residues, decay_rate, skip_gain, doc_lengths):
    row_count, channels = query_proj.shape
    ctx_count = lax.axis_size("ctx")
    my_index = lax.axis_index("ctx")
    first_row = my_index * row_count
    seg_rows = row_count // SEGMENTS
    local_rows = jnp.arange(row_count, dtype=jnp.int32)
    positions = first_row + local_rows
    doc_starts = jnp.cumsum(doc_lengths) - doc_lengths
    row_start = jnp.max(
        jnp.where(doc_starts[None, :] <= positions[:, None], doc_starts[None, :], 0), axis=1
    )
    since = (positions - row_start).astype(jnp.float32)
    keep = (positions != row_start).astype(jnp.float32)
    seg_first = first_row + (local_rows // seg_rows) * seg_rows
    cont = (row_start < seg_first).astype(jnp.float32)
    seg_ids = jnp.arange(SEGMENTS, dtype=jnp.int32)
    seg_lo = first_row + seg_ids * seg_rows
    in_seg = (doc_starts[None, :] >= seg_lo[:, None]) & (doc_starts[None, :] < seg_lo[:, None] + seg_rows)
    segkeep = 1.0 - jnp.any(in_seg, axis=1).astype(jnp.float32)
    before = (doc_starts[None, :] >= first_row) & (doc_starts[None, :] < seg_lo[:, None])
    opened = 1.0 - jnp.any(before, axis=1).astype(jnp.float32)

    small = jnp.zeros((row_count,), jnp.float32).at[0:SEGMENTS].set(segkeep).at[8:8 + SEGMENTS].set(opened)
    masks = jnp.broadcast_to(jnp.stack([since, keep, cont, small])[:, :, None], (4, row_count, LANES))

    stacked = jnp.stack([query_proj, key_proj, value_proj])
    rim = from_behind(stacked[:, row_count - TAPS + 1:, :], "ctx", 1)
    log_decay = jnp.log1p(-decay_rate)
    lam = jnp.exp(log_decay)
    amp = residues * jnp.sqrt(decay_rate * (2.0 - decay_rate))
    tiles = channels // LANES
    col = lambda *lead: pl.BlockSpec(tuple(lead) + (LANES,), lambda c: (0,) * len(lead) + (c,))
    fixed = lambda *shape: pl.BlockSpec(shape, lambda c: (0,) * len(shape))
    f32 = jnp.float32
    acc, q_short, cl, own_state = pl.pallas_call(
        local_kernel,
        grid=(tiles,),
        in_specs=[col(row_count), col(row_count), col(row_count), col(3, TAPS - 1), col(3, TAPS), col(MODES), col(MODES),
                  col(1), fixed(4, row_count, LANES)],
        out_specs=[col(row_count), col(row_count), col(MODES, 16), col(MODES)],
        out_shape=[jax.ShapeDtypeStruct((row_count, channels), f32), jax.ShapeDtypeStruct((row_count, channels), f32),
                   jax.ShapeDtypeStruct((MODES, 16, channels), f32), jax.ShapeDtypeStruct((MODES, channels), f32)],
        scratch_shapes=[pltpu.VMEM((row_count + 8, LANES), f32), pltpu.VMEM((row_count, LANES), f32)],
        interpret=INTERPRET,
    )(query_proj, key_proj, value_proj, rim, short_filter, amp, lam, skip_gain[None, :], masks)

    def starts_between(low_device, high_device):
        low_row = jnp.maximum(low_device, 0) * row_count
        high_row = (high_device + 1) * row_count
        return jnp.any((doc_starts >= low_row) & (doc_starts < high_row)).astype(jnp.float32)

    rounds = []
    span = 1
    while 2 * span < ctx_count:
        radix = max(2, min(4, -(-(ctx_count // 2) // span)))
        rounds.append((span, radix))
        span *= radix
    factors = []
    for d, radix in rounds:
        for k in range(1, radix):
            open_path = 1.0 - starts_between(my_index - k * d + 1, my_index)
            factors.append(open_path * jnp.exp(float(k * d * row_count) * log_decay))
    factors.append(jnp.ones_like(log_decay))
    open_path = 1.0 - starts_between(my_index - span, my_index - 1)
    factors.append(open_path * jnp.exp(float(span * row_count) * log_decay))
    factors = jnp.stack(factors)
    slot_count = factors.shape[0]
    vmem = pl.BlockSpec(memory_space=pltpu.VMEM)
    incoming = pl.pallas_call(
        functools.partial(scan_kernel, ctx_count, tuple(rounds), span),
        out_shape=jax.ShapeDtypeStruct((MODES, channels), f32),
        in_specs=[vmem, vmem],
        out_specs=vmem,
        scratch_shapes=[
            pltpu.VMEM((len(rounds), MODES, channels), f32),
            pltpu.VMEM((slot_count, MODES, channels), f32),
            pltpu.SemaphoreType.DMA((slot_count,)),
            pltpu.SemaphoreType.DMA((slot_count,)),
        ],
        compiler_params=pltpu.CompilerParams(collective_id=0, has_side_effects=True),
        interpret=INTERPRET,
    )(own_state, factors)

    wide = lambda *lead: pl.BlockSpec(tuple(lead) + (LANES_FIX,), lambda c: (0,) * len(lead) + (c,))
    return pl.pallas_call(
        fix_kernel,
        grid=(channels // LANES_FIX,),
        in_specs=[wide(row_count), wide(row_count), wide(MODES, 16), wide(MODES), wide(MODES), wide(MODES),
                  fixed(4, row_count, LANES)],
        out_specs=wide(row_count),
        out_shape=jax.ShapeDtypeStruct((row_count, channels), jnp.bfloat16),
        interpret=INTERPRET,
    )(acc, q_short, cl, incoming, amp, log_decay, masks)


def solution(mesh):
    in_specs = (
        P("ctx", "tp"),
        P("ctx", "tp"),
        P("ctx", "tp"),
        P(None, None, "tp"),
        P(None, "tp"),
        P(None, "tp"),
        P("tp"),
        P(),
    )
    out_specs = P("ctx", "tp")
    return jax.shard_map(body, mesh=mesh, in_specs=in_specs, out_specs=out_specs, check_vma=False)
```

```python
import functools

import jax
import jax.numpy as jnp
from jax import lax
from jax.experimental import pallas as pl
from jax.experimental.pallas import tpu as pltpu
from jax.sharding import PartitionSpec as P

MODES = 16
TAPS = 7
LANES = 128
LANES_FIX = 256
SEGMENTS = 8
INTERPRET = False


def from_behind(value, axis, steps):
    count = lax.axis_size(axis)
    first, last = (max(0, -steps), min(count, count - steps))
    return lax.ppermute(value, axis, [(source, source + steps) for source in range(first, last)])


def short_conv(block, rim_rows, taps, since, ext_ref):
    rows = block.shape[0]
    ext_ref[8 - TAPS + 1:8, :] = rim_rows.astype(jnp.float32)
    ext_ref[8:8 + rows, :] = block.astype(jnp.float32)
    total = jnp.zeros((rows, LANES), jnp.float32)
    for lag in range(TAPS):
        window = ext_ref[8 - lag:8 - lag + rows, :]
        total = total + jnp.where(since >= float(lag), taps[lag:lag + 1, :] * window, 0.0)
    return total


def local_kernel(k_ref, v_ref, rim_ref, filt_ref, amp_ref, lam_ref, skip_ref, mask_ref,
                 acc_ref, cl_ref, end_ref, ext_ref, g_ref):
    since_ref, keep_ref = mask_ref.at[0], mask_ref.at[1]
    rows = k_ref.shape[0]
    seg_rows = rows // SEGMENTS
    since = since_ref[...]
    filtered = [short_conv(src[...], rim_ref[branch], filt_ref[branch], since, ext_ref)
                for branch, src in ((1, k_ref), (2, v_ref))]
    g_ref[...] = (filtered[0] * filtered[1]).astype(jnp.bfloat16).astype(jnp.float32)
    lam = [jnp.broadcast_to(lam_ref[m:m + 1, :], (SEGMENTS, LANES)) for m in range(MODES)]
    amp = [jnp.broadcast_to(amp_ref[m:m + 1, :], (SEGMENTS, LANES)) for m in range(MODES)]
    skip = jnp.broadcast_to(skip_ref[...], (SEGMENTS, LANES))

    def step(j, states):
        x = g_ref[pl.ds(j, SEGMENTS, stride=seg_rows), :]
        keep = keep_ref[pl.ds(j, SEGMENTS, stride=seg_rows), :]
        new_states = []
        y = skip * x
        for m in range(MODES):
            h = lam[m] * (keep * states[m]) + x
            new_states.append(h)
            y = y + amp[m] * h
        acc_ref[pl.ds(j, SEGMENTS, stride=seg_rows), :] = y
        return tuple(new_states)

    zero = jnp.zeros((SEGMENTS, LANES), jnp.float32)
    ends = lax.fori_loop(0, seg_rows, step, tuple([zero] * MODES))
    segkeep = mask_ref[3, 0:SEGMENTS, :]
    for m in range(MODES):
        seg_decay = jnp.exp(float(seg_rows) * jnp.log(lam_ref[m:m + 1, :]))
        carried = jnp.zeros((1, LANES), jnp.float32)
        cl_ref[m, 0:1, :] = carried
        for p in range(SEGMENTS):
            carried = ends[m][p:p + 1, :] + segkeep[p:p + 1, :] * seg_decay * carried
            cl_ref[m, p + 1:p + 2, :] = carried
        cl_ref[m, SEGMENTS + 1:, :] = jnp.zeros((16 - SEGMENTS - 1, LANES), jnp.float32)
        end_ref[m:m + 1, :] = carried


def fix_kernel(acc_ref, qs_ref, cl_ref, hin_ref, amp_ref, logl_ref, mask_ref, out_ref):
    rows, width = acc_ref.shape
    seg_rows = rows // SEGMENTS
    copies = width // LANES
    widen = lambda part: jnp.concatenate([part] * copies, axis=1) if copies > 1 else part
    seg_index = lax.broadcasted_iota(jnp.int32, (SEGMENTS, width), 0).astype(jnp.float32)
    lag_index = lax.broadcasted_iota(jnp.int32, (seg_rows, width), 0).astype(jnp.float32) + 1.0
    opened = widen(mask_ref[3, 8:8 + SEGMENTS, :])
    starts = []
    powers = []
    for m in range(MODES):
        logl = logl_ref[m:m + 1, :]
        start = cl_ref[m, 0:SEGMENTS, :] + opened * jnp.exp(seg_index * (float(seg_rows) * logl)) * hin_ref[m:m + 1, :]
        starts.append(start)
        powers.append(amp_ref[m:m + 1, :] * jnp.exp(lag_index * logl))
    for p in range(SEGMENTS):
        lo = p * seg_rows
        corr = jnp.zeros((seg_rows, width), jnp.float32)
        for m in range(MODES):
            corr = corr + powers[m] * starts[m][p:p + 1, :]
        conv = acc_ref[lo:lo + seg_rows, :] + widen(mask_ref[2, lo:lo + seg_rows, :]) * corr
        out_ref[lo:lo + seg_rows, :] = (qs_ref[lo:lo + seg_rows, :] * conv).astype(out_ref.dtype)


def scan_kernel(count, spans, own_ref, fac_ref, q_ref, rim_ref, filt_ref, mask_ref, out_ref, qs_ref, sums, slots,
                send_sems, recv_sems, ext_ref):
    columns = q_ref.shape[1] // LANES
    groups = len(spans) + 1
    since = mask_ref[0]

    def filter_columns(group):
        for c in range(group * columns // groups, (group + 1) * columns // groups):
            lanes = slice(c * LANES, (c + 1) * LANES)
            qs_ref[:, lanes] = short_conv(q_ref[:, lanes], rim_ref[0, :, lanes], filt_ref[0, :, lanes], since, ext_ref)

    me = lax.axis_index("ctx")
    lane = lax.axis_index("tp")
    last = spans[-1] * 2 if spans else 1
    offsets = sorted(set(spans) | {1, 1 + last})
    barrier = pltpu.get_barrier_semaphore()
    for d in offsets:
        for other in (me - d, me + d):
            @pl.when((other >= 0) & (other < count))
            def _():
                pl.semaphore_signal(barrier, inc=1, device_id=(other, lane), device_id_type=pl.DeviceIdType.MESH)
    partners = 0
    for d in offsets:
        partners = partners + (me + count - d) // count + (2 * count - 1 - me - d) // count
    pl.semaphore_wait(barrier, partners)

    def transfer(src, slot, target):
        return pltpu.make_async_remote_copy(
            src_ref=src, dst_ref=slots.at[slot], send_sem=send_sems.at[slot], recv_sem=recv_sems.at[slot],
            device_id=(target, lane), device_id_type=pl.DeviceIdType.MESH)

    def exchange(src, sends):
        for slot, d in sends:
            @pl.when(me + d < count)
            def _():
                transfer(src, slot, me + d).start()

    def settle(src, sends):
        for slot, d in sends:
            @pl.when(me + d < count)
            def _():
                transfer(src, slot, me + d).wait_send()

    current = own_ref
    for r, d in enumerate(spans):
        exchange(current, [(r, d)])
        filter_columns(r)

        @pl.when(me - d >= 0)
        def _():
            transfer(current, r, me - d).wait_recv()
            sums[r] = current[...] + fac_ref[r] * slots[r]

        @pl.when(me - d < 0)
        def _():
            sums[r] = current[...]
        settle(current, [(r, d)])
        current = sums.at[r]
    near, far = len(spans), len(spans) + 1
    final = [(near, 1), (far, 1 + last)]
    exchange(current, final)
    filter_columns(len(spans))
    out_ref[...] = jnp.zeros(out_ref.shape, out_ref.dtype)

    @pl.when(me - 1 >= 0)
    def _():
        transfer(current, near, me - 1).wait_recv()
        out_ref[...] = slots[near]

    @pl.when(me - 1 - last >= 0)
    def _():
        transfer(current, far, me - 1 - last).wait_recv()
        out_ref[...] = out_ref[...] + fac_ref[len(spans)] * slots[far]
    settle(current, final)


def body(query_proj, key_proj, value_proj, short_filter, residues, decay_rate, skip_gain, doc_lengths):
    row_count, channels = query_proj.shape
    ctx_count = lax.axis_size("ctx")
    my_index = lax.axis_index("ctx")
    first_row = my_index * row_count
    seg_rows = row_count // SEGMENTS
    local_rows = jnp.arange(row_count, dtype=jnp.int32)
    positions = first_row + local_rows
    doc_starts = jnp.cumsum(doc_lengths) - doc_lengths
    row_start = jnp.max(
        jnp.where(doc_starts[None, :] <= positions[:, None], doc_starts[None, :], 0), axis=1
    )
    since = (positions - row_start).astype(jnp.float32)
    keep = (positions != row_start).astype(jnp.float32)
    seg_first = first_row + (local_rows // seg_rows) * seg_rows
    cont = (row_start < seg_first).astype(jnp.float32)
    seg_ids = jnp.arange(SEGMENTS, dtype=jnp.int32)
    seg_lo = first_row + seg_ids * seg_rows
    in_seg = (doc_starts[None, :] >= seg_lo[:, None]) & (doc_starts[None, :] < seg_lo[:, None] + seg_rows)
    segkeep = 1.0 - jnp.any(in_seg, axis=1).astype(jnp.float32)
    before = (doc_starts[None, :] >= first_row) & (doc_starts[None, :] < seg_lo[:, None])
    opened = 1.0 - jnp.any(before, axis=1).astype(jnp.float32)

    small = jnp.zeros((row_count,), jnp.float32).at[0:SEGMENTS].set(segkeep).at[8:8 + SEGMENTS].set(opened)
    masks = jnp.broadcast_to(jnp.stack([since, keep, cont, small])[:, :, None], (4, row_count, LANES))

    stacked = jnp.stack([query_proj, key_proj, value_proj])
    rim = from_behind(stacked[:, row_count - TAPS + 1:, :], "ctx", 1)
    log_decay = jnp.log1p(-decay_rate)
    lam = jnp.exp(log_decay)
    amp = residues * jnp.sqrt(decay_rate * (2.0 - decay_rate))
    tiles = channels // LANES
    col = lambda *lead: pl.BlockSpec(tuple(lead) + (LANES,), lambda c: (0,) * len(lead) + (c,))
    fixed = lambda *shape: pl.BlockSpec(shape, lambda c: (0,) * len(shape))
    f32 = jnp.float32
    acc, cl, own_state = pl.pallas_call(
        local_kernel,
        grid=(tiles,),
        in_specs=[col(row_count), col(row_count), col(3, TAPS - 1), col(3, TAPS), col(MODES), col(MODES),
                  col(1), fixed(4, row_count, LANES)],
        out_specs=[col(row_count), col(MODES, 16), col(MODES)],
        out_shape=[jax.ShapeDtypeStruct((row_count, channels), f32),
                   jax.ShapeDtypeStruct((MODES, 16, channels), f32), jax.ShapeDtypeStruct((MODES, channels), f32)],
        scratch_shapes=[pltpu.VMEM((row_count + 8, LANES), f32), pltpu.VMEM((row_count, LANES), f32)],
        interpret=INTERPRET,
    )(key_proj, value_proj, rim, short_filter, amp, lam, skip_gain[None, :], masks)

    def starts_between(low_device, high_device):
        low_row = jnp.maximum(low_device, 0) * row_count
        high_row = (high_device + 1) * row_count
        return jnp.any((doc_starts >= low_row) & (doc_starts < high_row)).astype(jnp.float32)

    spans = []
    span = 1
    while 2 * span < ctx_count:
        spans.append(span)
        span *= 2
    factors = []
    for d in spans:
        open_path = 1.0 - starts_between(my_index - d + 1, my_index)
        factors.append(open_path * jnp.exp(float(d * row_count) * log_decay))
    open_path = 1.0 - starts_between(my_index - span, my_index - 1)
    factors.append(open_path * jnp.exp(float(span * row_count) * log_decay))
    factors = jnp.stack(factors)
    vmem = pl.BlockSpec(memory_space=pltpu.VMEM)
    incoming, q_short = pl.pallas_call(
        functools.partial(scan_kernel, ctx_count, tuple(spans)),
        out_shape=[jax.ShapeDtypeStruct((MODES, channels), f32), jax.ShapeDtypeStruct((row_count, channels), f32)],
        in_specs=[vmem] * 6,
        out_specs=[vmem, vmem],
        scratch_shapes=[
            pltpu.VMEM((len(spans), MODES, channels), f32),
            pltpu.VMEM((len(spans) + 2, MODES, channels), f32),
            pltpu.SemaphoreType.DMA((len(spans) + 2,)),
            pltpu.SemaphoreType.DMA((len(spans) + 2,)),
            pltpu.VMEM((row_count + 8, LANES), f32),
        ],
        compiler_params=pltpu.CompilerParams(collective_id=0, has_side_effects=True),
        interpret=INTERPRET,
    )(own_state, factors, query_proj, rim, short_filter, masks)

    wide = lambda *lead: pl.BlockSpec(tuple(lead) + (LANES_FIX,), lambda c: (0,) * len(lead) + (c,))
    return pl.pallas_call(
        fix_kernel,
        grid=(channels // LANES_FIX,),
        in_specs=[wide(row_count), wide(row_count), wide(MODES, 16), wide(MODES), wide(MODES), wide(MODES),
                  fixed(4, row_count, LANES)],
        out_specs=wide(row_count),
        out_shape=jax.ShapeDtypeStruct((row_count, channels), jnp.bfloat16),
        interpret=INTERPRET,
    )(acc, q_short, cl, incoming, amp, log_decay, masks)


def solution(mesh):
    in_specs = (
        P("ctx", "tp"),
        P("ctx", "tp"),
        P("ctx", "tp"),
        P(None, None, "tp"),
        P(None, "tp"),
        P(None, "tp"),
        P("tp"),
        P(),
    )
    out_specs = P("ctx", "tp")
    return jax.shard_map(body, mesh=mesh, in_specs=in_specs, out_specs=out_specs, check_vma=False)
```

```python
import functools

import jax
import jax.numpy as jnp
from jax import lax
from jax.experimental import pallas as pl
from jax.experimental.pallas import tpu as pltpu
from jax.sharding import PartitionSpec as P

MODES = 16
TAPS = 7
LANES = 128
LANES_FIX = 256
SEGMENTS = 8
INTERPRET = False


def from_behind(value, axis, steps):
    count = lax.axis_size(axis)
    first, last = (max(0, -steps), min(count, count - steps))
    return lax.ppermute(value, axis, [(source, source + steps) for source in range(first, last)])


def short_conv(block, rim_rows, taps, since, ext_ref):
    rows = block.shape[0]
    ext_ref[8 - TAPS + 1:8, :] = rim_rows.astype(jnp.float32)
    ext_ref[8:8 + rows, :] = block.astype(jnp.float32)
    total = jnp.zeros((rows, LANES), jnp.float32)
    for lag in range(TAPS):
        window = ext_ref[8 - lag:8 - lag + rows, :]
        total = total + jnp.where(since >= float(lag), taps[lag:lag + 1, :] * window, 0.0)
    return total


def local_kernel(k_ref, v_ref, rim_ref, filt_ref, amp_ref, lam_ref, skip_ref, mask_ref,
                 acc_ref, cl_ref, end_ref, ext_ref, g_ref):
    since_ref, keep_ref = mask_ref.at[0], mask_ref.at[1]
    rows = k_ref.shape[0]
    seg_rows = rows // SEGMENTS
    since = since_ref[...]
    filtered = [short_conv(src[...], rim_ref[branch], filt_ref[branch], since, ext_ref)
                for branch, src in ((1, k_ref), (2, v_ref))]
    g_ref[...] = (filtered[0] * filtered[1]).astype(jnp.bfloat16).astype(jnp.float32)
    lam = [jnp.broadcast_to(lam_ref[m:m + 1, :], (SEGMENTS, LANES)) for m in range(MODES)]
    amp = [jnp.broadcast_to(amp_ref[m:m + 1, :], (SEGMENTS, LANES)) for m in range(MODES)]
    skip = jnp.broadcast_to(skip_ref[...], (SEGMENTS, LANES))

    def step(j, states):
        x = g_ref[pl.ds(j, SEGMENTS, stride=seg_rows), :]
        keep = keep_ref[pl.ds(j, SEGMENTS, stride=seg_rows), :]
        new_states = [lam[m] * (keep * states[m]) + x for m in range(MODES)]
        terms = [amp[m] * new_states[m] for m in range(MODES)] + [skip * x]
        while len(terms) > 1:
            terms = [terms[i] + terms[i + 1] for i in range(0, len(terms) - 1, 2)] + terms[len(terms) - len(terms) % 2:]
        acc_ref[pl.ds(j, SEGMENTS, stride=seg_rows), :] = terms[0]
        return tuple(new_states)

    zero = jnp.zeros((SEGMENTS, LANES), jnp.float32)
    ends = lax.fori_loop(0, seg_rows, step, tuple([zero] * MODES), unroll=2)
    segkeep = mask_ref[3, 0:SEGMENTS, :]
    for m in range(MODES):
        seg_decay = jnp.exp(float(seg_rows) * jnp.log(lam_ref[m:m + 1, :]))
        carried = jnp.zeros((1, LANES), jnp.float32)
        cl_ref[m, 0:1, :] = carried
        for p in range(SEGMENTS):
            carried = ends[m][p:p + 1, :] + segkeep[p:p + 1, :] * seg_decay * carried
            cl_ref[m, p + 1:p + 2, :] = carried
        cl_ref[m, SEGMENTS + 1:, :] = jnp.zeros((16 - SEGMENTS - 1, LANES), jnp.float32)
        end_ref[m:m + 1, :] = carried


def fix_kernel(acc_ref, qs_ref, cl_ref, hin_ref, amp_ref, logl_ref, mask_ref, out_ref):
    rows, width = acc_ref.shape
    seg_rows = rows // SEGMENTS
    copies = width // LANES
    widen = lambda part: jnp.concatenate([part] * copies, axis=1) if copies > 1 else part
    seg_index = lax.broadcasted_iota(jnp.int32, (SEGMENTS, width), 0).astype(jnp.float32)
    lag_index = lax.broadcasted_iota(jnp.int32, (seg_rows, width), 0).astype(jnp.float32) + 1.0
    opened = widen(mask_ref[3, 8:8 + SEGMENTS, :])
    starts = []
    powers = []
    for m in range(MODES):
        logl = logl_ref[m:m + 1, :]
        start = cl_ref[m, 0:SEGMENTS, :] + opened * jnp.exp(seg_index * (float(seg_rows) * logl)) * hin_ref[m:m + 1, :]
        starts.append(start)
        powers.append(amp_ref[m:m + 1, :] * jnp.exp(lag_index * logl))
    for p in range(SEGMENTS):
        lo = p * seg_rows
        corr = jnp.zeros((seg_rows, width), jnp.float32)
        for m in range(MODES):
            corr = corr + powers[m] * starts[m][p:p + 1, :]
        conv = acc_ref[lo:lo + seg_rows, :] + widen(mask_ref[2, lo:lo + seg_rows, :]) * corr
        out_ref[lo:lo + seg_rows, :] = (qs_ref[lo:lo + seg_rows, :] * conv).astype(out_ref.dtype)


def scan_kernel(count, spans, own_ref, fac_ref, q_ref, rim_ref, filt_ref, mask_ref, out_ref, qs_ref, sums, slots,
                send_sems, recv_sems, ext_ref):
    columns = q_ref.shape[1] // LANES
    groups = len(spans) + 1
    since = mask_ref[0]

    def filter_columns(group):
        for c in range(group * columns // groups, (group + 1) * columns // groups):
            lanes = slice(c * LANES, (c + 1) * LANES)
            qs_ref[:, lanes] = short_conv(q_ref[:, lanes], rim_ref[0, :, lanes], filt_ref[0, :, lanes], since, ext_ref)

    me = lax.axis_index("ctx")
    lane = lax.axis_index("tp")
    last = spans[-1] * 2 if spans else 1
    offsets = sorted(set(spans) | {1, 1 + last})
    barrier = pltpu.get_barrier_semaphore()
    for d in offsets:
        for other in (me - d, me + d):
            @pl.when((other >= 0) & (other < count))
            def _():
                pl.semaphore_signal(barrier, inc=1, device_id=(other, lane), device_id_type=pl.DeviceIdType.MESH)
    partners = 0
    for d in offsets:
        partners = partners + (me + count - d) // count + (2 * count - 1 - me - d) // count
    pl.semaphore_wait(barrier, partners)

    def transfer(src, slot, target):
        return pltpu.make_async_remote_copy(
            src_ref=src, dst_ref=slots.at[slot], send_sem=send_sems.at[slot], recv_sem=recv_sems.at[slot],
            device_id=(target, lane), device_id_type=pl.DeviceIdType.MESH)

    def exchange(src, sends):
        for slot, d in sends:
            @pl.when(me + d < count)
            def _():
                transfer(src, slot, me + d).start()

    def settle(src, sends):
        for slot, d in sends:
            @pl.when(me + d < count)
            def _():
                transfer(src, slot, me + d).wait_send()

    current = own_ref
    for r, d in enumerate(spans):
        exchange(current, [(r, d)])
        filter_columns(r)

        @pl.when(me - d >= 0)
        def _():
            transfer(current, r, me - d).wait_recv()
            sums[r] = current[...] + fac_ref[r] * slots[r]

        @pl.when(me - d < 0)
        def _():
            sums[r] = current[...]
        settle(current, [(r, d)])
        current = sums.at[r]
    near, far = len(spans), len(spans) + 1
    final = [(near, 1), (far, 1 + last)]
    exchange(current, final)
    filter_columns(len(spans))
    out_ref[...] = jnp.zeros(out_ref.shape, out_ref.dtype)

    @pl.when(me - 1 >= 0)
    def _():
        transfer(current, near, me - 1).wait_recv()
        out_ref[...] = slots[near]

    @pl.when(me - 1 - last >= 0)
    def _():
        transfer(current, far, me - 1 - last).wait_recv()
        out_ref[...] = out_ref[...] + fac_ref[len(spans)] * slots[far]
    settle(current, final)


def body(query_proj, key_proj, value_proj, short_filter, residues, decay_rate, skip_gain, doc_lengths):
    row_count, channels = query_proj.shape
    ctx_count = lax.axis_size("ctx")
    my_index = lax.axis_index("ctx")
    first_row = my_index * row_count
    seg_rows = row_count // SEGMENTS
    local_rows = jnp.arange(row_count, dtype=jnp.int32)
    positions = first_row + local_rows
    doc_starts = jnp.cumsum(doc_lengths) - doc_lengths
    row_start = jnp.max(
        jnp.where(doc_starts[None, :] <= positions[:, None], doc_starts[None, :], 0), axis=1
    )
    since = (positions - row_start).astype(jnp.float32)
    keep = (positions != row_start).astype(jnp.float32)
    seg_first = first_row + (local_rows // seg_rows) * seg_rows
    cont = (row_start < seg_first).astype(jnp.float32)
    seg_ids = jnp.arange(SEGMENTS, dtype=jnp.int32)
    seg_lo = first_row + seg_ids * seg_rows
    in_seg = (doc_starts[None, :] >= seg_lo[:, None]) & (doc_starts[None, :] < seg_lo[:, None] + seg_rows)
    segkeep = 1.0 - jnp.any(in_seg, axis=1).astype(jnp.float32)
    before = (doc_starts[None, :] >= first_row) & (doc_starts[None, :] < seg_lo[:, None])
    opened = 1.0 - jnp.any(before, axis=1).astype(jnp.float32)

    small = jnp.zeros((row_count,), jnp.float32).at[0:SEGMENTS].set(segkeep).at[8:8 + SEGMENTS].set(opened)
    masks = jnp.broadcast_to(jnp.stack([since, keep, cont, small])[:, :, None], (4, row_count, LANES))

    stacked = jnp.stack([query_proj, key_proj, value_proj])
    rim = from_behind(stacked[:, row_count - TAPS + 1:, :], "ctx", 1)
    log_decay = jnp.log1p(-decay_rate)
    lam = jnp.exp(log_decay)
    amp = residues * jnp.sqrt(decay_rate * (2.0 - decay_rate))
    tiles = channels // LANES
    col = lambda *lead: pl.BlockSpec(tuple(lead) + (LANES,), lambda c: (0,) * len(lead) + (c,))
    fixed = lambda *shape: pl.BlockSpec(shape, lambda c: (0,) * len(shape))
    f32 = jnp.float32
    acc, cl, own_state = pl.pallas_call(
        local_kernel,
        grid=(tiles,),
        in_specs=[col(row_count), col(row_count), col(3, TAPS - 1), col(3, TAPS), col(MODES), col(MODES),
                  col(1), fixed(4, row_count, LANES)],
        out_specs=[col(row_count), col(MODES, 16), col(MODES)],
        out_shape=[jax.ShapeDtypeStruct((row_count, channels), f32),
                   jax.ShapeDtypeStruct((MODES, 16, channels), f32), jax.ShapeDtypeStruct((MODES, channels), f32)],
        scratch_shapes=[pltpu.VMEM((row_count + 8, LANES), f32), pltpu.VMEM((row_count, LANES), f32)],
        interpret=INTERPRET,
    )(key_proj, value_proj, rim, short_filter, amp, lam, skip_gain[None, :], masks)

    def starts_between(low_device, high_device):
        low_row = jnp.maximum(low_device, 0) * row_count
        high_row = (high_device + 1) * row_count
        return jnp.any((doc_starts >= low_row) & (doc_starts < high_row)).astype(jnp.float32)

    spans = []
    span = 1
    while 2 * span < ctx_count:
        spans.append(span)
        span *= 2
    factors = []
    for d in spans:
        open_path = 1.0 - starts_between(my_index - d + 1, my_index)
        factors.append(open_path * jnp.exp(float(d * row_count) * log_decay))
    open_path = 1.0 - starts_between(my_index - span, my_index - 1)
    factors.append(open_path * jnp.exp(float(span * row_count) * log_decay))
    factors = jnp.stack(factors)
    vmem = pl.BlockSpec(memory_space=pltpu.VMEM)
    incoming, q_short = pl.pallas_call(
        functools.partial(scan_kernel, ctx_count, tuple(spans)),
        out_shape=[jax.ShapeDtypeStruct((MODES, channels), f32), jax.ShapeDtypeStruct((row_count, channels), f32)],
        in_specs=[vmem] * 6,
        out_specs=[vmem, vmem],
        scratch_shapes=[
            pltpu.VMEM((len(spans), MODES, channels), f32),
            pltpu.VMEM((len(spans) + 2, MODES, channels), f32),
            pltpu.SemaphoreType.DMA((len(spans) + 2,)),
            pltpu.SemaphoreType.DMA((len(spans) + 2,)),
            pltpu.VMEM((row_count + 8, LANES), f32),
        ],
        compiler_params=pltpu.CompilerParams(collective_id=0, has_side_effects=True),
        interpret=INTERPRET,
    )(own_state, factors, query_proj, rim, short_filter, masks)

    wide = lambda *lead: pl.BlockSpec(tuple(lead) + (LANES_FIX,), lambda c: (0,) * len(lead) + (c,))
    return pl.pallas_call(
        fix_kernel,
        grid=(channels // LANES_FIX,),
        in_specs=[wide(row_count), wide(row_count), wide(MODES, 16), wide(MODES), wide(MODES), wide(MODES),
                  fixed(4, row_count, LANES)],
        out_specs=wide(row_count),
        out_shape=jax.ShapeDtypeStruct((row_count, channels), jnp.bfloat16),
        interpret=INTERPRET,
    )(acc, q_short, cl, incoming, amp, log_decay, masks)


def solution(mesh):
    in_specs = (
        P("ctx", "tp"),
        P("ctx", "tp"),
        P("ctx", "tp"),
        P(None, None, "tp"),
        P(None, "tp"),
        P(None, "tp"),
        P("tp"),
        P(),
    )
    out_specs = P("ctx", "tp")
    return jax.shard_map(body, mesh=mesh, in_specs=in_specs, out_specs=out_specs, check_vma=False)
```

```python
import functools

import jax
import jax.numpy as jnp
from jax import lax
from jax.experimental import pallas as pl
from jax.experimental.pallas import tpu as pltpu
from jax.sharding import PartitionSpec as P

MODES = 16
TAPS = 7
LANES = 128
LANES_FIX = 256
SEGMENTS = 8
INTERPRET = False


def from_behind(value, axis, steps):
    count = lax.axis_size(axis)
    first, last = (max(0, -steps), min(count, count - steps))
    return lax.ppermute(value, axis, [(source, source + steps) for source in range(first, last)])


def tree_sum(terms):
    while len(terms) > 1:
        terms = [terms[i] + terms[i + 1] for i in range(0, len(terms) - 1, 2)] + terms[len(terms) - len(terms) % 2:]
    return terms[0]


def short_conv(block, rim_rows, taps, since, ext_ref):
    rows = block.shape[0]
    ext_ref[8 - TAPS + 1:8, :] = rim_rows.astype(jnp.float32)
    ext_ref[8:8 + rows, :] = block.astype(jnp.float32)
    terms = [taps[0:1, :] * ext_ref[8:8 + rows, :]]
    for lag in range(1, TAPS):
        window = ext_ref[8 - lag:8 - lag + rows, :]
        terms.append(jnp.where(since >= float(lag), taps[lag:lag + 1, :] * window, 0.0))
    return tree_sum(terms)


def local_kernel(k_ref, v_ref, rim_ref, filt_ref, amp_ref, lam_ref, skip_ref, mask_ref,
                 acc_ref, cl_ref, end_ref, ext_ref, g_ref):
    since_ref, keep_ref = mask_ref.at[0], mask_ref.at[1]
    rows = k_ref.shape[0]
    seg_rows = rows // SEGMENTS
    since = since_ref[...]
    filtered = [short_conv(src[...], rim_ref[branch], filt_ref[branch], since, ext_ref)
                for branch, src in ((1, k_ref), (2, v_ref))]
    g_ref[...] = (filtered[0] * filtered[1]).astype(jnp.bfloat16).astype(jnp.float32)
    lam = [jnp.broadcast_to(lam_ref[m:m + 1, :], (SEGMENTS, LANES)) for m in range(MODES)]
    amp = [jnp.broadcast_to(amp_ref[m:m + 1, :], (SEGMENTS, LANES)) for m in range(MODES)]
    skip = jnp.broadcast_to(skip_ref[...], (SEGMENTS, LANES))

    def step(j, states):
        x = g_ref[pl.ds(j, SEGMENTS, stride=seg_rows), :]
        keep = keep_ref[pl.ds(j, SEGMENTS, stride=seg_rows), :]
        new_states = [lam[m] * (keep * states[m]) + x for m in range(MODES)]
        terms = [amp[m] * new_states[m] for m in range(MODES)] + [skip * x]
        acc_ref[pl.ds(j, SEGMENTS, stride=seg_rows), :] = tree_sum(terms)
        return tuple(new_states)

    zero = jnp.zeros((SEGMENTS, LANES), jnp.float32)
    ends = lax.fori_loop(0, seg_rows, step, tuple([zero] * MODES), unroll=2)
    segkeep = mask_ref[3, 0:SEGMENTS, :]
    for m in range(MODES):
        seg_decay = jnp.exp(float(seg_rows) * jnp.log(lam_ref[m:m + 1, :]))
        carried = jnp.zeros((1, LANES), jnp.float32)
        cl_ref[m, 0:1, :] = carried
        for p in range(SEGMENTS):
            carried = ends[m][p:p + 1, :] + segkeep[p:p + 1, :] * seg_decay * carried
            cl_ref[m, p + 1:p + 2, :] = carried
        cl_ref[m, SEGMENTS + 1:, :] = jnp.zeros((16 - SEGMENTS - 1, LANES), jnp.float32)
        end_ref[m:m + 1, :] = carried


def fix_kernel(acc_ref, qs_ref, cl_ref, hin_ref, amp_ref, logl_ref, mask_ref, out_ref):
    rows, width = acc_ref.shape
    seg_rows = rows // SEGMENTS
    copies = width // LANES
    widen = lambda part: jnp.concatenate([part] * copies, axis=1) if copies > 1 else part
    seg_index = lax.broadcasted_iota(jnp.int32, (SEGMENTS, width), 0).astype(jnp.float32)
    lag_index = lax.broadcasted_iota(jnp.int32, (seg_rows, width), 0).astype(jnp.float32) + 1.0
    opened = widen(mask_ref[3, 8:8 + SEGMENTS, :])
    starts = []
    powers = []
    for m in range(MODES):
        logl = logl_ref[m:m + 1, :]
        start = cl_ref[m, 0:SEGMENTS, :] + opened * jnp.exp(seg_index * (float(seg_rows) * logl)) * hin_ref[m:m + 1, :]
        starts.append(start)
        powers.append(amp_ref[m:m + 1, :] * jnp.exp(lag_index * logl))
    for p in range(SEGMENTS):
        lo = p * seg_rows
        corr = tree_sum([powers[m] * starts[m][p:p + 1, :] for m in range(MODES)])
        conv = acc_ref[lo:lo + seg_rows, :] + widen(mask_ref[2, lo:lo + seg_rows, :]) * corr
        out_ref[lo:lo + seg_rows, :] = (qs_ref[lo:lo + seg_rows, :] * conv).astype(out_ref.dtype)


def scan_kernel(count, spans, own_ref, fac_ref, q_ref, rim_ref, filt_ref, mask_ref, out_ref, qs_ref, sums, slots,
                send_sems, recv_sems, ext_ref):
    columns = q_ref.shape[1] // LANES
    groups = len(spans) + 1
    since = mask_ref[0]

    def filter_columns(group):
        for c in range(group * columns // groups, (group + 1) * columns // groups):
            lanes = slice(c * LANES, (c + 1) * LANES)
            qs_ref[:, lanes] = short_conv(q_ref[:, lanes], rim_ref[0, :, lanes], filt_ref[0, :, lanes], since, ext_ref)

    me = lax.axis_index("ctx")
    lane = lax.axis_index("tp")
    last = spans[-1] * 2 if spans else 1
    offsets = sorted(set(spans) | {1, 1 + last})
    barrier = pltpu.get_barrier_semaphore()
    for d in offsets:
        for other in (me - d, me + d):
            @pl.when((other >= 0) & (other < count))
            def _():
                pl.semaphore_signal(barrier, inc=1, device_id=(other, lane), device_id_type=pl.DeviceIdType.MESH)
    partners = 0
    for d in offsets:
        partners = partners + (me + count - d) // count + (2 * count - 1 - me - d) // count
    pl.semaphore_wait(barrier, partners)

    def transfer(src, slot, target):
        return pltpu.make_async_remote_copy(
            src_ref=src, dst_ref=slots.at[slot], send_sem=send_sems.at[slot], recv_sem=recv_sems.at[slot],
            device_id=(target, lane), device_id_type=pl.DeviceIdType.MESH)

    def exchange(src, sends):
        for slot, d in sends:
            @pl.when(me + d < count)
            def _():
                transfer(src, slot, me + d).start()

    def settle(src, sends):
        for slot, d in sends:
            @pl.when(me + d < count)
            def _():
                transfer(src, slot, me + d).wait_send()

    current = own_ref
    for r, d in enumerate(spans):
        exchange(current, [(r, d)])
        filter_columns(r)

        @pl.when(me - d >= 0)
        def _():
            transfer(current, r, me - d).wait_recv()
            sums[r] = current[...] + fac_ref[r] * slots[r]

        @pl.when(me - d < 0)
        def _():
            sums[r] = current[...]
        settle(current, [(r, d)])
        current = sums.at[r]
    near, far = len(spans), len(spans) + 1
    final = [(near, 1), (far, 1 + last)]
    exchange(current, final)
    filter_columns(len(spans))
    out_ref[...] = jnp.zeros(out_ref.shape, out_ref.dtype)

    @pl.when(me - 1 >= 0)
    def _():
        transfer(current, near, me - 1).wait_recv()
        out_ref[...] = slots[near]

    @pl.when(me - 1 - last >= 0)
    def _():
        transfer(current, far, me - 1 - last).wait_recv()
        out_ref[...] = out_ref[...] + fac_ref[len(spans)] * slots[far]
    settle(current, final)


def body(query_proj, key_proj, value_proj, short_filter, residues, decay_rate, skip_gain, doc_lengths):
    row_count, channels = query_proj.shape
    ctx_count = lax.axis_size("ctx")
    my_index = lax.axis_index("ctx")
    first_row = my_index * row_count
    seg_rows = row_count // SEGMENTS
    local_rows = jnp.arange(row_count, dtype=jnp.int32)
    positions = first_row + local_rows
    doc_starts = jnp.cumsum(doc_lengths) - doc_lengths
    row_start = jnp.max(
        jnp.where(doc_starts[None, :] <= positions[:, None], doc_starts[None, :], 0), axis=1
    )
    since = (positions - row_start).astype(jnp.float32)
    keep = (positions != row_start).astype(jnp.float32)
    seg_first = first_row + (local_rows // seg_rows) * seg_rows
    cont = (row_start < seg_first).astype(jnp.float32)
    seg_ids = jnp.arange(SEGMENTS, dtype=jnp.int32)
    seg_lo = first_row + seg_ids * seg_rows
    in_seg = (doc_starts[None, :] >= seg_lo[:, None]) & (doc_starts[None, :] < seg_lo[:, None] + seg_rows)
    segkeep = 1.0 - jnp.any(in_seg, axis=1).astype(jnp.float32)
    before = (doc_starts[None, :] >= first_row) & (doc_starts[None, :] < seg_lo[:, None])
    opened = 1.0 - jnp.any(before, axis=1).astype(jnp.float32)

    small = jnp.zeros((row_count,), jnp.float32).at[0:SEGMENTS].set(segkeep).at[8:8 + SEGMENTS].set(opened)
    masks = jnp.broadcast_to(jnp.stack([since, keep, cont, small])[:, :, None], (4, row_count, LANES))

    stacked = jnp.stack([query_proj, key_proj, value_proj])
    rim = from_behind(stacked[:, row_count - TAPS + 1:, :], "ctx", 1)
    log_decay = jnp.log1p(-decay_rate)
    lam = jnp.exp(log_decay)
    amp = residues * jnp.sqrt(decay_rate * (2.0 - decay_rate))
    tiles = channels // LANES
    col = lambda *lead: pl.BlockSpec(tuple(lead) + (LANES,), lambda c: (0,) * len(lead) + (c,))
    fixed = lambda *shape: pl.BlockSpec(shape, lambda c: (0,) * len(shape))
    f32 = jnp.float32
    acc, cl, own_state = pl.pallas_call(
        local_kernel,
        grid=(tiles,),
        in_specs=[col(row_count), col(row_count), col(3, TAPS - 1), col(3, TAPS), col(MODES), col(MODES),
                  col(1), fixed(4, row_count, LANES)],
        out_specs=[col(row_count), col(MODES, 16), col(MODES)],
        out_shape=[jax.ShapeDtypeStruct((row_count, channels), f32),
                   jax.ShapeDtypeStruct((MODES, 16, channels), f32), jax.ShapeDtypeStruct((MODES, channels), f32)],
        scratch_shapes=[pltpu.VMEM((row_count + 8, LANES), f32), pltpu.VMEM((row_count, LANES), f32)],
        interpret=INTERPRET,
    )(key_proj, value_proj, rim, short_filter, amp, lam, skip_gain[None, :], masks)

    def starts_between(low_device, high_device):
        low_row = jnp.maximum(low_device, 0) * row_count
        high_row = (high_device + 1) * row_count
        return jnp.any((doc_starts >= low_row) & (doc_starts < high_row)).astype(jnp.float32)

    spans = []
    span = 1
    while 2 * span < ctx_count:
        spans.append(span)
        span *= 2
    factors = []
    for d in spans:
        open_path = 1.0 - starts_between(my_index - d + 1, my_index)
        factors.append(open_path * jnp.exp(float(d * row_count) * log_decay))
    open_path = 1.0 - starts_between(my_index - span, my_index - 1)
    factors.append(open_path * jnp.exp(float(span * row_count) * log_decay))
    factors = jnp.stack(factors)
    vmem = pl.BlockSpec(memory_space=pltpu.VMEM)
    incoming, q_short = pl.pallas_call(
        functools.partial(scan_kernel, ctx_count, tuple(spans)),
        out_shape=[jax.ShapeDtypeStruct((MODES, channels), f32), jax.ShapeDtypeStruct((row_count, channels), f32)],
        in_specs=[vmem] * 6,
        out_specs=[vmem, vmem],
        scratch_shapes=[
            pltpu.VMEM((len(spans), MODES, channels), f32),
            pltpu.VMEM((len(spans) + 2, MODES, channels), f32),
            pltpu.SemaphoreType.DMA((len(spans) + 2,)),
            pltpu.SemaphoreType.DMA((len(spans) + 2,)),
            pltpu.VMEM((row_count + 8, LANES), f32),
        ],
        compiler_params=pltpu.CompilerParams(collective_id=0, has_side_effects=True),
        interpret=INTERPRET,
    )(own_state, factors, query_proj, rim, short_filter, masks)

    wide = lambda *lead: pl.BlockSpec(tuple(lead) + (LANES_FIX,), lambda c: (0,) * len(lead) + (c,))
    return pl.pallas_call(
        fix_kernel,
        grid=(channels // LANES_FIX,),
        in_specs=[wide(row_count), wide(row_count), wide(MODES, 16), wide(MODES), wide(MODES), wide(MODES),
                  fixed(4, row_count, LANES)],
        out_specs=wide(row_count),
        out_shape=jax.ShapeDtypeStruct((row_count, channels), jnp.bfloat16),
        interpret=INTERPRET,
    )(acc, q_short, cl, incoming, amp, log_decay, masks)


def solution(mesh):
    in_specs = (
        P("ctx", "tp"),
        P("ctx", "tp"),
        P("ctx", "tp"),
        P(None, None, "tp"),
        P(None, "tp"),
        P(None, "tp"),
        P("tp"),
        P(),
    )
    out_specs = P("ctx", "tp")
    return jax.shard_map(body, mesh=mesh, in_specs=in_specs, out_specs=out_specs, check_vma=False)
```

```python
import functools

import jax
import jax.numpy as jnp
from jax import lax
from jax.experimental import pallas as pl
from jax.experimental.pallas import tpu as pltpu
from jax.sharding import PartitionSpec as P

MODES = 16
TAPS = 7
LANES = 128
LANES_FIX = 256
LANES_LOCAL = 512
SEGMENTS = 8
INTERPRET = False


def from_behind(value, axis, steps):
    count = lax.axis_size(axis)
    first, last = (max(0, -steps), min(count, count - steps))
    return lax.ppermute(value, axis, [(source, source + steps) for source in range(first, last)])


def short_conv(block, rim_rows, taps, since, ext_ref):
    rows = block.shape[0]
    ext_ref[8 - TAPS + 1:8, :] = rim_rows.astype(jnp.float32)
    ext_ref[8:8 + rows, :] = block.astype(jnp.float32)
    total = jnp.zeros((rows, LANES), jnp.float32)
    for lag in range(TAPS):
        window = ext_ref[8 - lag:8 - lag + rows, :]
        total = total + jnp.where(since >= float(lag), taps[lag:lag + 1, :] * window, 0.0)
    return total


def local_kernel(k_ref, v_ref, rim_ref, filt_ref, amp_ref, lam_ref, skip_ref, mask_ref,
                 acc_ref, cl_ref, end_ref, ext_ref, g_ref, sum_ref):
    since_ref, keep_ref = mask_ref.at[0], mask_ref.at[1]
    rows = k_ref.shape[0]
    seg_rows = rows // SEGMENTS
    since = since_ref[...]
    segkeep = mask_ref[3, 0:SEGMENTS, :]
    for c in range(k_ref.shape[1] // LANES):
        lanes = slice(c * LANES, (c + 1) * LANES)
        filtered = [short_conv(src[:, lanes], rim_ref[branch, :, lanes], filt_ref[branch, :, lanes], since, ext_ref)
                    for branch, src in ((1, k_ref), (2, v_ref))]
        g_ref[...] = (filtered[0] * filtered[1]).astype(jnp.bfloat16).astype(jnp.float32)
        lam = [jnp.broadcast_to(lam_ref[m:m + 1, lanes], (SEGMENTS, LANES)) for m in range(MODES)]
        amp = [jnp.broadcast_to(amp_ref[m:m + 1, lanes], (SEGMENTS, LANES)) for m in range(MODES)]
        skip = jnp.broadcast_to(skip_ref[:, lanes], (SEGMENTS, LANES))

        def step(j, states):
            x = g_ref[pl.ds(j, SEGMENTS, stride=seg_rows), :]
            keep = keep_ref[pl.ds(j, SEGMENTS, stride=seg_rows), :]
            new_states = [lam[m] * (keep * states[m]) + x for m in range(MODES)]
            terms = [amp[m] * new_states[m] for m in range(MODES)] + [skip * x]
            while len(terms) > 1:
                terms = [terms[i] + terms[i + 1] for i in range(0, len(terms) - 1, 2)] + terms[len(terms) - len(terms) % 2:]
            sum_ref[pl.ds(j, SEGMENTS, stride=seg_rows), :] = terms[0]
            return tuple(new_states)

        zero = jnp.zeros((SEGMENTS, LANES), jnp.float32)
        ends = lax.fori_loop(0, seg_rows, step, tuple([zero] * MODES), unroll=2)
        acc_ref[:, lanes] = sum_ref[...]
        for m in range(MODES):
            seg_decay = jnp.exp(float(seg_rows) * jnp.log(lam_ref[m:m + 1, lanes]))
            carried = jnp.zeros((1, LANES), jnp.float32)
            cl_ref[m, 0:1, lanes] = carried
            for p in range(SEGMENTS):
                carried = ends[m][p:p + 1, :] + segkeep[p:p + 1, :] * seg_decay * carried
                cl_ref[m, p + 1:p + 2, lanes] = carried
            cl_ref[m, SEGMENTS + 1:, lanes] = jnp.zeros((16 - SEGMENTS - 1, LANES), jnp.float32)
            end_ref[m:m + 1, lanes] = carried


def fix_kernel(acc_ref, qs_ref, cl_ref, hin_ref, amp_ref, logl_ref, mask_ref, out_ref):
    rows, width = acc_ref.shape
    seg_rows = rows // SEGMENTS
    copies = width // LANES
    widen = lambda part: jnp.concatenate([part] * copies, axis=1) if copies > 1 else part
    seg_index = lax.broadcasted_iota(jnp.int32, (SEGMENTS, width), 0).astype(jnp.float32)
    lag_index = lax.broadcasted_iota(jnp.int32, (seg_rows, width), 0).astype(jnp.float32) + 1.0
    opened = widen(mask_ref[3, 8:8 + SEGMENTS, :])
    starts = []
    powers = []
    for m in range(MODES):
        logl = logl_ref[m:m + 1, :]
        start = cl_ref[m, 0:SEGMENTS, :] + opened * jnp.exp(seg_index * (float(seg_rows) * logl)) * hin_ref[m:m + 1, :]
        starts.append(start)
        powers.append(amp_ref[m:m + 1, :] * jnp.exp(lag_index * logl))
    for p in range(SEGMENTS):
        lo = p * seg_rows
        corr = jnp.zeros((seg_rows, width), jnp.float32)
        for m in range(MODES):
            corr = corr + powers[m] * starts[m][p:p + 1, :]
        conv = acc_ref[lo:lo + seg_rows, :] + widen(mask_ref[2, lo:lo + seg_rows, :]) * corr
        out_ref[lo:lo + seg_rows, :] = (qs_ref[lo:lo + seg_rows, :] * conv).astype(out_ref.dtype)


def scan_kernel(count, spans, own_ref, fac_ref, q_ref, rim_ref, filt_ref, mask_ref, out_ref, qs_ref, sums, slots,
                send_sems, recv_sems, ext_ref):
    columns = q_ref.shape[1] // LANES
    groups = len(spans) + 1
    since = mask_ref[0]

    def filter_columns(group):
        for c in range(group * columns // groups, (group + 1) * columns // groups):
            lanes = slice(c * LANES, (c + 1) * LANES)
            qs_ref[:, lanes] = short_conv(q_ref[:, lanes], rim_ref[0, :, lanes], filt_ref[0, :, lanes], since, ext_ref)

    me = lax.axis_index("ctx")
    lane = lax.axis_index("tp")
    last = spans[-1] * 2 if spans else 1
    offsets = sorted(set(spans) | {1, 1 + last})
    barrier = pltpu.get_barrier_semaphore()
    for d in offsets:
        for other in (me - d, me + d):
            @pl.when((other >= 0) & (other < count))
            def _():
                pl.semaphore_signal(barrier, inc=1, device_id=(other, lane), device_id_type=pl.DeviceIdType.MESH)
    partners = 0
    for d in offsets:
        partners = partners + (me + count - d) // count + (2 * count - 1 - me - d) // count
    pl.semaphore_wait(barrier, partners)

    def transfer(src, slot, target):
        return pltpu.make_async_remote_copy(
            src_ref=src, dst_ref=slots.at[slot], send_sem=send_sems.at[slot], recv_sem=recv_sems.at[slot],
            device_id=(target, lane), device_id_type=pl.DeviceIdType.MESH)

    def exchange(src, sends):
        for slot, d in sends:
            @pl.when(me + d < count)
            def _():
                transfer(src, slot, me + d).start()

    def settle(src, sends):
        for slot, d in sends:
            @pl.when(me + d < count)
            def _():
                transfer(src, slot, me + d).wait_send()

    current = own_ref
    for r, d in enumerate(spans):
        exchange(current, [(r, d)])
        filter_columns(r)

        @pl.when(me - d >= 0)
        def _():
            transfer(current, r, me - d).wait_recv()
            sums[r] = current[...] + fac_ref[r] * slots[r]

        @pl.when(me - d < 0)
        def _():
            sums[r] = current[...]
        settle(current, [(r, d)])
        current = sums.at[r]
    near, far = len(spans), len(spans) + 1
    final = [(near, 1), (far, 1 + last)]
    exchange(current, final)
    filter_columns(len(spans))
    out_ref[...] = jnp.zeros(out_ref.shape, out_ref.dtype)

    @pl.when(me - 1 >= 0)
    def _():
        transfer(current, near, me - 1).wait_recv()
        out_ref[...] = slots[near]

    @pl.when(me - 1 - last >= 0)
    def _():
        transfer(current, far, me - 1 - last).wait_recv()
        out_ref[...] = out_ref[...] + fac_ref[len(spans)] * slots[far]
    settle(current, final)


def body(query_proj, key_proj, value_proj, short_filter, residues, decay_rate, skip_gain, doc_lengths):
    row_count, channels = query_proj.shape
    ctx_count = lax.axis_size("ctx")
    my_index = lax.axis_index("ctx")
    first_row = my_index * row_count
    seg_rows = row_count // SEGMENTS
    local_rows = jnp.arange(row_count, dtype=jnp.int32)
    positions = first_row + local_rows
    doc_starts = jnp.cumsum(doc_lengths) - doc_lengths
    row_start = jnp.max(
        jnp.where(doc_starts[None, :] <= positions[:, None], doc_starts[None, :], 0), axis=1
    )
    since = (positions - row_start).astype(jnp.float32)
    keep = (positions != row_start).astype(jnp.float32)
    seg_first = first_row + (local_rows // seg_rows) * seg_rows
    cont = (row_start < seg_first).astype(jnp.float32)
    seg_ids = jnp.arange(SEGMENTS, dtype=jnp.int32)
    seg_lo = first_row + seg_ids * seg_rows
    in_seg = (doc_starts[None, :] >= seg_lo[:, None]) & (doc_starts[None, :] < seg_lo[:, None] + seg_rows)
    segkeep = 1.0 - jnp.any(in_seg, axis=1).astype(jnp.float32)
    before = (doc_starts[None, :] >= first_row) & (doc_starts[None, :] < seg_lo[:, None])
    opened = 1.0 - jnp.any(before, axis=1).astype(jnp.float32)

    small = jnp.zeros((row_count,), jnp.float32).at[0:SEGMENTS].set(segkeep).at[8:8 + SEGMENTS].set(opened)
    masks = jnp.broadcast_to(jnp.stack([since, keep, cont, small])[:, :, None], (4, row_count, LANES))

    stacked = jnp.stack([query_proj, key_proj, value_proj])
    rim = from_behind(stacked[:, row_count - TAPS + 1:, :], "ctx", 1)
    log_decay = jnp.log1p(-decay_rate)
    lam = jnp.exp(log_decay)
    amp = residues * jnp.sqrt(decay_rate * (2.0 - decay_rate))
    tiles = channels // LANES
    col = lambda *lead: pl.BlockSpec(tuple(lead) + (LANES,), lambda c: (0,) * len(lead) + (c,))
    fixed = lambda *shape: pl.BlockSpec(shape, lambda c: (0,) * len(shape))
    f32 = jnp.float32
    cola = lambda *lead: pl.BlockSpec(tuple(lead) + (LANES_LOCAL,), lambda c: (0,) * len(lead) + (c,))
    acc, cl, own_state = pl.pallas_call(
        local_kernel,
        grid=(channels // LANES_LOCAL,),
        in_specs=[cola(row_count), cola(row_count), cola(3, TAPS - 1), cola(3, TAPS), cola(MODES), cola(MODES),
                  cola(1), fixed(4, row_count, LANES)],
        out_specs=[cola(row_count), cola(MODES, 16), cola(MODES)],
        out_shape=[jax.ShapeDtypeStruct((row_count, channels), f32),
                   jax.ShapeDtypeStruct((MODES, 16, channels), f32), jax.ShapeDtypeStruct((MODES, channels), f32)],
        scratch_shapes=[pltpu.VMEM((row_count + 8, LANES), f32), pltpu.VMEM((row_count, LANES), f32),
                        pltpu.VMEM((row_count, LANES), f32)],
        interpret=INTERPRET,
    )(key_proj, value_proj, rim, short_filter, amp, lam, skip_gain[None, :], masks)

    def starts_between(low_device, high_device):
        low_row = jnp.maximum(low_device, 0) * row_count
        high_row = (high_device + 1) * row_count
        return jnp.any((doc_starts >= low_row) & (doc_starts < high_row)).astype(jnp.float32)

    spans = []
    span = 1
    while 2 * span < ctx_count:
        spans.append(span)
        span *= 2
    factors = []
    for d in spans:
        open_path = 1.0 - starts_between(my_index - d + 1, my_index)
        factors.append(open_path * jnp.exp(float(d * row_count) * log_decay))
    open_path = 1.0 - starts_between(my_index - span, my_index - 1)
    factors.append(open_path * jnp.exp(float(span * row_count) * log_decay))
    factors = jnp.stack(factors)
    vmem = pl.BlockSpec(memory_space=pltpu.VMEM)
    incoming, q_short = pl.pallas_call(
        functools.partial(scan_kernel, ctx_count, tuple(spans)),
        out_shape=[jax.ShapeDtypeStruct((MODES, channels), f32), jax.ShapeDtypeStruct((row_count, channels), f32)],
        in_specs=[vmem] * 6,
        out_specs=[vmem, vmem],
        scratch_shapes=[
            pltpu.VMEM((len(spans), MODES, channels), f32),
            pltpu.VMEM((len(spans) + 2, MODES, channels), f32),
            pltpu.SemaphoreType.DMA((len(spans) + 2,)),
            pltpu.SemaphoreType.DMA((len(spans) + 2,)),
            pltpu.VMEM((row_count + 8, LANES), f32),
        ],
        compiler_params=pltpu.CompilerParams(collective_id=0, has_side_effects=True),
        interpret=INTERPRET,
    )(own_state, factors, query_proj, rim, short_filter, masks)

    wide = lambda *lead: pl.BlockSpec(tuple(lead) + (LANES_FIX,), lambda c: (0,) * len(lead) + (c,))
    return pl.pallas_call(
        fix_kernel,
        grid=(channels // LANES_FIX,),
        in_specs=[wide(row_count), wide(row_count), wide(MODES, 16), wide(MODES), wide(MODES), wide(MODES),
                  fixed(4, row_count, LANES)],
        out_specs=wide(row_count),
        out_shape=jax.ShapeDtypeStruct((row_count, channels), jnp.bfloat16),
        interpret=INTERPRET,
    )(acc, q_short, cl, incoming, amp, log_decay, masks)


def solution(mesh):
    in_specs = (
        P("ctx", "tp"),
        P("ctx", "tp"),
        P("ctx", "tp"),
        P(None, None, "tp"),
        P(None, "tp"),
        P(None, "tp"),
        P("tp"),
        P(),
    )
    out_specs = P("ctx", "tp")
    return jax.shard_map(body, mesh=mesh, in_specs=in_specs, out_specs=out_specs, check_vma=False)
```

```python
import functools

import jax
import jax.numpy as jnp
from jax import lax
from jax.experimental import pallas as pl
from jax.experimental.pallas import tpu as pltpu
from jax.sharding import PartitionSpec as P

MODES = 16
TAPS = 7
LANES = 128
LANES_FIX = 256
LANES_LOCAL = 512
SEGMENTS = 8
INTERPRET = False


def from_behind(value, axis, steps):
    count = lax.axis_size(axis)
    first, last = (max(0, -steps), min(count, count - steps))
    return lax.ppermute(value, axis, [(source, source + steps) for source in range(first, last)])


def short_conv(block, rim_rows, taps, since, ext_ref):
    rows = block.shape[0]
    ext_ref[8 - TAPS + 1:8, :] = rim_rows.astype(jnp.float32)
    ext_ref[8:8 + rows, :] = block.astype(jnp.float32)
    total = jnp.zeros((rows, LANES), jnp.float32)
    for lag in range(TAPS):
        window = ext_ref[8 - lag:8 - lag + rows, :]
        total = total + jnp.where(since >= float(lag), taps[lag:lag + 1, :] * window, 0.0)
    return total


def local_kernel(k_ref, v_ref, rim_ref, filt_ref, amp_ref, lam_ref, skip_ref, mask_ref,
                 acc_ref, cl_ref, end_ref, ext_ref, g_ref, sum_ref):
    since_ref, keep_ref = mask_ref.at[0], mask_ref.at[1]
    rows = k_ref.shape[0]
    seg_rows = rows // SEGMENTS
    since = since_ref[...]
    segkeep = mask_ref[3, 0:SEGMENTS, :]
    for c in range(k_ref.shape[1] // LANES):
        lanes = slice(c * LANES, (c + 1) * LANES)
        filtered = [short_conv(src[:, lanes], rim_ref[branch, :, lanes], filt_ref[branch, :, lanes], since, ext_ref)
                    for branch, src in ((1, k_ref), (2, v_ref))]
        g_ref[...] = (filtered[0] * filtered[1]).astype(jnp.bfloat16).astype(jnp.float32)
        lam = [jnp.broadcast_to(lam_ref[m:m + 1, lanes], (SEGMENTS, LANES)) for m in range(MODES)]
        amp = [jnp.broadcast_to(amp_ref[m:m + 1, lanes], (SEGMENTS, LANES)) for m in range(MODES)]
        skip = jnp.broadcast_to(skip_ref[:, lanes], (SEGMENTS, LANES))

        def step(j, states):
            x = g_ref[pl.ds(j, SEGMENTS, stride=seg_rows), :]
            keep = keep_ref[pl.ds(j, SEGMENTS, stride=seg_rows), :]
            new_states = [lam[m] * (keep * states[m]) + x for m in range(MODES)]
            terms = [amp[m] * new_states[m] for m in range(MODES)] + [skip * x]
            while len(terms) > 1:
                terms = [terms[i] + terms[i + 1] for i in range(0, len(terms) - 1, 2)] + terms[len(terms) - len(terms) % 2:]
            sum_ref[pl.ds(j, SEGMENTS, stride=seg_rows), :] = terms[0]
            return tuple(new_states)

        zero = jnp.zeros((SEGMENTS, LANES), jnp.float32)
        ends = lax.fori_loop(0, seg_rows, step, tuple([zero] * MODES), unroll=2)
        acc_ref[:, lanes] = sum_ref[...]
        for m in range(MODES):
            seg_decay = jnp.exp(float(seg_rows) * jnp.log(lam_ref[m:m + 1, lanes]))
            carried = jnp.zeros((1, LANES), jnp.float32)
            cl_ref[m, 0:1, lanes] = carried
            for p in range(SEGMENTS):
                carried = ends[m][p:p + 1, :] + segkeep[p:p + 1, :] * seg_decay * carried
                cl_ref[m, p + 1:p + 2, lanes] = carried
            cl_ref[m, SEGMENTS + 1:, lanes] = jnp.zeros((16 - SEGMENTS - 1, LANES), jnp.float32)
            end_ref[m:m + 1, lanes] = carried


def fix_kernel(acc_ref, qs_ref, cl_ref, hin_ref, amp_ref, logl_ref, mask_ref, out_ref):
    rows, width = acc_ref.shape
    seg_rows = rows // SEGMENTS
    copies = width // LANES
    widen = lambda part: jnp.concatenate([part] * copies, axis=1) if copies > 1 else part
    seg_index = lax.broadcasted_iota(jnp.int32, (SEGMENTS, width), 0).astype(jnp.float32)
    lag_index = lax.broadcasted_iota(jnp.int32, (seg_rows, width), 0).astype(jnp.float32) + 1.0
    opened = widen(mask_ref[3, 8:8 + SEGMENTS, :])
    starts = []
    powers = []
    for m in range(MODES):
        logl = logl_ref[m:m + 1, :]
        start = cl_ref[m, 0:SEGMENTS, :] + opened * jnp.exp(seg_index * (float(seg_rows) * logl)) * hin_ref[m:m + 1, :]
        starts.append(start)
        powers.append(amp_ref[m:m + 1, :] * jnp.exp(lag_index * logl))
    for p in range(SEGMENTS):
        lo = p * seg_rows
        corr = jnp.zeros((seg_rows, width), jnp.float32)
        for m in range(MODES):
            corr = corr + powers[m] * starts[m][p:p + 1, :]
        conv = acc_ref[lo:lo + seg_rows, :] + widen(mask_ref[2, lo:lo + seg_rows, :]) * corr
        out_ref[lo:lo + seg_rows, :] = (qs_ref[lo:lo + seg_rows, :] * conv).astype(out_ref.dtype)


def scan_kernel(count, spans, own_ref, fac_ref, q_ref, rim_ref, filt_ref, mask_ref, out_ref, qs_ref, sums, slots,
                send_sems, recv_sems, ext_ref):
    columns = q_ref.shape[1] // LANES
    groups = len(spans) + 1
    since = mask_ref[0]

    def filter_columns(group):
        for c in range(group * columns // groups, (group + 1) * columns // groups):
            lanes = slice(c * LANES, (c + 1) * LANES)
            qs_ref[:, lanes] = short_conv(q_ref[:, lanes], rim_ref[0, :, lanes], filt_ref[0, :, lanes], since, ext_ref)

    me = lax.axis_index("ctx")
    lane = lax.axis_index("tp")
    last = spans[-1] * 2 if spans else 1
    offsets = sorted(set(spans) | {1, 1 + last})
    barrier = pltpu.get_barrier_semaphore()
    for d in offsets:
        for other in (me - d, me + d):
            @pl.when((other >= 0) & (other < count))
            def _():
                pl.semaphore_signal(barrier, inc=1, device_id=(other, lane), device_id_type=pl.DeviceIdType.MESH)
    partners = 0
    for d in offsets:
        partners = partners + (me + count - d) // count + (2 * count - 1 - me - d) // count
    pl.semaphore_wait(barrier, partners)

    def transfer(src, slot, target):
        return pltpu.make_async_remote_copy(
            src_ref=src, dst_ref=slots.at[slot], send_sem=send_sems.at[slot], recv_sem=recv_sems.at[slot],
            device_id=(target, lane), device_id_type=pl.DeviceIdType.MESH)

    def exchange(src, sends):
        for slot, d in sends:
            @pl.when(me + d < count)
            def _():
                transfer(src, slot, me + d).start()

    def settle(src, sends):
        for slot, d in sends:
            @pl.when(me + d < count)
            def _():
                transfer(src, slot, me + d).wait_send()

    current = own_ref
    for r, d in enumerate(spans):
        exchange(current, [(r, d)])
        filter_columns(r)

        @pl.when(me - d >= 0)
        def _():
            transfer(current, r, me - d).wait_recv()
            sums[r] = current[...] + fac_ref[r] * slots[r]

        @pl.when(me - d < 0)
        def _():
            sums[r] = current[...]
        settle(current, [(r, d)])
        current = sums.at[r]
    near, far = len(spans), len(spans) + 1
    final = [(near, 1), (far, 1 + last)]
    exchange(current, final)
    filter_columns(len(spans))
    out_ref[...] = jnp.zeros(out_ref.shape, out_ref.dtype)

    @pl.when(me - 1 >= 0)
    def _():
        transfer(current, near, me - 1).wait_recv()
        out_ref[...] = slots[near]

    @pl.when(me - 1 - last >= 0)
    def _():
        transfer(current, far, me - 1 - last).wait_recv()
        out_ref[...] = out_ref[...] + fac_ref[len(spans)] * slots[far]
    settle(current, final)


def rim_kernel(count, tail_ref, out_ref, slot, send_sem, recv_sem):
    me = lax.axis_index("ctx")
    lane = lax.axis_index("tp")
    barrier = pltpu.get_barrier_semaphore()
    for other in (me - 1, me + 1):
        @pl.when((other >= 0) & (other < count))
        def _():
            pl.semaphore_signal(barrier, inc=1, device_id=(other, lane), device_id_type=pl.DeviceIdType.MESH)
    pl.semaphore_wait(barrier, (me + count - 1) // count + (2 * count - 2 - me) // count)

    def transfer(target):
        return pltpu.make_async_remote_copy(
            src_ref=tail_ref, dst_ref=slot, send_sem=send_sem, recv_sem=recv_sem,
            device_id=(target, lane), device_id_type=pl.DeviceIdType.MESH)

    @pl.when(me + 1 < count)
    def _():
        transfer(me + 1).start()
    out_ref[...] = jnp.zeros(out_ref.shape, out_ref.dtype)

    @pl.when(me >= 1)
    def _():
        transfer(me - 1).wait_recv()
        out_ref[...] = slot[...]

    @pl.when(me + 1 < count)
    def _():
        transfer(me + 1).wait_send()


def body(query_proj, key_proj, value_proj, short_filter, residues, decay_rate, skip_gain, doc_lengths):
    row_count, channels = query_proj.shape
    ctx_count = lax.axis_size("ctx")
    my_index = lax.axis_index("ctx")
    first_row = my_index * row_count
    seg_rows = row_count // SEGMENTS
    local_rows = jnp.arange(row_count, dtype=jnp.int32)
    positions = first_row + local_rows
    doc_starts = jnp.cumsum(doc_lengths) - doc_lengths
    row_start = jnp.max(
        jnp.where(doc_starts[None, :] <= positions[:, None], doc_starts[None, :], 0), axis=1
    )
    since = (positions - row_start).astype(jnp.float32)
    keep = (positions != row_start).astype(jnp.float32)
    seg_first = first_row + (local_rows // seg_rows) * seg_rows
    cont = (row_start < seg_first).astype(jnp.float32)
    seg_ids = jnp.arange(SEGMENTS, dtype=jnp.int32)
    seg_lo = first_row + seg_ids * seg_rows
    in_seg = (doc_starts[None, :] >= seg_lo[:, None]) & (doc_starts[None, :] < seg_lo[:, None] + seg_rows)
    segkeep = 1.0 - jnp.any(in_seg, axis=1).astype(jnp.float32)
    before = (doc_starts[None, :] >= first_row) & (doc_starts[None, :] < seg_lo[:, None])
    opened = 1.0 - jnp.any(before, axis=1).astype(jnp.float32)

    small = jnp.zeros((row_count,), jnp.float32).at[0:SEGMENTS].set(segkeep).at[8:8 + SEGMENTS].set(opened)
    masks = jnp.broadcast_to(jnp.stack([since, keep, cont, small])[:, :, None], (4, row_count, LANES))

    stacked = jnp.stack([query_proj, key_proj, value_proj])
    tail = stacked[:, row_count - TAPS + 1:, :]
    rim = pl.pallas_call(
        functools.partial(rim_kernel, ctx_count),
        out_shape=jax.ShapeDtypeStruct(tail.shape, tail.dtype),
        in_specs=[pl.BlockSpec(memory_space=pltpu.VMEM)],
        out_specs=pl.BlockSpec(memory_space=pltpu.VMEM),
        scratch_shapes=[pltpu.VMEM(tail.shape, tail.dtype), pltpu.SemaphoreType.DMA, pltpu.SemaphoreType.DMA],
        compiler_params=pltpu.CompilerParams(collective_id=1, has_side_effects=True),
        interpret=INTERPRET,
    )(tail)
    log_decay = jnp.log1p(-decay_rate)
    lam = jnp.exp(log_decay)
    amp = residues * jnp.sqrt(decay_rate * (2.0 - decay_rate))
    tiles = channels // LANES
    col = lambda *lead: pl.BlockSpec(tuple(lead) + (LANES,), lambda c: (0,) * len(lead) + (c,))
    fixed = lambda *shape: pl.BlockSpec(shape, lambda c: (0,) * len(shape))
    f32 = jnp.float32
    cola = lambda *lead: pl.BlockSpec(tuple(lead) + (LANES_LOCAL,), lambda c: (0,) * len(lead) + (c,))
    acc, cl, own_state = pl.pallas_call(
        local_kernel,
        grid=(channels // LANES_LOCAL,),
        in_specs=[cola(row_count), cola(row_count), cola(3, TAPS - 1), cola(3, TAPS), cola(MODES), cola(MODES),
                  cola(1), fixed(4, row_count, LANES)],
        out_specs=[cola(row_count), cola(MODES, 16), cola(MODES)],
        out_shape=[jax.ShapeDtypeStruct((row_count, channels), f32),
                   jax.ShapeDtypeStruct((MODES, 16, channels), f32), jax.ShapeDtypeStruct((MODES, channels), f32)],
        scratch_shapes=[pltpu.VMEM((row_count + 8, LANES), f32), pltpu.VMEM((row_count, LANES), f32),
                        pltpu.VMEM((row_count, LANES), f32)],
        interpret=INTERPRET,
    )(key_proj, value_proj, rim, short_filter, amp, lam, skip_gain[None, :], masks)

    def starts_between(low_device, high_device):
        low_row = jnp.maximum(low_device, 0) * row_count
        high_row = (high_device + 1) * row_count
        return jnp.any((doc_starts >= low_row) & (doc_starts < high_row)).astype(jnp.float32)

    spans = []
    span = 1
    while 2 * span < ctx_count:
        spans.append(span)
        span *= 2
    factors = []
    for d in spans:
        open_path = 1.0 - starts_between(my_index - d + 1, my_index)
        factors.append(open_path * jnp.exp(float(d * row_count) * log_decay))
    open_path = 1.0 - starts_between(my_index - span, my_index - 1)
    factors.append(open_path * jnp.exp(float(span * row_count) * log_decay))
    factors = jnp.stack(factors)
    vmem = pl.BlockSpec(memory_space=pltpu.VMEM)
    incoming, q_short = pl.pallas_call(
        functools.partial(scan_kernel, ctx_count, tuple(spans)),
        out_shape=[jax.ShapeDtypeStruct((MODES, channels), f32), jax.ShapeDtypeStruct((row_count, channels), f32)],
        in_specs=[vmem] * 6,
        out_specs=[vmem, vmem],
        scratch_shapes=[
            pltpu.VMEM((len(spans), MODES, channels), f32),
            pltpu.VMEM((len(spans) + 2, MODES, channels), f32),
            pltpu.SemaphoreType.DMA((len(spans) + 2,)),
            pltpu.SemaphoreType.DMA((len(spans) + 2,)),
            pltpu.VMEM((row_count + 8, LANES), f32),
        ],
        compiler_params=pltpu.CompilerParams(collective_id=0, has_side_effects=True),
        interpret=INTERPRET,
    )(own_state, factors, query_proj, rim, short_filter, masks)

    wide = lambda *lead: pl.BlockSpec(tuple(lead) + (LANES_FIX,), lambda c: (0,) * len(lead) + (c,))
    return pl.pallas_call(
        fix_kernel,
        grid=(channels // LANES_FIX,),
        in_specs=[wide(row_count), wide(row_count), wide(MODES, 16), wide(MODES), wide(MODES), wide(MODES),
                  fixed(4, row_count, LANES)],
        out_specs=wide(row_count),
        out_shape=jax.ShapeDtypeStruct((row_count, channels), jnp.bfloat16),
        interpret=INTERPRET,
    )(acc, q_short, cl, incoming, amp, log_decay, masks)


def solution(mesh):
    in_specs = (
        P("ctx", "tp"),
        P("ctx", "tp"),
        P("ctx", "tp"),
        P(None, None, "tp"),
        P(None, "tp"),
        P(None, "tp"),
        P("tp"),
        P(),
    )
    out_specs = P("ctx", "tp")
    return jax.shard_map(body, mesh=mesh, in_specs=in_specs, out_specs=out_specs, check_vma=False)
```

```python
import functools

import jax
import jax.numpy as jnp
from jax import lax
from jax.experimental import pallas as pl
from jax.experimental.pallas import tpu as pltpu
from jax.sharding import PartitionSpec as P

MODES = 16
TAPS = 7
LANES = 128
LANES_FIX = 256
LANES_LOCAL = 512
SEGMENTS = 8
INTERPRET = False


def from_behind(value, axis, steps):
    count = lax.axis_size(axis)
    first, last = (max(0, -steps), min(count, count - steps))
    return lax.ppermute(value, axis, [(source, source + steps) for source in range(first, last)])


def short_conv(block, rim_rows, taps, since, ext_ref):
    rows = block.shape[0]
    ext_ref[8 - TAPS + 1:8, :] = rim_rows.astype(jnp.float32)
    ext_ref[8:8 + rows, :] = block.astype(jnp.float32)
    total = jnp.zeros((rows, LANES), jnp.float32)
    for lag in range(TAPS):
        window = ext_ref[8 - lag:8 - lag + rows, :]
        total = total + jnp.where(since >= float(lag), taps[lag:lag + 1, :] * window, 0.0)
    return total


def local_kernel(k_ref, v_ref, rim_ref, filt_ref, amp_ref, lam_ref, skip_ref, mask_ref,
                 acc_ref, cl_ref, end_ref, ext_ref, g_ref, sum_ref):
    since_ref, keep_ref = mask_ref.at[0], mask_ref.at[1]
    rows = k_ref.shape[0]
    seg_rows = rows // SEGMENTS
    since = since_ref[...]
    segkeep = mask_ref[3, 0:SEGMENTS, :]
    for c in range(k_ref.shape[1] // LANES):
        lanes = slice(c * LANES, (c + 1) * LANES)
        filtered = [short_conv(src[:, lanes], rim_ref[branch, :, lanes], filt_ref[branch, :, lanes], since, ext_ref)
                    for branch, src in ((1, k_ref), (2, v_ref))]
        g_ref[...] = (filtered[0] * filtered[1]).astype(jnp.bfloat16).astype(jnp.float32)
        lam = [jnp.broadcast_to(lam_ref[m:m + 1, lanes], (SEGMENTS, LANES)) for m in range(MODES)]
        amp = [jnp.broadcast_to(amp_ref[m:m + 1, lanes], (SEGMENTS, LANES)) for m in range(MODES)]
        skip = jnp.broadcast_to(skip_ref[:, lanes], (SEGMENTS, LANES))

        def step(j, states):
            x = g_ref[pl.ds(j, SEGMENTS, stride=seg_rows), :]
            keep = keep_ref[pl.ds(j, SEGMENTS, stride=seg_rows), :]
            new_states = [(lam[m] * keep) * states[m] + x for m in range(MODES)]
            terms = [amp[m] * new_states[m] for m in range(MODES)] + [skip * x]
            while len(terms) > 1:
                terms = [terms[i] + terms[i + 1] for i in range(0, len(terms) - 1, 2)] + terms[len(terms) - len(terms) % 2:]
            sum_ref[pl.ds(j, SEGMENTS, stride=seg_rows), :] = terms[0]
            return tuple(new_states)

        zero = jnp.zeros((SEGMENTS, LANES), jnp.float32)
        ends = lax.fori_loop(0, seg_rows, step, tuple([zero] * MODES), unroll=2)
        acc_ref[:, lanes] = sum_ref[...]
        for m in range(MODES):
            seg_decay = jnp.exp(float(seg_rows) * jnp.log(lam_ref[m:m + 1, lanes]))
            carried = jnp.zeros((1, LANES), jnp.float32)
            cl_ref[m, 0:1, lanes] = carried
            for p in range(SEGMENTS):
                carried = ends[m][p:p + 1, :] + segkeep[p:p + 1, :] * seg_decay * carried
                cl_ref[m, p + 1:p + 2, lanes] = carried
            cl_ref[m, SEGMENTS + 1:, lanes] = jnp.zeros((16 - SEGMENTS - 1, LANES), jnp.float32)
            end_ref[m:m + 1, lanes] = carried


def fix_kernel(acc_ref, qs_ref, cl_ref, hin_ref, amp_ref, logl_ref, mask_ref, out_ref):
    rows, width = acc_ref.shape
    seg_rows = rows // SEGMENTS
    copies = width // LANES
    widen = lambda part: jnp.concatenate([part] * copies, axis=1) if copies > 1 else part
    seg_index = lax.broadcasted_iota(jnp.int32, (SEGMENTS, width), 0).astype(jnp.float32)
    lag_index = lax.broadcasted_iota(jnp.int32, (seg_rows, width), 0).astype(jnp.float32) + 1.0
    opened = widen(mask_ref[3, 8:8 + SEGMENTS, :])
    starts = []
    powers = []
    for m in range(MODES):
        logl = logl_ref[m:m + 1, :]
        start = cl_ref[m, 0:SEGMENTS, :] + opened * jnp.exp(seg_index * (float(seg_rows) * logl)) * hin_ref[m:m + 1, :]
        starts.append(start)
        powers.append(amp_ref[m:m + 1, :] * jnp.exp(lag_index * logl))
    for p in range(SEGMENTS):
        lo = p * seg_rows
        corr = jnp.zeros((seg_rows, width), jnp.float32)
        for m in range(MODES):
            corr = corr + powers[m] * starts[m][p:p + 1, :]
        conv = acc_ref[lo:lo + seg_rows, :] + widen(mask_ref[2, lo:lo + seg_rows, :]) * corr
        out_ref[lo:lo + seg_rows, :] = (qs_ref[lo:lo + seg_rows, :] * conv).astype(out_ref.dtype)


def scan_kernel(count, spans, own_ref, fac_ref, q_ref, rim_ref, filt_ref, mask_ref, out_ref, qs_ref, sums, slots,
                send_sems, recv_sems, ext_ref):
    columns = q_ref.shape[1] // LANES
    groups = len(spans) + 1
    since = mask_ref[0]

    def filter_columns(group):
        for c in range(group * columns // groups, (group + 1) * columns // groups):
            lanes = slice(c * LANES, (c + 1) * LANES)
            qs_ref[:, lanes] = short_conv(q_ref[:, lanes], rim_ref[0, :, lanes], filt_ref[0, :, lanes], since, ext_ref)

    me = lax.axis_index("ctx")
    lane = lax.axis_index("tp")
    last = spans[-1] * 2 if spans else 1
    offsets = sorted(set(spans) | {1, 1 + last})
    barrier = pltpu.get_barrier_semaphore()
    for d in offsets:
        for other in (me - d, me + d):
            @pl.when((other >= 0) & (other < count))
            def _():
                pl.semaphore_signal(barrier, inc=1, device_id=(other, lane), device_id_type=pl.DeviceIdType.MESH)
    partners = 0
    for d in offsets:
        partners = partners + (me + count - d) // count + (2 * count - 1 - me - d) // count
    pl.semaphore_wait(barrier, partners)

    def transfer(src, slot, target):
        return pltpu.make_async_remote_copy(
            src_ref=src, dst_ref=slots.at[slot], send_sem=send_sems.at[slot], recv_sem=recv_sems.at[slot],
            device_id=(target, lane), device_id_type=pl.DeviceIdType.MESH)

    def exchange(src, sends):
        for slot, d in sends:
            @pl.when(me + d < count)
            def _():
                transfer(src, slot, me + d).start()

    def settle(src, sends):
        for slot, d in sends:
            @pl.when(me + d < count)
            def _():
                transfer(src, slot, me + d).wait_send()

    current = own_ref
    for r, d in enumerate(spans):
        exchange(current, [(r, d)])
        filter_columns(r)

        @pl.when(me - d >= 0)
        def _():
            transfer(current, r, me - d).wait_recv()
            sums[r] = current[...] + fac_ref[r] * slots[r]

        @pl.when(me - d < 0)
        def _():
            sums[r] = current[...]
        settle(current, [(r, d)])
        current = sums.at[r]
    near, far = len(spans), len(spans) + 1
    final = [(near, 1), (far, 1 + last)]
    exchange(current, final)
    filter_columns(len(spans))
    out_ref[...] = jnp.zeros(out_ref.shape, out_ref.dtype)

    @pl.when(me - 1 >= 0)
    def _():
        transfer(current, near, me - 1).wait_recv()
        out_ref[...] = slots[near]

    @pl.when(me - 1 - last >= 0)
    def _():
        transfer(current, far, me - 1 - last).wait_recv()
        out_ref[...] = out_ref[...] + fac_ref[len(spans)] * slots[far]
    settle(current, final)


def body(query_proj, key_proj, value_proj, short_filter, residues, decay_rate, skip_gain, doc_lengths):
    row_count, channels = query_proj.shape
    ctx_count = lax.axis_size("ctx")
    my_index = lax.axis_index("ctx")
    first_row = my_index * row_count
    seg_rows = row_count // SEGMENTS
    local_rows = jnp.arange(row_count, dtype=jnp.int32)
    positions = first_row + local_rows
    doc_starts = jnp.cumsum(doc_lengths) - doc_lengths
    row_start = jnp.max(
        jnp.where(doc_starts[None, :] <= positions[:, None], doc_starts[None, :], 0), axis=1
    )
    since = (positions - row_start).astype(jnp.float32)
    keep = (positions != row_start).astype(jnp.float32)
    seg_first = first_row + (local_rows // seg_rows) * seg_rows
    cont = (row_start < seg_first).astype(jnp.float32)
    seg_ids = jnp.arange(SEGMENTS, dtype=jnp.int32)
    seg_lo = first_row + seg_ids * seg_rows
    in_seg = (doc_starts[None, :] >= seg_lo[:, None]) & (doc_starts[None, :] < seg_lo[:, None] + seg_rows)
    segkeep = 1.0 - jnp.any(in_seg, axis=1).astype(jnp.float32)
    before = (doc_starts[None, :] >= first_row) & (doc_starts[None, :] < seg_lo[:, None])
    opened = 1.0 - jnp.any(before, axis=1).astype(jnp.float32)

    small = jnp.zeros((row_count,), jnp.float32).at[0:SEGMENTS].set(segkeep).at[8:8 + SEGMENTS].set(opened)
    masks = jnp.broadcast_to(jnp.stack([since, keep, cont, small])[:, :, None], (4, row_count, LANES))

    stacked = jnp.stack([query_proj, key_proj, value_proj])
    rim = from_behind(stacked[:, row_count - TAPS + 1:, :], "ctx", 1)
    log_decay = jnp.log1p(-decay_rate)
    lam = jnp.exp(log_decay)
    amp = residues * jnp.sqrt(decay_rate * (2.0 - decay_rate))
    tiles = channels // LANES
    col = lambda *lead: pl.BlockSpec(tuple(lead) + (LANES,), lambda c: (0,) * len(lead) + (c,))
    fixed = lambda *shape: pl.BlockSpec(shape, lambda c: (0,) * len(shape))
    f32 = jnp.float32
    cola = lambda *lead: pl.BlockSpec(tuple(lead) + (LANES_LOCAL,), lambda c: (0,) * len(lead) + (c,))
    acc, cl, own_state = pl.pallas_call(
        local_kernel,
        grid=(channels // LANES_LOCAL,),
        in_specs=[cola(row_count), cola(row_count), cola(3, TAPS - 1), cola(3, TAPS), cola(MODES), cola(MODES),
                  cola(1), fixed(4, row_count, LANES)],
        out_specs=[cola(row_count), cola(MODES, 16), cola(MODES)],
        out_shape=[jax.ShapeDtypeStruct((row_count, channels), f32),
                   jax.ShapeDtypeStruct((MODES, 16, channels), f32), jax.ShapeDtypeStruct((MODES, channels), f32)],
        scratch_shapes=[pltpu.VMEM((row_count + 8, LANES), f32), pltpu.VMEM((row_count, LANES), f32),
                        pltpu.VMEM((row_count, LANES), f32)],
        interpret=INTERPRET,
    )(key_proj, value_proj, rim, short_filter, amp, lam, skip_gain[None, :], masks)

    def starts_between(low_device, high_device):
        low_row = jnp.maximum(low_device, 0) * row_count
        high_row = (high_device + 1) * row_count
        return jnp.any((doc_starts >= low_row) & (doc_starts < high_row)).astype(jnp.float32)

    spans = []
    span = 1
    while 2 * span < ctx_count:
        spans.append(span)
        span *= 2
    factors = []
    for d in spans:
        open_path = 1.0 - starts_between(my_index - d + 1, my_index)
        factors.append(open_path * jnp.exp(float(d * row_count) * log_decay))
    open_path = 1.0 - starts_between(my_index - span, my_index - 1)
    factors.append(open_path * jnp.exp(float(span * row_count) * log_decay))
    factors = jnp.stack(factors)
    vmem = pl.BlockSpec(memory_space=pltpu.VMEM)
    incoming, q_short = pl.pallas_call(
        functools.partial(scan_kernel, ctx_count, tuple(spans)),
        out_shape=[jax.ShapeDtypeStruct((MODES, channels), f32), jax.ShapeDtypeStruct((row_count, channels), f32)],
        in_specs=[vmem] * 6,
        out_specs=[vmem, vmem],
        scratch_shapes=[
            pltpu.VMEM((len(spans), MODES, channels), f32),
            pltpu.VMEM((len(spans) + 2, MODES, channels), f32),
            pltpu.SemaphoreType.DMA((len(spans) + 2,)),
            pltpu.SemaphoreType.DMA((len(spans) + 2,)),
            pltpu.VMEM((row_count + 8, LANES), f32),
        ],
        compiler_params=pltpu.CompilerParams(collective_id=0, has_side_effects=True),
        interpret=INTERPRET,
    )(own_state, factors, query_proj, rim, short_filter, masks)

    wide = lambda *lead: pl.BlockSpec(tuple(lead) + (LANES_FIX,), lambda c: (0,) * len(lead) + (c,))
    return pl.pallas_call(
        fix_kernel,
        grid=(channels // LANES_FIX,),
        in_specs=[wide(row_count), wide(row_count), wide(MODES, 16), wide(MODES), wide(MODES), wide(MODES),
                  fixed(4, row_count, LANES)],
        out_specs=wide(row_count),
        out_shape=jax.ShapeDtypeStruct((row_count, channels), jnp.bfloat16),
        interpret=INTERPRET,
    )(acc, q_short, cl, incoming, amp, log_decay, masks)


def solution(mesh):
    in_specs = (
        P("ctx", "tp"),
        P("ctx", "tp"),
        P("ctx", "tp"),
        P(None, None, "tp"),
        P(None, "tp"),
        P(None, "tp"),
        P("tp"),
        P(),
    )
    out_specs = P("ctx", "tp")
    return jax.shard_map(body, mesh=mesh, in_specs=in_specs, out_specs=out_specs, check_vma=False)
```

```python
import functools

import jax
import jax.numpy as jnp
from jax import lax
from jax.experimental import pallas as pl
from jax.experimental.pallas import tpu as pltpu
from jax.sharding import PartitionSpec as P

MODES = 16
TAPS = 7
LANES = 128
LANES_FIX = 512
LANES_LOCAL = 512
SEGMENTS = 8
INTERPRET = False


def from_behind(value, axis, steps):
    count = lax.axis_size(axis)
    first, last = (max(0, -steps), min(count, count - steps))
    return lax.ppermute(value, axis, [(source, source + steps) for source in range(first, last)])


def short_conv(block, rim_rows, taps, since, ext_ref):
    rows = block.shape[0]
    ext_ref[8 - TAPS + 1:8, :] = rim_rows.astype(jnp.float32)
    ext_ref[8:8 + rows, :] = block.astype(jnp.float32)
    total = jnp.zeros((rows, LANES), jnp.float32)
    for lag in range(TAPS):
        window = ext_ref[8 - lag:8 - lag + rows, :]
        total = total + jnp.where(since >= float(lag), taps[lag:lag + 1, :] * window, 0.0)
    return total


def local_kernel(k_ref, v_ref, rim_ref, filt_ref, amp_ref, lam_ref, skip_ref, mask_ref,
                 acc_ref, cl_ref, end_ref, ext_ref, g_ref, sum_ref):
    since_ref, keep_ref = mask_ref.at[0], mask_ref.at[1]
    rows = k_ref.shape[0]
    seg_rows = rows // SEGMENTS
    since = since_ref[...]
    segkeep = mask_ref[3, 0:SEGMENTS, :]
    for c in range(k_ref.shape[1] // LANES):
        lanes = slice(c * LANES, (c + 1) * LANES)
        filtered = [short_conv(src[:, lanes], rim_ref[branch, :, lanes], filt_ref[branch, :, lanes], since, ext_ref)
                    for branch, src in ((1, k_ref), (2, v_ref))]
        g_ref[...] = (filtered[0] * filtered[1]).astype(jnp.bfloat16).astype(jnp.float32)
        lam = [jnp.broadcast_to(lam_ref[m:m + 1, lanes], (SEGMENTS, LANES)) for m in range(MODES)]
        amp = [jnp.broadcast_to(amp_ref[m:m + 1, lanes], (SEGMENTS, LANES)) for m in range(MODES)]
        skip = jnp.broadcast_to(skip_ref[:, lanes], (SEGMENTS, LANES))

        def step(j, states):
            x = g_ref[pl.ds(j, SEGMENTS, stride=seg_rows), :]
            keep = keep_ref[pl.ds(j, SEGMENTS, stride=seg_rows), :]
            new_states = [(lam[m] * keep) * states[m] + x for m in range(MODES)]
            terms = [amp[m] * new_states[m] for m in range(MODES)] + [skip * x]
            while len(terms) > 1:
                terms = [terms[i] + terms[i + 1] for i in range(0, len(terms) - 1, 2)] + terms[len(terms) - len(terms) % 2:]
            sum_ref[pl.ds(j, SEGMENTS, stride=seg_rows), :] = terms[0]
            return tuple(new_states)

        zero = jnp.zeros((SEGMENTS, LANES), jnp.float32)
        ends = lax.fori_loop(0, seg_rows, step, tuple([zero] * MODES), unroll=2)
        acc_ref[:, lanes] = sum_ref[...]
        for m in range(MODES):
            seg_decay = jnp.exp(float(seg_rows) * jnp.log(lam_ref[m:m + 1, lanes]))
            carried = jnp.zeros((1, LANES), jnp.float32)
            cl_ref[m, 0:1, lanes] = carried
            for p in range(SEGMENTS):
                carried = ends[m][p:p + 1, :] + segkeep[p:p + 1, :] * seg_decay * carried
                cl_ref[m, p + 1:p + 2, lanes] = carried
            cl_ref[m, SEGMENTS + 1:, lanes] = jnp.zeros((16 - SEGMENTS - 1, LANES), jnp.float32)
            end_ref[m:m + 1, lanes] = carried


def fix_kernel(acc_ref, qs_ref, cl_ref, hin_ref, amp_ref, logl_ref, mask_ref, out_ref):
    rows, width = acc_ref.shape
    seg_rows = rows // SEGMENTS
    copies = width // LANES
    widen = lambda part: jnp.concatenate([part] * copies, axis=1) if copies > 1 else part
    seg_index = lax.broadcasted_iota(jnp.int32, (SEGMENTS, width), 0).astype(jnp.float32)
    lag_index = lax.broadcasted_iota(jnp.int32, (seg_rows, width), 0).astype(jnp.float32) + 1.0
    opened = widen(mask_ref[3, 8:8 + SEGMENTS, :])
    starts = []
    powers = []
    for m in range(MODES):
        logl = logl_ref[m:m + 1, :]
        start = cl_ref[m, 0:SEGMENTS, :] + opened * jnp.exp(seg_index * (float(seg_rows) * logl)) * hin_ref[m:m + 1, :]
        starts.append(start)
        powers.append(amp_ref[m:m + 1, :] * jnp.exp(lag_index * logl))
    for p in range(SEGMENTS):
        lo = p * seg_rows
        corr = jnp.zeros((seg_rows, width), jnp.float32)
        for m in range(MODES):
            corr = corr + powers[m] * starts[m][p:p + 1, :]
        conv = acc_ref[lo:lo + seg_rows, :] + widen(mask_ref[2, lo:lo + seg_rows, :]) * corr
        out_ref[lo:lo + seg_rows, :] = (qs_ref[lo:lo + seg_rows, :] * conv).astype(out_ref.dtype)


def scan_kernel(count, spans, own_ref, fac_ref, q_ref, rim_ref, filt_ref, mask_ref, out_ref, qs_ref, sums, slots,
                send_sems, recv_sems, ext_ref):
    columns = q_ref.shape[1] // LANES
    groups = len(spans) + 1
    since = mask_ref[0]

    def filter_columns(group):
        for c in range(group * columns // groups, (group + 1) * columns // groups):
            lanes = slice(c * LANES, (c + 1) * LANES)
            qs_ref[:, lanes] = short_conv(q_ref[:, lanes], rim_ref[0, :, lanes], filt_ref[0, :, lanes], since, ext_ref)

    me = lax.axis_index("ctx")
    lane = lax.axis_index("tp")
    last = spans[-1] * 2 if spans else 1
    offsets = sorted(set(spans) | {1, 1 + last})
    barrier = pltpu.get_barrier_semaphore()
    for d in offsets:
        for other in (me - d, me + d):
            @pl.when((other >= 0) & (other < count))
            def _():
                pl.semaphore_signal(barrier, inc=1, device_id=(other, lane), device_id_type=pl.DeviceIdType.MESH)
    partners = 0
    for d in offsets:
        partners = partners + (me + count - d) // count + (2 * count - 1 - me - d) // count
    pl.semaphore_wait(barrier, partners)

    def transfer(src, slot, target):
        return pltpu.make_async_remote_copy(
            src_ref=src, dst_ref=slots.at[slot], send_sem=send_sems.at[slot], recv_sem=recv_sems.at[slot],
            device_id=(target, lane), device_id_type=pl.DeviceIdType.MESH)

    def exchange(src, sends):
        for slot, d in sends:
            @pl.when(me + d < count)
            def _():
                transfer(src, slot, me + d).start()

    def settle(src, sends):
        for slot, d in sends:
            @pl.when(me + d < count)
            def _():
                transfer(src, slot, me + d).wait_send()

    current = own_ref
    for r, d in enumerate(spans):
        exchange(current, [(r, d)])
        filter_columns(r)

        @pl.when(me - d >= 0)
        def _():
            transfer(current, r, me - d).wait_recv()
            sums[r] = current[...] + fac_ref[r] * slots[r]

        @pl.when(me - d < 0)
        def _():
            sums[r] = current[...]
        settle(current, [(r, d)])
        current = sums.at[r]
    near, far = len(spans), len(spans) + 1
    final = [(near, 1), (far, 1 + last)]
    exchange(current, final)
    filter_columns(len(spans))
    out_ref[...] = jnp.zeros(out_ref.shape, out_ref.dtype)

    @pl.when(me - 1 >= 0)
    def _():
        transfer(current, near, me - 1).wait_recv()
        out_ref[...] = slots[near]

    @pl.when(me - 1 - last >= 0)
    def _():
        transfer(current, far, me - 1 - last).wait_recv()
        out_ref[...] = out_ref[...] + fac_ref[len(spans)] * slots[far]
    settle(current, final)


def body(query_proj, key_proj, value_proj, short_filter, residues, decay_rate, skip_gain, doc_lengths):
    row_count, channels = query_proj.shape
    ctx_count = lax.axis_size("ctx")
    my_index = lax.axis_index("ctx")
    first_row = my_index * row_count
    seg_rows = row_count // SEGMENTS
    local_rows = jnp.arange(row_count, dtype=jnp.int32)
    positions = first_row + local_rows
    doc_starts = jnp.cumsum(doc_lengths) - doc_lengths
    row_start = jnp.max(
        jnp.where(doc_starts[None, :] <= positions[:, None], doc_starts[None, :], 0), axis=1
    )
    since = (positions - row_start).astype(jnp.float32)
    keep = (positions != row_start).astype(jnp.float32)
    seg_first = first_row + (local_rows // seg_rows) * seg_rows
    cont = (row_start < seg_first).astype(jnp.float32)
    seg_ids = jnp.arange(SEGMENTS, dtype=jnp.int32)
    seg_lo = first_row + seg_ids * seg_rows
    in_seg = (doc_starts[None, :] >= seg_lo[:, None]) & (doc_starts[None, :] < seg_lo[:, None] + seg_rows)
    segkeep = 1.0 - jnp.any(in_seg, axis=1).astype(jnp.float32)
    before = (doc_starts[None, :] >= first_row) & (doc_starts[None, :] < seg_lo[:, None])
    opened = 1.0 - jnp.any(before, axis=1).astype(jnp.float32)

    small = jnp.zeros((row_count,), jnp.float32).at[0:SEGMENTS].set(segkeep).at[8:8 + SEGMENTS].set(opened)
    masks = jnp.broadcast_to(jnp.stack([since, keep, cont, small])[:, :, None], (4, row_count, LANES))

    stacked = jnp.stack([query_proj, key_proj, value_proj])
    rim = from_behind(stacked[:, row_count - TAPS + 1:, :], "ctx", 1)
    log_decay = jnp.log1p(-decay_rate)
    lam = jnp.exp(log_decay)
    amp = residues * jnp.sqrt(decay_rate * (2.0 - decay_rate))
    tiles = channels // LANES
    col = lambda *lead: pl.BlockSpec(tuple(lead) + (LANES,), lambda c: (0,) * len(lead) + (c,))
    fixed = lambda *shape: pl.BlockSpec(shape, lambda c: (0,) * len(shape))
    f32 = jnp.float32
    cola = lambda *lead: pl.BlockSpec(tuple(lead) + (LANES_LOCAL,), lambda c: (0,) * len(lead) + (c,))
    acc, cl, own_state = pl.pallas_call(
        local_kernel,
        grid=(channels // LANES_LOCAL,),
        in_specs=[cola(row_count), cola(row_count), cola(3, TAPS - 1), cola(3, TAPS), cola(MODES), cola(MODES),
                  cola(1), fixed(4, row_count, LANES)],
        out_specs=[cola(row_count), cola(MODES, 16), cola(MODES)],
        out_shape=[jax.ShapeDtypeStruct((row_count, channels), f32),
                   jax.ShapeDtypeStruct((MODES, 16, channels), f32), jax.ShapeDtypeStruct((MODES, channels), f32)],
        scratch_shapes=[pltpu.VMEM((row_count + 8, LANES), f32), pltpu.VMEM((row_count, LANES), f32),
                        pltpu.VMEM((row_count, LANES), f32)],
        interpret=INTERPRET,
    )(key_proj, value_proj, rim, short_filter, amp, lam, skip_gain[None, :], masks)

    def starts_between(low_device, high_device):
        low_row = jnp.maximum(low_device, 0) * row_count
        high_row = (high_device + 1) * row_count
        return jnp.any((doc_starts >= low_row) & (doc_starts < high_row)).astype(jnp.float32)

    spans = []
    span = 1
    while 2 * span < ctx_count:
        spans.append(span)
        span *= 2
    factors = []
    for d in spans:
        open_path = 1.0 - starts_between(my_index - d + 1, my_index)
        factors.append(open_path * jnp.exp(float(d * row_count) * log_decay))
    open_path = 1.0 - starts_between(my_index - span, my_index - 1)
    factors.append(open_path * jnp.exp(float(span * row_count) * log_decay))
    factors = jnp.stack(factors)
    vmem = pl.BlockSpec(memory_space=pltpu.VMEM)
    incoming, q_short = pl.pallas_call(
        functools.partial(scan_kernel, ctx_count, tuple(spans)),
        out_shape=[jax.ShapeDtypeStruct((MODES, channels), f32), jax.ShapeDtypeStruct((row_count, channels), f32)],
        in_specs=[vmem] * 6,
        out_specs=[vmem, vmem],
        scratch_shapes=[
            pltpu.VMEM((len(spans), MODES, channels), f32),
            pltpu.VMEM((len(spans) + 2, MODES, channels), f32),
            pltpu.SemaphoreType.DMA((len(spans) + 2,)),
            pltpu.SemaphoreType.DMA((len(spans) + 2,)),
            pltpu.VMEM((row_count + 8, LANES), f32),
        ],
        compiler_params=pltpu.CompilerParams(collective_id=0, has_side_effects=True),
        interpret=INTERPRET,
    )(own_state, factors, query_proj, rim, short_filter, masks)

    wide = lambda *lead: pl.BlockSpec(tuple(lead) + (LANES_FIX,), lambda c: (0,) * len(lead) + (c,))
    return pl.pallas_call(
        fix_kernel,
        grid=(channels // LANES_FIX,),
        in_specs=[wide(row_count), wide(row_count), wide(MODES, 16), wide(MODES), wide(MODES), wide(MODES),
                  fixed(4, row_count, LANES)],
        out_specs=wide(row_count),
        out_shape=jax.ShapeDtypeStruct((row_count, channels), jnp.bfloat16),
        interpret=INTERPRET,
    )(acc, q_short, cl, incoming, amp, log_decay, masks)


def solution(mesh):
    in_specs = (
        P("ctx", "tp"),
        P("ctx", "tp"),
        P("ctx", "tp"),
        P(None, None, "tp"),
        P(None, "tp"),
        P(None, "tp"),
        P("tp"),
        P(),
    )
    out_specs = P("ctx", "tp")
    return jax.shard_map(body, mesh=mesh, in_specs=in_specs, out_specs=out_specs, check_vma=False)
```

```python
import functools

import jax
import jax.numpy as jnp
from jax import lax
from jax.experimental import pallas as pl
from jax.experimental.pallas import tpu as pltpu
from jax.sharding import PartitionSpec as P

MODES = 16
TAPS = 7
LANES = 128
LANES_FIX = 1024
LANES_LOCAL = 512
SEGMENTS = 8
INTERPRET = False


def from_behind(value, axis, steps):
    count = lax.axis_size(axis)
    first, last = (max(0, -steps), min(count, count - steps))
    return lax.ppermute(value, axis, [(source, source + steps) for source in range(first, last)])


def short_conv(block, rim_rows, taps, since, ext_ref):
    rows = block.shape[0]
    ext_ref[8 - TAPS + 1:8, :] = rim_rows.astype(jnp.float32)
    ext_ref[8:8 + rows, :] = block.astype(jnp.float32)
    total = jnp.zeros((rows, LANES), jnp.float32)
    for lag in range(TAPS):
        window = ext_ref[8 - lag:8 - lag + rows, :]
        total = total + jnp.where(since >= float(lag), taps[lag:lag + 1, :] * window, 0.0)
    return total


def local_kernel(k_ref, v_ref, rim_ref, filt_ref, amp_ref, lam_ref, skip_ref, mask_ref,
                 acc_ref, cl_ref, end_ref, ext_ref, g_ref, sum_ref):
    since_ref, keep_ref = mask_ref.at[0], mask_ref.at[1]
    rows = k_ref.shape[0]
    seg_rows = rows // SEGMENTS
    since = since_ref[...]
    segkeep = mask_ref[3, 0:SEGMENTS, :]
    for c in range(k_ref.shape[1] // LANES):
        lanes = slice(c * LANES, (c + 1) * LANES)
        filtered = [short_conv(src[:, lanes], rim_ref[branch, :, lanes], filt_ref[branch, :, lanes], since, ext_ref)
                    for branch, src in ((1, k_ref), (2, v_ref))]
        g_ref[...] = (filtered[0] * filtered[1]).astype(jnp.bfloat16).astype(jnp.float32)
        lam = [jnp.broadcast_to(lam_ref[m:m + 1, lanes], (SEGMENTS, LANES)) for m in range(MODES)]
        amp = [jnp.broadcast_to(amp_ref[m:m + 1, lanes], (SEGMENTS, LANES)) for m in range(MODES)]
        skip = jnp.broadcast_to(skip_ref[:, lanes], (SEGMENTS, LANES))

        def step(j, states):
            x = g_ref[pl.ds(j, SEGMENTS, stride=seg_rows), :]
            keep = keep_ref[pl.ds(j, SEGMENTS, stride=seg_rows), :]
            new_states = [(lam[m] * keep) * states[m] + x for m in range(MODES)]
            terms = [amp[m] * new_states[m] for m in range(MODES)] + [skip * x]
            while len(terms) > 1:
                terms = [terms[i] + terms[i + 1] for i in range(0, len(terms) - 1, 2)] + terms[len(terms) - len(terms) % 2:]
            sum_ref[pl.ds(j, SEGMENTS, stride=seg_rows), :] = terms[0]
            return tuple(new_states)

        zero = jnp.zeros((SEGMENTS, LANES), jnp.float32)
        ends = lax.fori_loop(0, seg_rows, step, tuple([zero] * MODES), unroll=2)
        acc_ref[:, lanes] = sum_ref[...]
        for m in range(MODES):
            seg_decay = jnp.exp(float(seg_rows) * jnp.log(lam_ref[m:m + 1, lanes]))
            carried = jnp.zeros((1, LANES), jnp.float32)
            cl_ref[m, 0:1, lanes] = carried
            for p in range(SEGMENTS):
                carried = ends[m][p:p + 1, :] + segkeep[p:p + 1, :] * seg_decay * carried
                cl_ref[m, p + 1:p + 2, lanes] = carried
            cl_ref[m, SEGMENTS + 1:, lanes] = jnp.zeros((16 - SEGMENTS - 1, LANES), jnp.float32)
            end_ref[m:m + 1, lanes] = carried


def fix_kernel(acc_ref, qs_ref, cl_ref, hin_ref, amp_ref, logl_ref, mask_ref, out_ref):
    rows, width = acc_ref.shape
    seg_rows = rows // SEGMENTS
    copies = width // LANES
    widen = lambda part: jnp.concatenate([part] * copies, axis=1) if copies > 1 else part
    seg_index = lax.broadcasted_iota(jnp.int32, (SEGMENTS, width), 0).astype(jnp.float32)
    lag_index = lax.broadcasted_iota(jnp.int32, (seg_rows, width), 0).astype(jnp.float32) + 1.0
    opened = widen(mask_ref[3, 8:8 + SEGMENTS, :])
    starts = []
    powers = []
    for m in range(MODES):
        logl = logl_ref[m:m + 1, :]
        start = cl_ref[m, 0:SEGMENTS, :] + opened * jnp.exp(seg_index * (float(seg_rows) * logl)) * hin_ref[m:m + 1, :]
        starts.append(start)
        powers.append(amp_ref[m:m + 1, :] * jnp.exp(lag_index * logl))
    for p in range(SEGMENTS):
        lo = p * seg_rows
        corr = jnp.zeros((seg_rows, width), jnp.float32)
        for m in range(MODES):
            corr = corr + powers[m] * starts[m][p:p + 1, :]
        conv = acc_ref[lo:lo + seg_rows, :] + widen(mask_ref[2, lo:lo + seg_rows, :]) * corr
        out_ref[lo:lo + seg_rows, :] = (qs_ref[lo:lo + seg_rows, :] * conv).astype(out_ref.dtype)


def scan_kernel(count, spans, own_ref, fac_ref, q_ref, rim_ref, filt_ref, mask_ref, out_ref, qs_ref, sums, slots,
                send_sems, recv_sems, ext_ref):
    columns = q_ref.shape[1] // LANES
    groups = len(spans) + 1
    since = mask_ref[0]

    def filter_columns(group):
        for c in range(group * columns // groups, (group + 1) * columns // groups):
            lanes = slice(c * LANES, (c + 1) * LANES)
            qs_ref[:, lanes] = short_conv(q_ref[:, lanes], rim_ref[0, :, lanes], filt_ref[0, :, lanes], since, ext_ref)

    me = lax.axis_index("ctx")
    lane = lax.axis_index("tp")
    last = spans[-1] * 2 if spans else 1
    offsets = sorted(set(spans) | {1, 1 + last})
    barrier = pltpu.get_barrier_semaphore()
    for d in offsets:
        for other in (me - d, me + d):
            @pl.when((other >= 0) & (other < count))
            def _():
                pl.semaphore_signal(barrier, inc=1, device_id=(other, lane), device_id_type=pl.DeviceIdType.MESH)
    partners = 0
    for d in offsets:
        partners = partners + (me + count - d) // count + (2 * count - 1 - me - d) // count
    pl.semaphore_wait(barrier, partners)

    def transfer(src, slot, target):
        return pltpu.make_async_remote_copy(
            src_ref=src, dst_ref=slots.at[slot], send_sem=send_sems.at[slot], recv_sem=recv_sems.at[slot],
            device_id=(target, lane), device_id_type=pl.DeviceIdType.MESH)

    def exchange(src, sends):
        for slot, d in sends:
            @pl.when(me + d < count)
            def _():
                transfer(src, slot, me + d).start()

    def settle(src, sends):
        for slot, d in sends:
            @pl.when(me + d < count)
            def _():
                transfer(src, slot, me + d).wait_send()

    current = own_ref
    for r, d in enumerate(spans):
        exchange(current, [(r, d)])
        filter_columns(r)

        @pl.when(me - d >= 0)
        def _():
            transfer(current, r, me - d).wait_recv()
            sums[r] = current[...] + fac_ref[r] * slots[r]

        @pl.when(me - d < 0)
        def _():
            sums[r] = current[...]
        settle(current, [(r, d)])
        current = sums.at[r]
    near, far = len(spans), len(spans) + 1
    final = [(near, 1), (far, 1 + last)]
    exchange(current, final)
    filter_columns(len(spans))
    out_ref[...] = jnp.zeros(out_ref.shape, out_ref.dtype)

    @pl.when(me - 1 >= 0)
    def _():
        transfer(current, near, me - 1).wait_recv()
        out_ref[...] = slots[near]

    @pl.when(me - 1 - last >= 0)
    def _():
        transfer(current, far, me - 1 - last).wait_recv()
        out_ref[...] = out_ref[...] + fac_ref[len(spans)] * slots[far]
    settle(current, final)


def body(query_proj, key_proj, value_proj, short_filter, residues, decay_rate, skip_gain, doc_lengths):
    row_count, channels = query_proj.shape
    ctx_count = lax.axis_size("ctx")
    my_index = lax.axis_index("ctx")
    first_row = my_index * row_count
    seg_rows = row_count // SEGMENTS
    local_rows = jnp.arange(row_count, dtype=jnp.int32)
    positions = first_row + local_rows
    doc_starts = jnp.cumsum(doc_lengths) - doc_lengths
    row_start = jnp.max(
        jnp.where(doc_starts[None, :] <= positions[:, None], doc_starts[None, :], 0), axis=1
    )
    since = (positions - row_start).astype(jnp.float32)
    keep = (positions != row_start).astype(jnp.float32)
    seg_first = first_row + (local_rows // seg_rows) * seg_rows
    cont = (row_start < seg_first).astype(jnp.float32)
    seg_ids = jnp.arange(SEGMENTS, dtype=jnp.int32)
    seg_lo = first_row + seg_ids * seg_rows
    in_seg = (doc_starts[None, :] >= seg_lo[:, None]) & (doc_starts[None, :] < seg_lo[:, None] + seg_rows)
    segkeep = 1.0 - jnp.any(in_seg, axis=1).astype(jnp.float32)
    before = (doc_starts[None, :] >= first_row) & (doc_starts[None, :] < seg_lo[:, None])
    opened = 1.0 - jnp.any(before, axis=1).astype(jnp.float32)

    small = jnp.zeros((row_count,), jnp.float32).at[0:SEGMENTS].set(segkeep).at[8:8 + SEGMENTS].set(opened)
    masks = jnp.broadcast_to(jnp.stack([since, keep, cont, small])[:, :, None], (4, row_count, LANES))

    stacked = jnp.stack([query_proj, key_proj, value_proj])
    rim = from_behind(stacked[:, row_count - TAPS + 1:, :], "ctx", 1)
    log_decay = jnp.log1p(-decay_rate)
    lam = jnp.exp(log_decay)
    amp = residues * jnp.sqrt(decay_rate * (2.0 - decay_rate))
    tiles = channels // LANES
    col = lambda *lead: pl.BlockSpec(tuple(lead) + (LANES,), lambda c: (0,) * len(lead) + (c,))
    fixed = lambda *shape: pl.BlockSpec(shape, lambda c: (0,) * len(shape))
    f32 = jnp.float32
    cola = lambda *lead: pl.BlockSpec(tuple(lead) + (LANES_LOCAL,), lambda c: (0,) * len(lead) + (c,))
    acc, cl, own_state = pl.pallas_call(
        local_kernel,
        grid=(channels // LANES_LOCAL,),
        in_specs=[cola(row_count), cola(row_count), cola(3, TAPS - 1), cola(3, TAPS), cola(MODES), cola(MODES),
                  cola(1), fixed(4, row_count, LANES)],
        out_specs=[cola(row_count), cola(MODES, 16), cola(MODES)],
        out_shape=[jax.ShapeDtypeStruct((row_count, channels), f32),
                   jax.ShapeDtypeStruct((MODES, 16, channels), f32), jax.ShapeDtypeStruct((MODES, channels), f32)],
        scratch_shapes=[pltpu.VMEM((row_count + 8, LANES), f32), pltpu.VMEM((row_count, LANES), f32),
                        pltpu.VMEM((row_count, LANES), f32)],
        interpret=INTERPRET,
    )(key_proj, value_proj, rim, short_filter, amp, lam, skip_gain[None, :], masks)

    def starts_between(low_device, high_device):
        low_row = jnp.maximum(low_device, 0) * row_count
        high_row = (high_device + 1) * row_count
        return jnp.any((doc_starts >= low_row) & (doc_starts < high_row)).astype(jnp.float32)

    spans = []
    span = 1
    while 2 * span < ctx_count:
        spans.append(span)
        span *= 2
    factors = []
    for d in spans:
        open_path = 1.0 - starts_between(my_index - d + 1, my_index)
        factors.append(open_path * jnp.exp(float(d * row_count) * log_decay))
    open_path = 1.0 - starts_between(my_index - span, my_index - 1)
    factors.append(open_path * jnp.exp(float(span * row_count) * log_decay))
    factors = jnp.stack(factors)
    vmem = pl.BlockSpec(memory_space=pltpu.VMEM)
    incoming, q_short = pl.pallas_call(
        functools.partial(scan_kernel, ctx_count, tuple(spans)),
        out_shape=[jax.ShapeDtypeStruct((MODES, channels), f32), jax.ShapeDtypeStruct((row_count, channels), f32)],
        in_specs=[vmem] * 6,
        out_specs=[vmem, vmem],
        scratch_shapes=[
            pltpu.VMEM((len(spans), MODES, channels), f32),
            pltpu.VMEM((len(spans) + 2, MODES, channels), f32),
            pltpu.SemaphoreType.DMA((len(spans) + 2,)),
            pltpu.SemaphoreType.DMA((len(spans) + 2,)),
            pltpu.VMEM((row_count + 8, LANES), f32),
        ],
        compiler_params=pltpu.CompilerParams(collective_id=0, has_side_effects=True),
        interpret=INTERPRET,
    )(own_state, factors, query_proj, rim, short_filter, masks)

    wide = lambda *lead: pl.BlockSpec(tuple(lead) + (LANES_FIX,), lambda c: (0,) * len(lead) + (c,))
    return pl.pallas_call(
        fix_kernel,
        grid=(channels // LANES_FIX,),
        in_specs=[wide(row_count), wide(row_count), wide(MODES, 16), wide(MODES), wide(MODES), wide(MODES),
                  fixed(4, row_count, LANES)],
        out_specs=wide(row_count),
        out_shape=jax.ShapeDtypeStruct((row_count, channels), jnp.bfloat16),
        interpret=INTERPRET,
    )(acc, q_short, cl, incoming, amp, log_decay, masks)


def solution(mesh):
    in_specs = (
        P("ctx", "tp"),
        P("ctx", "tp"),
        P("ctx", "tp"),
        P(None, None, "tp"),
        P(None, "tp"),
        P(None, "tp"),
        P("tp"),
        P(),
    )
    out_specs = P("ctx", "tp")
    return jax.shard_map(body, mesh=mesh, in_specs=in_specs, out_specs=out_specs, check_vma=False)
```

```python
import functools

import jax
import jax.numpy as jnp
from jax import lax
from jax.experimental import pallas as pl
from jax.experimental.pallas import tpu as pltpu
from jax.sharding import PartitionSpec as P

MODES = 16
TAPS = 7
LANES = 128
LANES_FIX = 512
LANES_LOCAL = 1024
SEGMENTS = 8
INTERPRET = False


def from_behind(value, axis, steps):
    count = lax.axis_size(axis)
    first, last = (max(0, -steps), min(count, count - steps))
    return lax.ppermute(value, axis, [(source, source + steps) for source in range(first, last)])


def short_conv(block, rim_rows, taps, since, ext_ref):
    rows = block.shape[0]
    ext_ref[8 - TAPS + 1:8, :] = rim_rows.astype(jnp.float32)
    ext_ref[8:8 + rows, :] = block.astype(jnp.float32)
    total = jnp.zeros((rows, LANES), jnp.float32)
    for lag in range(TAPS):
        window = ext_ref[8 - lag:8 - lag + rows, :]
        total = total + jnp.where(since >= float(lag), taps[lag:lag + 1, :] * window, 0.0)
    return total


def local_kernel(k_ref, v_ref, rim_ref, filt_ref, amp_ref, lam_ref, skip_ref, mask_ref,
                 acc_ref, cl_ref, end_ref, ext_ref, g_ref, sum_ref):
    since_ref, keep_ref = mask_ref.at[0], mask_ref.at[1]
    rows = k_ref.shape[0]
    seg_rows = rows // SEGMENTS
    since = since_ref[...]
    segkeep = mask_ref[3, 0:SEGMENTS, :]
    for c in range(k_ref.shape[1] // LANES):
        lanes = slice(c * LANES, (c + 1) * LANES)
        filtered = [short_conv(src[:, lanes], rim_ref[branch, :, lanes], filt_ref[branch, :, lanes], since, ext_ref)
                    for branch, src in ((1, k_ref), (2, v_ref))]
        g_ref[...] = (filtered[0] * filtered[1]).astype(jnp.bfloat16).astype(jnp.float32)
        lam = [jnp.broadcast_to(lam_ref[m:m + 1, lanes], (SEGMENTS, LANES)) for m in range(MODES)]
        amp = [jnp.broadcast_to(amp_ref[m:m + 1, lanes], (SEGMENTS, LANES)) for m in range(MODES)]
        skip = jnp.broadcast_to(skip_ref[:, lanes], (SEGMENTS, LANES))

        def step(j, states):
            x = g_ref[pl.ds(j, SEGMENTS, stride=seg_rows), :]
            keep = keep_ref[pl.ds(j, SEGMENTS, stride=seg_rows), :]
            new_states = [(lam[m] * keep) * states[m] + x for m in range(MODES)]
            terms = [amp[m] * new_states[m] for m in range(MODES)] + [skip * x]
            while len(terms) > 1:
                terms = [terms[i] + terms[i + 1] for i in range(0, len(terms) - 1, 2)] + terms[len(terms) - len(terms) % 2:]
            sum_ref[pl.ds(j, SEGMENTS, stride=seg_rows), :] = terms[0]
            return tuple(new_states)

        zero = jnp.zeros((SEGMENTS, LANES), jnp.float32)
        ends = lax.fori_loop(0, seg_rows, step, tuple([zero] * MODES), unroll=2)
        acc_ref[:, lanes] = sum_ref[...]
        for m in range(MODES):
            seg_decay = jnp.exp(float(seg_rows) * jnp.log(lam_ref[m:m + 1, lanes]))
            carried = jnp.zeros((1, LANES), jnp.float32)
            cl_ref[m, 0:1, lanes] = carried
            for p in range(SEGMENTS):
                carried = ends[m][p:p + 1, :] + segkeep[p:p + 1, :] * seg_decay * carried
                cl_ref[m, p + 1:p + 2, lanes] = carried
            cl_ref[m, SEGMENTS + 1:, lanes] = jnp.zeros((16 - SEGMENTS - 1, LANES), jnp.float32)
            end_ref[m:m + 1, lanes] = carried


def fix_kernel(acc_ref, qs_ref, cl_ref, hin_ref, amp_ref, logl_ref, mask_ref, out_ref):
    rows, width = acc_ref.shape
    seg_rows = rows // SEGMENTS
    copies = width // LANES
    widen = lambda part: jnp.concatenate([part] * copies, axis=1) if copies > 1 else part
    seg_index = lax.broadcasted_iota(jnp.int32, (SEGMENTS, width), 0).astype(jnp.float32)
    lag_index = lax.broadcasted_iota(jnp.int32, (seg_rows, width), 0).astype(jnp.float32) + 1.0
    opened = widen(mask_ref[3, 8:8 + SEGMENTS, :])
    starts = []
    powers = []
    for m in range(MODES):
        logl = logl_ref[m:m + 1, :]
        start = cl_ref[m, 0:SEGMENTS, :] + opened * jnp.exp(seg_index * (float(seg_rows) * logl)) * hin_ref[m:m + 1, :]
        starts.append(start)
        powers.append(amp_ref[m:m + 1, :] * jnp.exp(lag_index * logl))
    for p in range(SEGMENTS):
        lo = p * seg_rows
        corr = jnp.zeros((seg_rows, width), jnp.float32)
        for m in range(MODES):
            corr = corr + powers[m] * starts[m][p:p + 1, :]
        conv = acc_ref[lo:lo + seg_rows, :] + widen(mask_ref[2, lo:lo + seg_rows, :]) * corr
        out_ref[lo:lo + seg_rows, :] = (qs_ref[lo:lo + seg_rows, :] * conv).astype(out_ref.dtype)


def scan_kernel(count, spans, own_ref, fac_ref, q_ref, rim_ref, filt_ref, mask_ref, out_ref, qs_ref, sums, slots,
                send_sems, recv_sems, ext_ref):
    columns = q_ref.shape[1] // LANES
    groups = len(spans) + 1
    since = mask_ref[0]

    def filter_columns(group):
        for c in range(group * columns // groups, (group + 1) * columns // groups):
            lanes = slice(c * LANES, (c + 1) * LANES)
            qs_ref[:, lanes] = short_conv(q_ref[:, lanes], rim_ref[0, :, lanes], filt_ref[0, :, lanes], since, ext_ref)

    me = lax.axis_index("ctx")
    lane = lax.axis_index("tp")
    last = spans[-1] * 2 if spans else 1
    offsets = sorted(set(spans) | {1, 1 + last})
    barrier = pltpu.get_barrier_semaphore()
    for d in offsets:
        for other in (me - d, me + d):
            @pl.when((other >= 0) & (other < count))
            def _():
                pl.semaphore_signal(barrier, inc=1, device_id=(other, lane), device_id_type=pl.DeviceIdType.MESH)
    partners = 0
    for d in offsets:
        partners = partners + (me + count - d) // count + (2 * count - 1 - me - d) // count
    pl.semaphore_wait(barrier, partners)

    def transfer(src, slot, target):
        return pltpu.make_async_remote_copy(
            src_ref=src, dst_ref=slots.at[slot], send_sem=send_sems.at[slot], recv_sem=recv_sems.at[slot],
            device_id=(target, lane), device_id_type=pl.DeviceIdType.MESH)

    def exchange(src, sends):
        for slot, d in sends:
            @pl.when(me + d < count)
            def _():
                transfer(src, slot, me + d).start()

    def settle(src, sends):
        for slot, d in sends:
            @pl.when(me + d < count)
            def _():
                transfer(src, slot, me + d).wait_send()

    current = own_ref
    for r, d in enumerate(spans):
        exchange(current, [(r, d)])
        filter_columns(r)

        @pl.when(me - d >= 0)
        def _():
            transfer(current, r, me - d).wait_recv()
            sums[r] = current[...] + fac_ref[r] * slots[r]

        @pl.when(me - d < 0)
        def _():
            sums[r] = current[...]
        settle(current, [(r, d)])
        current = sums.at[r]
    near, far = len(spans), len(spans) + 1
    final = [(near, 1), (far, 1 + last)]
    exchange(current, final)
    filter_columns(len(spans))
    out_ref[...] = jnp.zeros(out_ref.shape, out_ref.dtype)

    @pl.when(me - 1 >= 0)
    def _():
        transfer(current, near, me - 1).wait_recv()
        out_ref[...] = slots[near]

    @pl.when(me - 1 - last >= 0)
    def _():
        transfer(current, far, me - 1 - last).wait_recv()
        out_ref[...] = out_ref[...] + fac_ref[len(spans)] * slots[far]
    settle(current, final)


def body(query_proj, key_proj, value_proj, short_filter, residues, decay_rate, skip_gain, doc_lengths):
    row_count, channels = query_proj.shape
    ctx_count = lax.axis_size("ctx")
    my_index = lax.axis_index("ctx")
    first_row = my_index * row_count
    seg_rows = row_count // SEGMENTS
    local_rows = jnp.arange(row_count, dtype=jnp.int32)
    positions = first_row + local_rows
    doc_starts = jnp.cumsum(doc_lengths) - doc_lengths
    row_start = jnp.max(
        jnp.where(doc_starts[None, :] <= positions[:, None], doc_starts[None, :], 0), axis=1
    )
    since = (positions - row_start).astype(jnp.float32)
    keep = (positions != row_start).astype(jnp.float32)
    seg_first = first_row + (local_rows // seg_rows) * seg_rows
    cont = (row_start < seg_first).astype(jnp.float32)
    seg_ids = jnp.arange(SEGMENTS, dtype=jnp.int32)
    seg_lo = first_row + seg_ids * seg_rows
    in_seg = (doc_starts[None, :] >= seg_lo[:, None]) & (doc_starts[None, :] < seg_lo[:, None] + seg_rows)
    segkeep = 1.0 - jnp.any(in_seg, axis=1).astype(jnp.float32)
    before = (doc_starts[None, :] >= first_row) & (doc_starts[None, :] < seg_lo[:, None])
    opened = 1.0 - jnp.any(before, axis=1).astype(jnp.float32)

    small = jnp.zeros((row_count,), jnp.float32).at[0:SEGMENTS].set(segkeep).at[8:8 + SEGMENTS].set(opened)
    masks = jnp.broadcast_to(jnp.stack([since, keep, cont, small])[:, :, None], (4, row_count, LANES))

    stacked = jnp.stack([query_proj, key_proj, value_proj])
    rim = from_behind(stacked[:, row_count - TAPS + 1:, :], "ctx", 1)
    log_decay = jnp.log1p(-decay_rate)
    lam = jnp.exp(log_decay)
    amp = residues * jnp.sqrt(decay_rate * (2.0 - decay_rate))
    tiles = channels // LANES
    col = lambda *lead: pl.BlockSpec(tuple(lead) + (LANES,), lambda c: (0,) * len(lead) + (c,))
    fixed = lambda *shape: pl.BlockSpec(shape, lambda c: (0,) * len(shape))
    f32 = jnp.float32
    cola = lambda *lead: pl.BlockSpec(tuple(lead) + (LANES_LOCAL,), lambda c: (0,) * len(lead) + (c,))
    acc, cl, own_state = pl.pallas_call(
        local_kernel,
        grid=(channels // LANES_LOCAL,),
        in_specs=[cola(row_count), cola(row_count), cola(3, TAPS - 1), cola(3, TAPS), cola(MODES), cola(MODES),
                  cola(1), fixed(4, row_count, LANES)],
        out_specs=[cola(row_count), cola(MODES, 16), cola(MODES)],
        out_shape=[jax.ShapeDtypeStruct((row_count, channels), f32),
                   jax.ShapeDtypeStruct((MODES, 16, channels), f32), jax.ShapeDtypeStruct((MODES, channels), f32)],
        scratch_shapes=[pltpu.VMEM((row_count + 8, LANES), f32), pltpu.VMEM((row_count, LANES), f32),
                        pltpu.VMEM((row_count, LANES), f32)],
        interpret=INTERPRET,
    )(key_proj, value_proj, rim, short_filter, amp, lam, skip_gain[None, :], masks)

    def starts_between(low_device, high_device):
        low_row = jnp.maximum(low_device, 0) * row_count
        high_row = (high_device + 1) * row_count
        return jnp.any((doc_starts >= low_row) & (doc_starts < high_row)).astype(jnp.float32)

    spans = []
    span = 1
    while 2 * span < ctx_count:
        spans.append(span)
        span *= 2
    factors = []
    for d in spans:
        open_path = 1.0 - starts_between(my_index - d + 1, my_index)
        factors.append(open_path * jnp.exp(float(d * row_count) * log_decay))
    open_path = 1.0 - starts_between(my_index - span, my_index - 1)
    factors.append(open_path * jnp.exp(float(span * row_count) * log_decay))
    factors = jnp.stack(factors)
    vmem = pl.BlockSpec(memory_space=pltpu.VMEM)
    incoming, q_short = pl.pallas_call(
        functools.partial(scan_kernel, ctx_count, tuple(spans)),
        out_shape=[jax.ShapeDtypeStruct((MODES, channels), f32), jax.ShapeDtypeStruct((row_count, channels), f32)],
        in_specs=[vmem] * 6,
        out_specs=[vmem, vmem],
        scratch_shapes=[
            pltpu.VMEM((len(spans), MODES, channels), f32),
            pltpu.VMEM((len(spans) + 2, MODES, channels), f32),
            pltpu.SemaphoreType.DMA((len(spans) + 2,)),
            pltpu.SemaphoreType.DMA((len(spans) + 2,)),
            pltpu.VMEM((row_count + 8, LANES), f32),
        ],
        compiler_params=pltpu.CompilerParams(collective_id=0, has_side_effects=True),
        interpret=INTERPRET,
    )(own_state, factors, query_proj, rim, short_filter, masks)

    wide = lambda *lead: pl.BlockSpec(tuple(lead) + (LANES_FIX,), lambda c: (0,) * len(lead) + (c,))
    return pl.pallas_call(
        fix_kernel,
        grid=(channels // LANES_FIX,),
        in_specs=[wide(row_count), wide(row_count), wide(MODES, 16), wide(MODES), wide(MODES), wide(MODES),
                  fixed(4, row_count, LANES)],
        out_specs=wide(row_count),
        out_shape=jax.ShapeDtypeStruct((row_count, channels), jnp.bfloat16),
        interpret=INTERPRET,
    )(acc, q_short, cl, incoming, amp, log_decay, masks)


def solution(mesh):
    in_specs = (
        P("ctx", "tp"),
        P("ctx", "tp"),
        P("ctx", "tp"),
        P(None, None, "tp"),
        P(None, "tp"),
        P(None, "tp"),
        P("tp"),
        P(),
    )
    out_specs = P("ctx", "tp")
    return jax.shard_map(body, mesh=mesh, in_specs=in_specs, out_specs=out_specs, check_vma=False)
```

```python
import functools

import jax
import jax.numpy as jnp
from jax import lax
from jax.experimental import pallas as pl
from jax.experimental.pallas import tpu as pltpu
from jax.sharding import PartitionSpec as P

MODES = 16
TAPS = 7
LANES = 128
LANES_FIX = 512
LANES_LOCAL = 512
SEGMENTS = 8
INTERPRET = False


def from_behind(value, axis, steps):
    count = lax.axis_size(axis)
    first, last = (max(0, -steps), min(count, count - steps))
    return lax.ppermute(value, axis, [(source, source + steps) for source in range(first, last)])


def short_conv(block, rim_rows, taps, since, ext_ref):
    rows = block.shape[0]
    ext_ref[8 - TAPS + 1:8, :] = rim_rows.astype(jnp.float32)
    ext_ref[8:8 + rows, :] = block.astype(jnp.float32)
    total = jnp.zeros((rows, LANES), jnp.float32)
    for lag in range(TAPS):
        window = ext_ref[8 - lag:8 - lag + rows, :]
        total = total + jnp.where(since >= float(lag), taps[lag:lag + 1, :] * window, 0.0)
    return total


def local_kernel(k_ref, v_ref, rim_ref, filt_ref, amp_ref, lam_ref, skip_ref, mask_ref,
                 acc_ref, cl_ref, end_ref, ext_ref, g_ref, sum_ref):
    since_ref, keep_ref = mask_ref.at[0], mask_ref.at[1]
    rows = k_ref.shape[0]
    seg_rows = rows // SEGMENTS
    since = since_ref[...]
    segkeep = mask_ref[3, 0:SEGMENTS, :]
    for c in range(k_ref.shape[1] // LANES):
        lanes = slice(c * LANES, (c + 1) * LANES)
        filtered = [short_conv(src[:, lanes], rim_ref[branch, :, lanes], filt_ref[branch, :, lanes], since, ext_ref)
                    for branch, src in ((1, k_ref), (2, v_ref))]
        g_ref[...] = (filtered[0] * filtered[1]).astype(jnp.bfloat16).astype(jnp.float32)
        lam = [jnp.broadcast_to(lam_ref[m:m + 1, lanes], (SEGMENTS, LANES)) for m in range(MODES)]
        amp = [jnp.broadcast_to(amp_ref[m:m + 1, lanes], (SEGMENTS, LANES)) for m in range(MODES)]
        skip = jnp.broadcast_to(skip_ref[:, lanes], (SEGMENTS, LANES))

        def step(j, states):
            x = g_ref[pl.ds(j, SEGMENTS, stride=seg_rows), :]
            keep = keep_ref[pl.ds(j, SEGMENTS, stride=seg_rows), :]
            new_states = [(lam[m] * keep) * states[m] + x for m in range(MODES)]
            terms = [amp[m] * new_states[m] for m in range(MODES)] + [skip * x]
            while len(terms) > 1:
                terms = [terms[i] + terms[i + 1] for i in range(0, len(terms) - 1, 2)] + terms[len(terms) - len(terms) % 2:]
            sum_ref[pl.ds(j, SEGMENTS, stride=seg_rows), :] = terms[0]
            return tuple(new_states)

        zero = jnp.zeros((SEGMENTS, LANES), jnp.float32)
        ends = lax.fori_loop(0, seg_rows, step, tuple([zero] * MODES), unroll=2)
        acc_ref[:, lanes] = sum_ref[...]
        for m in range(MODES):
            seg_decay = jnp.exp(float(seg_rows) * jnp.log(lam_ref[m:m + 1, lanes]))
            carried = jnp.zeros((1, LANES), jnp.float32)
            cl_ref[m, 0:1, lanes] = carried
            for p in range(SEGMENTS):
                carried = ends[m][p:p + 1, :] + segkeep[p:p + 1, :] * seg_decay * carried
                cl_ref[m, p + 1:p + 2, lanes] = carried
            cl_ref[m, SEGMENTS + 1:, lanes] = jnp.zeros((16 - SEGMENTS - 1, LANES), jnp.float32)
            end_ref[m:m + 1, lanes] = carried


def fix_kernel(acc_ref, qs_ref, cl_ref, hin_ref, amp_ref, logl_ref, mask_ref, out_ref):
    rows, width = acc_ref.shape
    seg_rows = rows // SEGMENTS
    copies = width // LANES
    widen = lambda part: jnp.concatenate([part] * copies, axis=1) if copies > 1 else part
    seg_index = lax.broadcasted_iota(jnp.int32, (SEGMENTS, width), 0).astype(jnp.float32)
    lag_index = lax.broadcasted_iota(jnp.int32, (seg_rows, width), 0).astype(jnp.float32) + 1.0
    opened = widen(mask_ref[3, 8:8 + SEGMENTS, :])
    starts = []
    powers = []
    for m in range(MODES):
        logl = logl_ref[m:m + 1, :]
        start = cl_ref[m, 0:SEGMENTS, :] + opened * jnp.exp(seg_index * (float(seg_rows) * logl)) * hin_ref[m:m + 1, :]
        starts.append(start)
        powers.append(amp_ref[m:m + 1, :] * jnp.exp(lag_index * logl))
    for p in range(SEGMENTS):
        lo = p * seg_rows
        corr = jnp.zeros((seg_rows, width), jnp.float32)
        for m in range(MODES):
            corr = corr + powers[m] * starts[m][p:p + 1, :]
        conv = acc_ref[lo:lo + seg_rows, :] + widen(mask_ref[2, lo:lo + seg_rows, :]) * corr
        out_ref[lo:lo + seg_rows, :] = (qs_ref[lo:lo + seg_rows, :] * conv).astype(out_ref.dtype)


def scan_kernel(count, spans, own_ref, fac_ref, q_ref, rim_ref, filt_ref, mask_ref, out_ref, qs_ref, sums, slots,
                send_sems, recv_sems, ext_ref):
    columns = q_ref.shape[1] // LANES
    groups = len(spans) + 1
    since = mask_ref[0]

    def filter_columns(group):
        for c in range(group * columns // groups, (group + 1) * columns // groups):
            lanes = slice(c * LANES, (c + 1) * LANES)
            qs_ref[:, lanes] = short_conv(q_ref[:, lanes], rim_ref[0, :, lanes], filt_ref[0, :, lanes], since, ext_ref)

    me = lax.axis_index("ctx")
    lane = lax.axis_index("tp")
    last = spans[-1] * 2 if spans else 1
    offsets = sorted(set(spans) | {1, 1 + last})
    barrier = pltpu.get_barrier_semaphore()
    for d in offsets:
        for other in (me - d, me + d):
            @pl.when((other >= 0) & (other < count))
            def _():
                pl.semaphore_signal(barrier, inc=1, device_id=(other, lane), device_id_type=pl.DeviceIdType.MESH)
    partners = 0
    for d in offsets:
        partners = partners + (me + count - d) // count + (2 * count - 1 - me - d) // count
    pl.semaphore_wait(barrier, partners)

    half = slots.shape[2] // 2

    class transfer:
        def __init__(self, src, slot, target):
            self.parts = [pltpu.make_async_remote_copy(
                src_ref=src.at[:, pl.ds(h * half, half)], dst_ref=slots.at[slot, :, pl.ds(h * half, half)],
                send_sem=send_sems.at[2 * slot + h], recv_sem=recv_sems.at[2 * slot + h],
                device_id=(target, lane), device_id_type=pl.DeviceIdType.MESH) for h in range(2)]

        def start(self):
            for part in self.parts:
                part.start()

        def wait_send(self):
            for part in self.parts:
                part.wait_send()

        def wait_recv(self):
            for part in self.parts:
                part.wait_recv()

    def exchange(src, sends):
        for slot, d in sends:
            @pl.when(me + d < count)
            def _():
                transfer(src, slot, me + d).start()

    def settle(src, sends):
        for slot, d in sends:
            @pl.when(me + d < count)
            def _():
                transfer(src, slot, me + d).wait_send()

    current = own_ref
    for r, d in enumerate(spans):
        exchange(current, [(r, d)])
        filter_columns(r)

        @pl.when(me - d >= 0)
        def _():
            transfer(current, r, me - d).wait_recv()
            sums[r] = current[...] + fac_ref[r] * slots[r]

        @pl.when(me - d < 0)
        def _():
            sums[r] = current[...]
        settle(current, [(r, d)])
        current = sums.at[r]
    near, far = len(spans), len(spans) + 1
    final = [(near, 1), (far, 1 + last)]
    exchange(current, final)
    filter_columns(len(spans))
    out_ref[...] = jnp.zeros(out_ref.shape, out_ref.dtype)

    @pl.when(me - 1 >= 0)
    def _():
        transfer(current, near, me - 1).wait_recv()
        out_ref[...] = slots[near]

    @pl.when(me - 1 - last >= 0)
    def _():
        transfer(current, far, me - 1 - last).wait_recv()
        out_ref[...] = out_ref[...] + fac_ref[len(spans)] * slots[far]
    settle(current, final)


def body(query_proj, key_proj, value_proj, short_filter, residues, decay_rate, skip_gain, doc_lengths):
    row_count, channels = query_proj.shape
    ctx_count = lax.axis_size("ctx")
    my_index = lax.axis_index("ctx")
    first_row = my_index * row_count
    seg_rows = row_count // SEGMENTS
    local_rows = jnp.arange(row_count, dtype=jnp.int32)
    positions = first_row + local_rows
    doc_starts = jnp.cumsum(doc_lengths) - doc_lengths
    row_start = jnp.max(
        jnp.where(doc_starts[None, :] <= positions[:, None], doc_starts[None, :], 0), axis=1
    )
    since = (positions - row_start).astype(jnp.float32)
    keep = (positions != row_start).astype(jnp.float32)
    seg_first = first_row + (local_rows // seg_rows) * seg_rows
    cont = (row_start < seg_first).astype(jnp.float32)
    seg_ids = jnp.arange(SEGMENTS, dtype=jnp.int32)
    seg_lo = first_row + seg_ids * seg_rows
    in_seg = (doc_starts[None, :] >= seg_lo[:, None]) & (doc_starts[None, :] < seg_lo[:, None] + seg_rows)
    segkeep = 1.0 - jnp.any(in_seg, axis=1).astype(jnp.float32)
    before = (doc_starts[None, :] >= first_row) & (doc_starts[None, :] < seg_lo[:, None])
    opened = 1.0 - jnp.any(before, axis=1).astype(jnp.float32)

    small = jnp.zeros((row_count,), jnp.float32).at[0:SEGMENTS].set(segkeep).at[8:8 + SEGMENTS].set(opened)
    masks = jnp.broadcast_to(jnp.stack([since, keep, cont, small])[:, :, None], (4, row_count, LANES))

    stacked = jnp.stack([query_proj, key_proj, value_proj])
    rim = from_behind(stacked[:, row_count - TAPS + 1:, :], "ctx", 1)
    log_decay = jnp.log1p(-decay_rate)
    lam = jnp.exp(log_decay)
    amp = residues * jnp.sqrt(decay_rate * (2.0 - decay_rate))
    tiles = channels // LANES
    col = lambda *lead: pl.BlockSpec(tuple(lead) + (LANES,), lambda c: (0,) * len(lead) + (c,))
    fixed = lambda *shape: pl.BlockSpec(shape, lambda c: (0,) * len(shape))
    f32 = jnp.float32
    cola = lambda *lead: pl.BlockSpec(tuple(lead) + (LANES_LOCAL,), lambda c: (0,) * len(lead) + (c,))
    acc, cl, own_state = pl.pallas_call(
        local_kernel,
        grid=(channels // LANES_LOCAL,),
        in_specs=[cola(row_count), cola(row_count), cola(3, TAPS - 1), cola(3, TAPS), cola(MODES), cola(MODES),
                  cola(1), fixed(4, row_count, LANES)],
        out_specs=[cola(row_count), cola(MODES, 16), cola(MODES)],
        out_shape=[jax.ShapeDtypeStruct((row_count, channels), f32),
                   jax.ShapeDtypeStruct((MODES, 16, channels), f32), jax.ShapeDtypeStruct((MODES, channels), f32)],
        scratch_shapes=[pltpu.VMEM((row_count + 8, LANES), f32), pltpu.VMEM((row_count, LANES), f32),
                        pltpu.VMEM((row_count, LANES), f32)],
        interpret=INTERPRET,
    )(key_proj, value_proj, rim, short_filter, amp, lam, skip_gain[None, :], masks)

    def starts_between(low_device, high_device):
        low_row = jnp.maximum(low_device, 0) * row_count
        high_row = (high_device + 1) * row_count
        return jnp.any((doc_starts >= low_row) & (doc_starts < high_row)).astype(jnp.float32)

    spans = []
    span = 1
    while 2 * span < ctx_count:
        spans.append(span)
        span *= 2
    factors = []
    for d in spans:
        open_path = 1.0 - starts_between(my_index - d + 1, my_index)
        factors.append(open_path * jnp.exp(float(d * row_count) * log_decay))
    open_path = 1.0 - starts_between(my_index - span, my_index - 1)
    factors.append(open_path * jnp.exp(float(span * row_count) * log_decay))
    factors = jnp.stack(factors)
    vmem = pl.BlockSpec(memory_space=pltpu.VMEM)
    incoming, q_short = pl.pallas_call(
        functools.partial(scan_kernel, ctx_count, tuple(spans)),
        out_shape=[jax.ShapeDtypeStruct((MODES, channels), f32), jax.ShapeDtypeStruct((row_count, channels), f32)],
        in_specs=[vmem] * 6,
        out_specs=[vmem, vmem],
        scratch_shapes=[
            pltpu.VMEM((len(spans), MODES, channels), f32),
            pltpu.VMEM((len(spans) + 2, MODES, channels), f32),
            pltpu.SemaphoreType.DMA((2 * len(spans) + 4,)),
            pltpu.SemaphoreType.DMA((2 * len(spans) + 4,)),
            pltpu.VMEM((row_count + 8, LANES), f32),
        ],
        compiler_params=pltpu.CompilerParams(collective_id=0, has_side_effects=True),
        interpret=INTERPRET,
    )(own_state, factors, query_proj, rim, short_filter, masks)

    wide = lambda *lead: pl.BlockSpec(tuple(lead) + (LANES_FIX,), lambda c: (0,) * len(lead) + (c,))
    return pl.pallas_call(
        fix_kernel,
        grid=(channels // LANES_FIX,),
        in_specs=[wide(row_count), wide(row_count), wide(MODES, 16), wide(MODES), wide(MODES), wide(MODES),
                  fixed(4, row_count, LANES)],
        out_specs=wide(row_count),
        out_shape=jax.ShapeDtypeStruct((row_count, channels), jnp.bfloat16),
        interpret=INTERPRET,
    )(acc, q_short, cl, incoming, amp, log_decay, masks)


def solution(mesh):
    in_specs = (
        P("ctx", "tp"),
        P("ctx", "tp"),
        P("ctx", "tp"),
        P(None, None, "tp"),
        P(None, "tp"),
        P(None, "tp"),
        P("tp"),
        P(),
    )
    out_specs = P("ctx", "tp")
    return jax.shard_map(body, mesh=mesh, in_specs=in_specs, out_specs=out_specs, check_vma=False)
```

```python
import functools

import jax
import jax.numpy as jnp
from jax import lax
from jax.experimental import pallas as pl
from jax.experimental.pallas import tpu as pltpu
from jax.sharding import PartitionSpec as P

MODES = 16
TAPS = 7
LANES = 128
LANES_FIX = 512
LANES_LOCAL = 512
SEGMENTS = 8
INTERPRET = False


def from_behind(value, axis, steps):
    count = lax.axis_size(axis)
    first, last = (max(0, -steps), min(count, count - steps))
    return lax.ppermute(value, axis, [(source, source + steps) for source in range(first, last)])


def short_conv(block, rim_rows, taps, since, ext_ref):
    rows = block.shape[0]
    ext_ref[8 - TAPS + 1:8, :] = rim_rows.astype(jnp.float32)
    ext_ref[8:8 + rows, :] = block.astype(jnp.float32)
    total = jnp.zeros((rows, LANES), jnp.float32)
    for lag in range(TAPS):
        window = ext_ref[8 - lag:8 - lag + rows, :]
        total = total + jnp.where(since >= float(lag), taps[lag:lag + 1, :] * window, 0.0)
    return total


def local_kernel(k_ref, v_ref, rim_ref, filt_ref, amp_ref, lam_ref, skip_ref, mask_ref,
                 acc_ref, cl_ref, end_ref, ext_ref, g_ref, sum_ref):
    since_ref, keep_ref = mask_ref.at[0], mask_ref.at[1]
    rows = k_ref.shape[0]
    seg_rows = rows // SEGMENTS
    since = since_ref[...]
    segkeep = mask_ref[3, 0:SEGMENTS, :]
    for c in range(k_ref.shape[1] // LANES):
        lanes = slice(c * LANES, (c + 1) * LANES)
        filtered = [short_conv(src[:, lanes], rim_ref[branch, :, lanes], filt_ref[branch, :, lanes], since, ext_ref)
                    for branch, src in ((1, k_ref), (2, v_ref))]
        g_ref[...] = (filtered[0] * filtered[1]).astype(jnp.bfloat16).astype(jnp.float32)
        lam = [jnp.broadcast_to(lam_ref[m:m + 1, lanes], (SEGMENTS, LANES)) for m in range(MODES)]
        amp = [jnp.broadcast_to(amp_ref[m:m + 1, lanes], (SEGMENTS, LANES)) for m in range(MODES)]
        skip = jnp.broadcast_to(skip_ref[:, lanes], (SEGMENTS, LANES))

        def step(j, states):
            x = g_ref[pl.ds(j, SEGMENTS, stride=seg_rows), :]
            keep = keep_ref[pl.ds(j, SEGMENTS, stride=seg_rows), :]
            new_states = [(lam[m] * keep) * states[m] + x for m in range(MODES)]
            terms = [amp[m] * new_states[m] for m in range(MODES)] + [skip * x]
            while len(terms) > 1:
                terms = [terms[i] + terms[i + 1] for i in range(0, len(terms) - 1, 2)] + terms[len(terms) - len(terms) % 2:]
            sum_ref[pl.ds(j, SEGMENTS, stride=seg_rows), :] = terms[0]
            return tuple(new_states)

        zero = jnp.zeros((SEGMENTS, LANES), jnp.float32)
        ends = lax.fori_loop(0, seg_rows, step, tuple([zero] * MODES), unroll=4)
        acc_ref[:, lanes] = sum_ref[...]
        for m in range(MODES):
            seg_decay = jnp.exp(float(seg_rows) * jnp.log(lam_ref[m:m + 1, lanes]))
            carried = jnp.zeros((1, LANES), jnp.float32)
            cl_ref[m, 0:1, lanes] = carried
            for p in range(SEGMENTS):
                carried = ends[m][p:p + 1, :] + segkeep[p:p + 1, :] * seg_decay * carried
                cl_ref[m, p + 1:p + 2, lanes] = carried
            cl_ref[m, SEGMENTS + 1:, lanes] = jnp.zeros((16 - SEGMENTS - 1, LANES), jnp.float32)
            end_ref[m:m + 1, lanes] = carried


def fix_kernel(acc_ref, qs_ref, cl_ref, hin_ref, amp_ref, logl_ref, mask_ref, out_ref):
    rows, width = acc_ref.shape
    seg_rows = rows // SEGMENTS
    copies = width // LANES
    widen = lambda part: jnp.concatenate([part] * copies, axis=1) if copies > 1 else part
    seg_index = lax.broadcasted_iota(jnp.int32, (SEGMENTS, width), 0).astype(jnp.float32)
    lag_index = lax.broadcasted_iota(jnp.int32, (seg_rows, width), 0).astype(jnp.float32) + 1.0
    opened = widen(mask_ref[3, 8:8 + SEGMENTS, :])
    starts = []
    powers = []
    for m in range(MODES):
        logl = logl_ref[m:m + 1, :]
        start = cl_ref[m, 0:SEGMENTS, :] + opened * jnp.exp(seg_index * (float(seg_rows) * logl)) * hin_ref[m:m + 1, :]
        starts.append(start)
        powers.append(amp_ref[m:m + 1, :] * jnp.exp(lag_index * logl))
    for p in range(SEGMENTS):
        lo = p * seg_rows
        corr = jnp.zeros((seg_rows, width), jnp.float32)
        for m in range(MODES):
            corr = corr + powers[m] * starts[m][p:p + 1, :]
        conv = acc_ref[lo:lo + seg_rows, :] + widen(mask_ref[2, lo:lo + seg_rows, :]) * corr
        out_ref[lo:lo + seg_rows, :] = (qs_ref[lo:lo + seg_rows, :] * conv).astype(out_ref.dtype)


def scan_kernel(count, spans, own_ref, fac_ref, q_ref, rim_ref, filt_ref, mask_ref, out_ref, qs_ref, sums, slots,
                send_sems, recv_sems, ext_ref):
    columns = q_ref.shape[1] // LANES
    groups = len(spans) + 1
    since = mask_ref[0]

    def filter_columns(group):
        for c in range(group * columns // groups, (group + 1) * columns // groups):
            lanes = slice(c * LANES, (c + 1) * LANES)
            qs_ref[:, lanes] = short_conv(q_ref[:, lanes], rim_ref[0, :, lanes], filt_ref[0, :, lanes], since, ext_ref)

    me = lax.axis_index("ctx")
    lane = lax.axis_index("tp")
    last = spans[-1] * 2 if spans else 1
    offsets = sorted(set(spans) | {1, 1 + last})
    barrier = pltpu.get_barrier_semaphore()
    for d in offsets:
        for other in (me - d, me + d):
            @pl.when((other >= 0) & (other < count))
            def _():
                pl.semaphore_signal(barrier, inc=1, device_id=(other, lane), device_id_type=pl.DeviceIdType.MESH)
    partners = 0
    for d in offsets:
        partners = partners + (me + count - d) // count + (2 * count - 1 - me - d) // count
    pl.semaphore_wait(barrier, partners)

    def transfer(src, slot, target):
        return pltpu.make_async_remote_copy(
            src_ref=src, dst_ref=slots.at[slot], send_sem=send_sems.at[slot], recv_sem=recv_sems.at[slot],
            device_id=(target, lane), device_id_type=pl.DeviceIdType.MESH)

    def exchange(src, sends):
        for slot, d in sends:
            @pl.when(me + d < count)
            def _():
                transfer(src, slot, me + d).start()

    def settle(src, sends):
        for slot, d in sends:
            @pl.when(me + d < count)
            def _():
                transfer(src, slot, me + d).wait_send()

    current = own_ref
    for r, d in enumerate(spans):
        exchange(current, [(r, d)])
        filter_columns(r)

        @pl.when(me - d >= 0)
        def _():
            transfer(current, r, me - d).wait_recv()
            sums[r] = current[...] + fac_ref[r] * slots[r]

        @pl.when(me - d < 0)
        def _():
            sums[r] = current[...]
        settle(current, [(r, d)])
        current = sums.at[r]
    near, far = len(spans), len(spans) + 1
    final = [(near, 1), (far, 1 + last)]
    exchange(current, final)
    filter_columns(len(spans))
    out_ref[...] = jnp.zeros(out_ref.shape, out_ref.dtype)

    @pl.when(me - 1 >= 0)
    def _():
        transfer(current, near, me - 1).wait_recv()
        out_ref[...] = slots[near]

    @pl.when(me - 1 - last >= 0)
    def _():
        transfer(current, far, me - 1 - last).wait_recv()
        out_ref[...] = out_ref[...] + fac_ref[len(spans)] * slots[far]
    settle(current, final)


def body(query_proj, key_proj, value_proj, short_filter, residues, decay_rate, skip_gain, doc_lengths):
    row_count, channels = query_proj.shape
    ctx_count = lax.axis_size("ctx")
    my_index = lax.axis_index("ctx")
    first_row = my_index * row_count
    seg_rows = row_count // SEGMENTS
    local_rows = jnp.arange(row_count, dtype=jnp.int32)
    positions = first_row + local_rows
    doc_starts = jnp.cumsum(doc_lengths) - doc_lengths
    row_start = jnp.max(
        jnp.where(doc_starts[None, :] <= positions[:, None], doc_starts[None, :], 0), axis=1
    )
    since = (positions - row_start).astype(jnp.float32)
    keep = (positions != row_start).astype(jnp.float32)
    seg_first = first_row + (local_rows // seg_rows) * seg_rows
    cont = (row_start < seg_first).astype(jnp.float32)
    seg_ids = jnp.arange(SEGMENTS, dtype=jnp.int32)
    seg_lo = first_row + seg_ids * seg_rows
    in_seg = (doc_starts[None, :] >= seg_lo[:, None]) & (doc_starts[None, :] < seg_lo[:, None] + seg_rows)
    segkeep = 1.0 - jnp.any(in_seg, axis=1).astype(jnp.float32)
    before = (doc_starts[None, :] >= first_row) & (doc_starts[None, :] < seg_lo[:, None])
    opened = 1.0 - jnp.any(before, axis=1).astype(jnp.float32)

    small = jnp.zeros((row_count,), jnp.float32).at[0:SEGMENTS].set(segkeep).at[8:8 + SEGMENTS].set(opened)
    masks = jnp.broadcast_to(jnp.stack([since, keep, cont, small])[:, :, None], (4, row_count, LANES))

    stacked = jnp.stack([query_proj, key_proj, value_proj])
    rim = from_behind(stacked[:, row_count - TAPS + 1:, :], "ctx", 1)
    log_decay = jnp.log1p(-decay_rate)
    lam = jnp.exp(log_decay)
    amp = residues * jnp.sqrt(decay_rate * (2.0 - decay_rate))
    tiles = channels // LANES
    col = lambda *lead: pl.BlockSpec(tuple(lead) + (LANES,), lambda c: (0,) * len(lead) + (c,))
    fixed = lambda *shape: pl.BlockSpec(shape, lambda c: (0,) * len(shape))
    f32 = jnp.float32
    cola = lambda *lead: pl.BlockSpec(tuple(lead) + (LANES_LOCAL,), lambda c: (0,) * len(lead) + (c,))
    acc, cl, own_state = pl.pallas_call(
        local_kernel,
        grid=(channels // LANES_LOCAL,),
        in_specs=[cola(row_count), cola(row_count), cola(3, TAPS - 1), cola(3, TAPS), cola(MODES), cola(MODES),
                  cola(1), fixed(4, row_count, LANES)],
        out_specs=[cola(row_count), cola(MODES, 16), cola(MODES)],
        out_shape=[jax.ShapeDtypeStruct((row_count, channels), f32),
                   jax.ShapeDtypeStruct((MODES, 16, channels), f32), jax.ShapeDtypeStruct((MODES, channels), f32)],
        scratch_shapes=[pltpu.VMEM((row_count + 8, LANES), f32), pltpu.VMEM((row_count, LANES), f32),
                        pltpu.VMEM((row_count, LANES), f32)],
        interpret=INTERPRET,
    )(key_proj, value_proj, rim, short_filter, amp, lam, skip_gain[None, :], masks)

    def starts_between(low_device, high_device):
        low_row = jnp.maximum(low_device, 0) * row_count
        high_row = (high_device + 1) * row_count
        return jnp.any((doc_starts >= low_row) & (doc_starts < high_row)).astype(jnp.float32)

    spans = []
    span = 1
    while 2 * span < ctx_count:
        spans.append(span)
        span *= 2
    factors = []
    for d in spans:
        open_path = 1.0 - starts_between(my_index - d + 1, my_index)
        factors.append(open_path * jnp.exp(float(d * row_count) * log_decay))
    open_path = 1.0 - starts_between(my_index - span, my_index - 1)
    factors.append(open_path * jnp.exp(float(span * row_count) * log_decay))
    factors = jnp.stack(factors)
    vmem = pl.BlockSpec(memory_space=pltpu.VMEM)
    incoming, q_short = pl.pallas_call(
        functools.partial(scan_kernel, ctx_count, tuple(spans)),
        out_shape=[jax.ShapeDtypeStruct((MODES, channels), f32), jax.ShapeDtypeStruct((row_count, channels), f32)],
        in_specs=[vmem] * 6,
        out_specs=[vmem, vmem],
        scratch_shapes=[
            pltpu.VMEM((len(spans), MODES, channels), f32),
            pltpu.VMEM((len(spans) + 2, MODES, channels), f32),
            pltpu.SemaphoreType.DMA((len(spans) + 2,)),
            pltpu.SemaphoreType.DMA((len(spans) + 2,)),
            pltpu.VMEM((row_count + 8, LANES), f32),
        ],
        compiler_params=pltpu.CompilerParams(collective_id=0, has_side_effects=True),
        interpret=INTERPRET,
    )(own_state, factors, query_proj, rim, short_filter, masks)

    wide = lambda *lead: pl.BlockSpec(tuple(lead) + (LANES_FIX,), lambda c: (0,) * len(lead) + (c,))
    return pl.pallas_call(
        fix_kernel,
        grid=(channels // LANES_FIX,),
        in_specs=[wide(row_count), wide(row_count), wide(MODES, 16), wide(MODES), wide(MODES), wide(MODES),
                  fixed(4, row_count, LANES)],
        out_specs=wide(row_count),
        out_shape=jax.ShapeDtypeStruct((row_count, channels), jnp.bfloat16),
        interpret=INTERPRET,
    )(acc, q_short, cl, incoming, amp, log_decay, masks)


def solution(mesh):
    in_specs = (
        P("ctx", "tp"),
        P("ctx", "tp"),
        P("ctx", "tp"),
        P(None, None, "tp"),
        P(None, "tp"),
        P(None, "tp"),
        P("tp"),
        P(),
    )
    out_specs = P("ctx", "tp")
    return jax.shard_map(body, mesh=mesh, in_specs=in_specs, out_specs=out_specs, check_vma=False)
```

```python
import functools

import jax
import jax.numpy as jnp
from jax import lax
from jax.experimental import pallas as pl
from jax.experimental.pallas import tpu as pltpu
from jax.sharding import PartitionSpec as P

MODES = 16
TAPS = 7
LANES = 128
LANES_FIX = 512
LANES_LOCAL = 512
SEGMENTS = 8
INTERPRET = False


def from_behind(value, axis, steps):
    count = lax.axis_size(axis)
    first, last = (max(0, -steps), min(count, count - steps))
    return lax.ppermute(value, axis, [(source, source + steps) for source in range(first, last)])


def short_conv(block, rim_rows, taps, since, ext_ref):
    rows = block.shape[0]
    ext_ref[8 - TAPS + 1:8, :] = rim_rows.astype(jnp.float32)
    ext_ref[8:8 + rows, :] = block.astype(jnp.float32)
    total = jnp.zeros((rows, LANES), jnp.float32)
    for lag in range(TAPS):
        window = ext_ref[8 - lag:8 - lag + rows, :]
        total = total + jnp.where(since >= float(lag), taps[lag:lag + 1, :] * window, 0.0)
    return total


def local_kernel(k_ref, v_ref, rim_ref, filt_ref, amp_ref, lam_ref, skip_ref, mask_ref,
                 acc_ref, cl_ref, end_ref, ext_ref, g_ref, sum_ref):
    since_ref, keep_ref = mask_ref.at[0], mask_ref.at[1]
    rows = k_ref.shape[0]
    seg_rows = rows // SEGMENTS
    since = since_ref[...]
    segkeep = mask_ref[3, 0:SEGMENTS, :]
    for c in range(k_ref.shape[1] // LANES):
        lanes = slice(c * LANES, (c + 1) * LANES)
        filtered = [short_conv(src[:, lanes], rim_ref[branch, :, lanes], filt_ref[branch, :, lanes], since, ext_ref)
                    for branch, src in ((1, k_ref), (2, v_ref))]
        g_ref[...] = (filtered[0] * filtered[1]).astype(jnp.bfloat16).astype(jnp.float32)
        lam = [jnp.broadcast_to(lam_ref[m:m + 1, lanes], (SEGMENTS, LANES)) for m in range(MODES)]
        amp = [jnp.broadcast_to(amp_ref[m:m + 1, lanes], (SEGMENTS, LANES)) for m in range(MODES)]
        skip = jnp.broadcast_to(skip_ref[:, lanes], (SEGMENTS, LANES))

        def step(j, states):
            x = g_ref[pl.ds(j, SEGMENTS, stride=seg_rows), :]
            keep = keep_ref[pl.ds(j, SEGMENTS, stride=seg_rows), :]
            new_states = [(lam[m] * keep) * states[m] + x for m in range(MODES)]
            terms = [amp[m] * new_states[m] for m in range(MODES)] + [skip * x]
            while len(terms) > 1:
                terms = [terms[i] + terms[i + 1] for i in range(0, len(terms) - 1, 2)] + terms[len(terms) - len(terms) % 2:]
            sum_ref[pl.ds(j, SEGMENTS, stride=seg_rows), :] = terms[0]
            return tuple(new_states)

        zero = jnp.zeros((SEGMENTS, LANES), jnp.float32)
        ends = lax.fori_loop(0, seg_rows, step, tuple([zero] * MODES), unroll=8)
        acc_ref[:, lanes] = sum_ref[...]
        for m in range(MODES):
            seg_decay = jnp.exp(float(seg_rows) * jnp.log(lam_ref[m:m + 1, lanes]))
            carried = jnp.zeros((1, LANES), jnp.float32)
            cl_ref[m, 0:1, lanes] = carried
            for p in range(SEGMENTS):
                carried = ends[m][p:p + 1, :] + segkeep[p:p + 1, :] * seg_decay * carried
                cl_ref[m, p + 1:p + 2, lanes] = carried
            cl_ref[m, SEGMENTS + 1:, lanes] = jnp.zeros((16 - SEGMENTS - 1, LANES), jnp.float32)
            end_ref[m:m + 1, lanes] = carried


def fix_kernel(acc_ref, qs_ref, cl_ref, hin_ref, amp_ref, logl_ref, mask_ref, out_ref):
    rows, width = acc_ref.shape
    seg_rows = rows // SEGMENTS
    copies = width // LANES
    widen = lambda part: jnp.concatenate([part] * copies, axis=1) if copies > 1 else part
    seg_index = lax.broadcasted_iota(jnp.int32, (SEGMENTS, width), 0).astype(jnp.float32)
    lag_index = lax.broadcasted_iota(jnp.int32, (seg_rows, width), 0).astype(jnp.float32) + 1.0
    opened = widen(mask_ref[3, 8:8 + SEGMENTS, :])
    starts = []
    powers = []
    for m in range(MODES):
        logl = logl_ref[m:m + 1, :]
        start = cl_ref[m, 0:SEGMENTS, :] + opened * jnp.exp(seg_index * (float(seg_rows) * logl)) * hin_ref[m:m + 1, :]
        starts.append(start)
        powers.append(amp_ref[m:m + 1, :] * jnp.exp(lag_index * logl))
    for p in range(SEGMENTS):
        lo = p * seg_rows
        corr = jnp.zeros((seg_rows, width), jnp.float32)
        for m in range(MODES):
            corr = corr + powers[m] * starts[m][p:p + 1, :]
        conv = acc_ref[lo:lo + seg_rows, :] + widen(mask_ref[2, lo:lo + seg_rows, :]) * corr
        out_ref[lo:lo + seg_rows, :] = (qs_ref[lo:lo + seg_rows, :] * conv).astype(out_ref.dtype)


def scan_kernel(count, spans, own_ref, fac_ref, q_ref, rim_ref, filt_ref, mask_ref, out_ref, qs_ref, sums, slots,
                send_sems, recv_sems, ext_ref):
    columns = q_ref.shape[1] // LANES
    groups = len(spans) + 1
    since = mask_ref[0]

    def filter_columns(group):
        for c in range(group * columns // groups, (group + 1) * columns // groups):
            lanes = slice(c * LANES, (c + 1) * LANES)
            qs_ref[:, lanes] = short_conv(q_ref[:, lanes], rim_ref[0, :, lanes], filt_ref[0, :, lanes], since, ext_ref)

    me = lax.axis_index("ctx")
    lane = lax.axis_index("tp")
    last = spans[-1] * 2 if spans else 1
    offsets = sorted(set(spans) | {1, 1 + last})
    barrier = pltpu.get_barrier_semaphore()
    for d in offsets:
        for other in (me - d, me + d):
            @pl.when((other >= 0) & (other < count))
            def _():
                pl.semaphore_signal(barrier, inc=1, device_id=(other, lane), device_id_type=pl.DeviceIdType.MESH)
    partners = 0
    for d in offsets:
        partners = partners + (me + count - d) // count + (2 * count - 1 - me - d) // count
    pl.semaphore_wait(barrier, partners)

    def transfer(src, slot, target):
        return pltpu.make_async_remote_copy(
            src_ref=src, dst_ref=slots.at[slot], send_sem=send_sems.at[slot], recv_sem=recv_sems.at[slot],
            device_id=(target, lane), device_id_type=pl.DeviceIdType.MESH)

    def exchange(src, sends):
        for slot, d in sends:
            @pl.when(me + d < count)
            def _():
                transfer(src, slot, me + d).start()

    def settle(src, sends):
        for slot, d in sends:
            @pl.when(me + d < count)
            def _():
                transfer(src, slot, me + d).wait_send()

    current = own_ref
    for r, d in enumerate(spans):
        exchange(current, [(r, d)])
        filter_columns(r)

        @pl.when(me - d >= 0)
        def _():
            transfer(current, r, me - d).wait_recv()
            sums[r] = current[...] + fac_ref[r] * slots[r]

        @pl.when(me - d < 0)
        def _():
            sums[r] = current[...]
        settle(current, [(r, d)])
        current = sums.at[r]
    near, far = len(spans), len(spans) + 1
    final = [(near, 1), (far, 1 + last)]
    exchange(current, final)
    filter_columns(len(spans))
    out_ref[...] = jnp.zeros(out_ref.shape, out_ref.dtype)

    @pl.when(me - 1 >= 0)
    def _():
        transfer(current, near, me - 1).wait_recv()
        out_ref[...] = slots[near]

    @pl.when(me - 1 - last >= 0)
    def _():
        transfer(current, far, me - 1 - last).wait_recv()
        out_ref[...] = out_ref[...] + fac_ref[len(spans)] * slots[far]
    settle(current, final)


def body(query_proj, key_proj, value_proj, short_filter, residues, decay_rate, skip_gain, doc_lengths):
    row_count, channels = query_proj.shape
    ctx_count = lax.axis_size("ctx")
    my_index = lax.axis_index("ctx")
    first_row = my_index * row_count
    seg_rows = row_count // SEGMENTS
    local_rows = jnp.arange(row_count, dtype=jnp.int32)
    positions = first_row + local_rows
    doc_starts = jnp.cumsum(doc_lengths) - doc_lengths
    row_start = jnp.max(
        jnp.where(doc_starts[None, :] <= positions[:, None], doc_starts[None, :], 0), axis=1
    )
    since = (positions - row_start).astype(jnp.float32)
    keep = (positions != row_start).astype(jnp.float32)
    seg_first = first_row + (local_rows // seg_rows) * seg_rows
    cont = (row_start < seg_first).astype(jnp.float32)
    seg_ids = jnp.arange(SEGMENTS, dtype=jnp.int32)
    seg_lo = first_row + seg_ids * seg_rows
    in_seg = (doc_starts[None, :] >= seg_lo[:, None]) & (doc_starts[None, :] < seg_lo[:, None] + seg_rows)
    segkeep = 1.0 - jnp.any(in_seg, axis=1).astype(jnp.float32)
    before = (doc_starts[None, :] >= first_row) & (doc_starts[None, :] < seg_lo[:, None])
    opened = 1.0 - jnp.any(before, axis=1).astype(jnp.float32)

    small = jnp.zeros((row_count,), jnp.float32).at[0:SEGMENTS].set(segkeep).at[8:8 + SEGMENTS].set(opened)
    masks = jnp.broadcast_to(jnp.stack([since, keep, cont, small])[:, :, None], (4, row_count, LANES))

    stacked = jnp.stack([query_proj, key_proj, value_proj])
    rim = from_behind(stacked[:, row_count - TAPS + 1:, :], "ctx", 1)
    log_decay = jnp.log1p(-decay_rate)
    lam = jnp.exp(log_decay)
    amp = residues * jnp.sqrt(decay_rate * (2.0 - decay_rate))
    tiles = channels // LANES
    col = lambda *lead: pl.BlockSpec(tuple(lead) + (LANES,), lambda c: (0,) * len(lead) + (c,))
    fixed = lambda *shape: pl.BlockSpec(shape, lambda c: (0,) * len(shape))
    f32 = jnp.float32
    cola = lambda *lead: pl.BlockSpec(tuple(lead) + (LANES_LOCAL,), lambda c: (0,) * len(lead) + (c,))
    acc, cl, own_state = pl.pallas_call(
        local_kernel,
        grid=(channels // LANES_LOCAL,),
        in_specs=[cola(row_count), cola(row_count), cola(3, TAPS - 1), cola(3, TAPS), cola(MODES), cola(MODES),
                  cola(1), fixed(4, row_count, LANES)],
        out_specs=[cola(row_count), cola(MODES, 16), cola(MODES)],
        out_shape=[jax.ShapeDtypeStruct((row_count, channels), f32),
                   jax.ShapeDtypeStruct((MODES, 16, channels), f32), jax.ShapeDtypeStruct((MODES, channels), f32)],
        scratch_shapes=[pltpu.VMEM((row_count + 8, LANES), f32), pltpu.VMEM((row_count, LANES), f32),
                        pltpu.VMEM((row_count, LANES), f32)],
        interpret=INTERPRET,
    )(key_proj, value_proj, rim, short_filter, amp, lam, skip_gain[None, :], masks)

    def starts_between(low_device, high_device):
        low_row = jnp.maximum(low_device, 0) * row_count
        high_row = (high_device + 1) * row_count
        return jnp.any((doc_starts >= low_row) & (doc_starts < high_row)).astype(jnp.float32)

    spans = []
    span = 1
    while 2 * span < ctx_count:
        spans.append(span)
        span *= 2
    factors = []
    for d in spans:
        open_path = 1.0 - starts_between(my_index - d + 1, my_index)
        factors.append(open_path * jnp.exp(float(d * row_count) * log_decay))
    open_path = 1.0 - starts_between(my_index - span, my_index - 1)
    factors.append(open_path * jnp.exp(float(span * row_count) * log_decay))
    factors = jnp.stack(factors)
    vmem = pl.BlockSpec(memory_space=pltpu.VMEM)
    incoming, q_short = pl.pallas_call(
        functools.partial(scan_kernel, ctx_count, tuple(spans)),
        out_shape=[jax.ShapeDtypeStruct((MODES, channels), f32), jax.ShapeDtypeStruct((row_count, channels), f32)],
        in_specs=[vmem] * 6,
        out_specs=[vmem, vmem],
        scratch_shapes=[
            pltpu.VMEM((len(spans), MODES, channels), f32),
            pltpu.VMEM((len(spans) + 2, MODES, channels), f32),
            pltpu.SemaphoreType.DMA((len(spans) + 2,)),
            pltpu.SemaphoreType.DMA((len(spans) + 2,)),
            pltpu.VMEM((row_count + 8, LANES), f32),
        ],
        compiler_params=pltpu.CompilerParams(collective_id=0, has_side_effects=True),
        interpret=INTERPRET,
    )(own_state, factors, query_proj, rim, short_filter, masks)

    wide = lambda *lead: pl.BlockSpec(tuple(lead) + (LANES_FIX,), lambda c: (0,) * len(lead) + (c,))
    return pl.pallas_call(
        fix_kernel,
        grid=(channels // LANES_FIX,),
        in_specs=[wide(row_count), wide(row_count), wide(MODES, 16), wide(MODES), wide(MODES), wide(MODES),
                  fixed(4, row_count, LANES)],
        out_specs=wide(row_count),
        out_shape=jax.ShapeDtypeStruct((row_count, channels), jnp.bfloat16),
        interpret=INTERPRET,
    )(acc, q_short, cl, incoming, amp, log_decay, masks)


def solution(mesh):
    in_specs = (
        P("ctx", "tp"),
        P("ctx", "tp"),
        P("ctx", "tp"),
        P(None, None, "tp"),
        P(None, "tp"),
        P(None, "tp"),
        P("tp"),
        P(),
    )
    out_specs = P("ctx", "tp")
    return jax.shard_map(body, mesh=mesh, in_specs=in_specs, out_specs=out_specs, check_vma=False)
```

```python
import functools

import jax
import jax.numpy as jnp
from jax import lax
from jax.experimental import pallas as pl
from jax.experimental.pallas import tpu as pltpu
from jax.sharding import PartitionSpec as P

MODES = 16
TAPS = 7
LANES = 128
LANES_FIX = 512
LANES_LOCAL = 512
SEGMENTS = 8
INTERPRET = False


def from_behind(value, axis, steps):
    count = lax.axis_size(axis)
    first, last = (max(0, -steps), min(count, count - steps))
    return lax.ppermute(value, axis, [(source, source + steps) for source in range(first, last)])


def short_conv(block, rim_rows, taps, since, ext_ref):
    rows = block.shape[0]
    ext_ref[8 - TAPS + 1:8, :] = rim_rows.astype(jnp.float32)
    ext_ref[8:8 + rows, :] = block.astype(jnp.float32)
    total = jnp.zeros((rows, LANES), jnp.float32)
    for lag in range(TAPS):
        window = ext_ref[8 - lag:8 - lag + rows, :]
        total = total + jnp.where(since >= float(lag), taps[lag:lag + 1, :] * window, 0.0)
    return total


def local_kernel(k_ref, v_ref, rim_ref, filt_ref, amp_ref, lam_ref, skip_ref, mask_ref,
                 acc_ref, cl_ref, end_ref, ext_ref, g_ref, sum_ref):
    since_ref, keep_ref = mask_ref.at[0], mask_ref.at[1]
    rows = k_ref.shape[0]
    seg_rows = rows // SEGMENTS
    since = since_ref[...]
    segkeep = mask_ref[3, 0:SEGMENTS, :]
    for c in range(k_ref.shape[1] // LANES):
        lanes = slice(c * LANES, (c + 1) * LANES)
        filtered = [short_conv(src[:, lanes], rim_ref[branch, :, lanes], filt_ref[branch, :, lanes], since, ext_ref)
                    for branch, src in ((1, k_ref), (2, v_ref))]
        g_ref[...] = (filtered[0] * filtered[1]).astype(jnp.bfloat16).astype(jnp.float32)
        lam = [jnp.broadcast_to(lam_ref[m:m + 1, lanes], (SEGMENTS, LANES)) for m in range(MODES)]
        amp = [jnp.broadcast_to(amp_ref[m:m + 1, lanes], (SEGMENTS, LANES)) for m in range(MODES)]
        skip = jnp.broadcast_to(skip_ref[:, lanes], (SEGMENTS, LANES))

        def step(j, states):
            x = g_ref[pl.ds(j, SEGMENTS, stride=seg_rows), :]
            keep = keep_ref[pl.ds(j, SEGMENTS, stride=seg_rows), :]
            new_states = [(lam[m] * keep) * states[m] + x for m in range(MODES)]
            terms = [amp[m] * new_states[m] for m in range(MODES)] + [skip * x]
            while len(terms) > 1:
                terms = [terms[i] + terms[i + 1] for i in range(0, len(terms) - 1, 2)] + terms[len(terms) - len(terms) % 2:]
            sum_ref[pl.ds(j, SEGMENTS, stride=seg_rows), :] = terms[0]
            return tuple(new_states)

        zero = jnp.zeros((SEGMENTS, LANES), jnp.float32)
        ends = lax.fori_loop(0, seg_rows, step, tuple([zero] * MODES), unroll=16)
        acc_ref[:, lanes] = sum_ref[...]
        for m in range(MODES):
            seg_decay = jnp.exp(float(seg_rows) * jnp.log(lam_ref[m:m + 1, lanes]))
            carried = jnp.zeros((1, LANES), jnp.float32)
            cl_ref[m, 0:1, lanes] = carried
            for p in range(SEGMENTS):
                carried = ends[m][p:p + 1, :] + segkeep[p:p + 1, :] * seg_decay * carried
                cl_ref[m, p + 1:p + 2, lanes] = carried
            cl_ref[m, SEGMENTS + 1:, lanes] = jnp.zeros((16 - SEGMENTS - 1, LANES), jnp.float32)
            end_ref[m:m + 1, lanes] = carried


def fix_kernel(acc_ref, qs_ref, cl_ref, hin_ref, amp_ref, logl_ref, mask_ref, out_ref):
    rows, width = acc_ref.shape
    seg_rows = rows // SEGMENTS
    copies = width // LANES
    widen = lambda part: jnp.concatenate([part] * copies, axis=1) if copies > 1 else part
    seg_index = lax.broadcasted_iota(jnp.int32, (SEGMENTS, width), 0).astype(jnp.float32)
    lag_index = lax.broadcasted_iota(jnp.int32, (seg_rows, width), 0).astype(jnp.float32) + 1.0
    opened = widen(mask_ref[3, 8:8 + SEGMENTS, :])
    starts = []
    powers = []
    for m in range(MODES):
        logl = logl_ref[m:m + 1, :]
        start = cl_ref[m, 0:SEGMENTS, :] + opened * jnp.exp(seg_index * (float(seg_rows) * logl)) * hin_ref[m:m + 1, :]
        starts.append(start)
        powers.append(amp_ref[m:m + 1, :] * jnp.exp(lag_index * logl))
    for p in range(SEGMENTS):
        lo = p * seg_rows
        corr = jnp.zeros((seg_rows, width), jnp.float32)
        for m in range(MODES):
            corr = corr + powers[m] * starts[m][p:p + 1, :]
        conv = acc_ref[lo:lo + seg_rows, :] + widen(mask_ref[2, lo:lo + seg_rows, :]) * corr
        out_ref[lo:lo + seg_rows, :] = (qs_ref[lo:lo + seg_rows, :] * conv).astype(out_ref.dtype)


def scan_kernel(count, spans, own_ref, fac_ref, q_ref, rim_ref, filt_ref, mask_ref, out_ref, qs_ref, sums, slots,
                send_sems, recv_sems, ext_ref):
    columns = q_ref.shape[1] // LANES
    groups = len(spans) + 1
    since = mask_ref[0]

    def filter_columns(group):
        for c in range(group * columns // groups, (group + 1) * columns // groups):
            lanes = slice(c * LANES, (c + 1) * LANES)
            qs_ref[:, lanes] = short_conv(q_ref[:, lanes], rim_ref[0, :, lanes], filt_ref[0, :, lanes], since, ext_ref)

    me = lax.axis_index("ctx")
    lane = lax.axis_index("tp")
    last = spans[-1] * 2 if spans else 1
    offsets = sorted(set(spans) | {1, 1 + last})
    barrier = pltpu.get_barrier_semaphore()
    for d in offsets:
        for other in (me - d, me + d):
            @pl.when((other >= 0) & (other < count))
            def _():
                pl.semaphore_signal(barrier, inc=1, device_id=(other, lane), device_id_type=pl.DeviceIdType.MESH)
    partners = 0
    for d in offsets:
        partners = partners + (me + count - d) // count + (2 * count - 1 - me - d) // count
    pl.semaphore_wait(barrier, partners)

    def transfer(src, slot, target):
        return pltpu.make_async_remote_copy(
            src_ref=src, dst_ref=slots.at[slot], send_sem=send_sems.at[slot], recv_sem=recv_sems.at[slot],
            device_id=(target, lane), device_id_type=pl.DeviceIdType.MESH)

    def exchange(src, sends):
        for slot, d in sends:
            @pl.when(me + d < count)
            def _():
                transfer(src, slot, me + d).start()

    def settle(src, sends):
        for slot, d in sends:
            @pl.when(me + d < count)
            def _():
                transfer(src, slot, me + d).wait_send()

    current = own_ref
    for r, d in enumerate(spans):
        exchange(current, [(r, d)])
        filter_columns(r)

        @pl.when(me - d >= 0)
        def _():
            transfer(current, r, me - d).wait_recv()
            sums[r] = current[...] + fac_ref[r] * slots[r]

        @pl.when(me - d < 0)
        def _():
            sums[r] = current[...]
        settle(current, [(r, d)])
        current = sums.at[r]
    near, far = len(spans), len(spans) + 1
    final = [(near, 1), (far, 1 + last)]
    exchange(current, final)
    filter_columns(len(spans))
    out_ref[...] = jnp.zeros(out_ref.shape, out_ref.dtype)

    @pl.when(me - 1 >= 0)
    def _():
        transfer(current, near, me - 1).wait_recv()
        out_ref[...] = slots[near]

    @pl.when(me - 1 - last >= 0)
    def _():
        transfer(current, far, me - 1 - last).wait_recv()
        out_ref[...] = out_ref[...] + fac_ref[len(spans)] * slots[far]
    settle(current, final)


def body(query_proj, key_proj, value_proj, short_filter, residues, decay_rate, skip_gain, doc_lengths):
    row_count, channels = query_proj.shape
    ctx_count = lax.axis_size("ctx")
    my_index = lax.axis_index("ctx")
    first_row = my_index * row_count
    seg_rows = row_count // SEGMENTS
    local_rows = jnp.arange(row_count, dtype=jnp.int32)
    positions = first_row + local_rows
    doc_starts = jnp.cumsum(doc_lengths) - doc_lengths
    row_start = jnp.max(
        jnp.where(doc_starts[None, :] <= positions[:, None], doc_starts[None, :], 0), axis=1
    )
    since = (positions - row_start).astype(jnp.float32)
    keep = (positions != row_start).astype(jnp.float32)
    seg_first = first_row + (local_rows // seg_rows) * seg_rows
    cont = (row_start < seg_first).astype(jnp.float32)
    seg_ids = jnp.arange(SEGMENTS, dtype=jnp.int32)
    seg_lo = first_row + seg_ids * seg_rows
    in_seg = (doc_starts[None, :] >= seg_lo[:, None]) & (doc_starts[None, :] < seg_lo[:, None] + seg_rows)
    segkeep = 1.0 - jnp.any(in_seg, axis=1).astype(jnp.float32)
    before = (doc_starts[None, :] >= first_row) & (doc_starts[None, :] < seg_lo[:, None])
    opened = 1.0 - jnp.any(before, axis=1).astype(jnp.float32)

    small = jnp.zeros((row_count,), jnp.float32).at[0:SEGMENTS].set(segkeep).at[8:8 + SEGMENTS].set(opened)
    masks = jnp.broadcast_to(jnp.stack([since, keep, cont, small])[:, :, None], (4, row_count, LANES))

    stacked = jnp.stack([query_proj, key_proj, value_proj])
    rim = from_behind(stacked[:, row_count - TAPS + 1:, :], "ctx", 1)
    log_decay = jnp.log1p(-decay_rate)
    lam = jnp.exp(log_decay)
    amp = residues * jnp.sqrt(decay_rate * (2.0 - decay_rate))
    tiles = channels // LANES
    col = lambda *lead: pl.BlockSpec(tuple(lead) + (LANES,), lambda c: (0,) * len(lead) + (c,))
    fixed = lambda *shape: pl.BlockSpec(shape, lambda c: (0,) * len(shape))
    f32 = jnp.float32
    cola = lambda *lead: pl.BlockSpec(tuple(lead) + (LANES_LOCAL,), lambda c: (0,) * len(lead) + (c,))
    acc, cl, own_state = pl.pallas_call(
        local_kernel,
        grid=(channels // LANES_LOCAL,),
        in_specs=[cola(row_count), cola(row_count), cola(3, TAPS - 1), cola(3, TAPS), cola(MODES), cola(MODES),
                  cola(1), fixed(4, row_count, LANES)],
        out_specs=[cola(row_count), cola(MODES, 16), cola(MODES)],
        out_shape=[jax.ShapeDtypeStruct((row_count, channels), f32),
                   jax.ShapeDtypeStruct((MODES, 16, channels), f32), jax.ShapeDtypeStruct((MODES, channels), f32)],
        scratch_shapes=[pltpu.VMEM((row_count + 8, LANES), f32), pltpu.VMEM((row_count, LANES), f32),
                        pltpu.VMEM((row_count, LANES), f32)],
        interpret=INTERPRET,
    )(key_proj, value_proj, rim, short_filter, amp, lam, skip_gain[None, :], masks)

    def starts_between(low_device, high_device):
        low_row = jnp.maximum(low_device, 0) * row_count
        high_row = (high_device + 1) * row_count
        return jnp.any((doc_starts >= low_row) & (doc_starts < high_row)).astype(jnp.float32)

    spans = []
    span = 1
    while 2 * span < ctx_count:
        spans.append(span)
        span *= 2
    factors = []
    for d in spans:
        open_path = 1.0 - starts_between(my_index - d + 1, my_index)
        factors.append(open_path * jnp.exp(float(d * row_count) * log_decay))
    open_path = 1.0 - starts_between(my_index - span, my_index - 1)
    factors.append(open_path * jnp.exp(float(span * row_count) * log_decay))
    factors = jnp.stack(factors)
    vmem = pl.BlockSpec(memory_space=pltpu.VMEM)
    incoming, q_short = pl.pallas_call(
        functools.partial(scan_kernel, ctx_count, tuple(spans)),
        out_shape=[jax.ShapeDtypeStruct((MODES, channels), f32), jax.ShapeDtypeStruct((row_count, channels), f32)],
        in_specs=[vmem] * 6,
        out_specs=[vmem, vmem],
        scratch_shapes=[
            pltpu.VMEM((len(spans), MODES, channels), f32),
            pltpu.VMEM((len(spans) + 2, MODES, channels), f32),
            pltpu.SemaphoreType.DMA((len(spans) + 2,)),
            pltpu.SemaphoreType.DMA((len(spans) + 2,)),
            pltpu.VMEM((row_count + 8, LANES), f32),
        ],
        compiler_params=pltpu.CompilerParams(collective_id=0, has_side_effects=True),
        interpret=INTERPRET,
    )(own_state, factors, query_proj, rim, short_filter, masks)

    wide = lambda *lead: pl.BlockSpec(tuple(lead) + (LANES_FIX,), lambda c: (0,) * len(lead) + (c,))
    return pl.pallas_call(
        fix_kernel,
        grid=(channels // LANES_FIX,),
        in_specs=[wide(row_count), wide(row_count), wide(MODES, 16), wide(MODES), wide(MODES), wide(MODES),
                  fixed(4, row_count, LANES)],
        out_specs=wide(row_count),
        out_shape=jax.ShapeDtypeStruct((row_count, channels), jnp.bfloat16),
        interpret=INTERPRET,
    )(acc, q_short, cl, incoming, amp, log_decay, masks)


def solution(mesh):
    in_specs = (
        P("ctx", "tp"),
        P("ctx", "tp"),
        P("ctx", "tp"),
        P(None, None, "tp"),
        P(None, "tp"),
        P(None, "tp"),
        P("tp"),
        P(),
    )
    out_specs = P("ctx", "tp")
    return jax.shard_map(body, mesh=mesh, in_specs=in_specs, out_specs=out_specs, check_vma=False)
```

```python
import functools

import jax
import jax.numpy as jnp
from jax import lax
from jax.experimental import pallas as pl
from jax.experimental.pallas import tpu as pltpu
from jax.sharding import PartitionSpec as P

MODES = 16
TAPS = 7
LANES = 128
LANES_FIX = 512
LANES_LOCAL = 512
SEGMENTS = 8
INTERPRET = False


def from_behind(value, axis, steps):
    count = lax.axis_size(axis)
    first, last = (max(0, -steps), min(count, count - steps))
    return lax.ppermute(value, axis, [(source, source + steps) for source in range(first, last)])


def short_conv(block, rim_rows, taps, since, ext_ref):
    rows = block.shape[0]
    ext_ref[8 - TAPS + 1:8, :] = rim_rows.astype(jnp.float32)
    ext_ref[8:8 + rows, :] = block.astype(jnp.float32)
    total = jnp.zeros((rows, LANES), jnp.float32)
    for lag in range(TAPS):
        window = ext_ref[8 - lag:8 - lag + rows, :]
        total = total + jnp.where(since >= float(lag), taps[lag:lag + 1, :] * window, 0.0)
    return total


def local_kernel(k_ref, v_ref, rim_ref, filt_ref, amp_ref, lam_ref, skip_ref, mask_ref,
                 acc_ref, cl_ref, end_ref, ext_ref, g_ref, sum_ref):
    since_ref, keep_ref = mask_ref.at[0], mask_ref.at[1]
    rows = k_ref.shape[0]
    seg_rows = rows // SEGMENTS
    since = since_ref[...]
    segkeep = mask_ref[3, 0:SEGMENTS, :]
    for c in range(k_ref.shape[1] // LANES):
        lanes = slice(c * LANES, (c + 1) * LANES)
        filtered = [short_conv(src[:, lanes], rim_ref[branch, :, lanes], filt_ref[branch, :, lanes], since, ext_ref)
                    for branch, src in ((1, k_ref), (2, v_ref))]
        g_ref[...] = (filtered[0] * filtered[1]).astype(jnp.bfloat16).astype(jnp.float32)
        lam = [jnp.broadcast_to(lam_ref[m:m + 1, lanes], (SEGMENTS, LANES)) for m in range(MODES)]
        amp = [jnp.broadcast_to(amp_ref[m:m + 1, lanes], (SEGMENTS, LANES)) for m in range(MODES)]
        skip = jnp.broadcast_to(skip_ref[:, lanes], (SEGMENTS, LANES))

        def step(j, states):
            x = g_ref[pl.ds(j, SEGMENTS, stride=seg_rows), :]
            keep = keep_ref[pl.ds(j, SEGMENTS, stride=seg_rows), :]
            new_states = [(lam[m] * keep) * states[m] + x for m in range(MODES)]
            terms = [amp[m] * new_states[m] for m in range(MODES)] + [skip * x]
            while len(terms) > 1:
                terms = [terms[i] + terms[i + 1] for i in range(0, len(terms) - 1, 2)] + terms[len(terms) - len(terms) % 2:]
            sum_ref[pl.ds(j, SEGMENTS, stride=seg_rows), :] = terms[0]
            return tuple(new_states)

        zero = jnp.zeros((SEGMENTS, LANES), jnp.float32)
        ends = lax.fori_loop(0, seg_rows, step, tuple([zero] * MODES), unroll=32)
        acc_ref[:, lanes] = sum_ref[...]
        for m in range(MODES):
            seg_decay = jnp.exp(float(seg_rows) * jnp.log(lam_ref[m:m + 1, lanes]))
            carried = jnp.zeros((1, LANES), jnp.float32)
            cl_ref[m, 0:1, lanes] = carried
            for p in range(SEGMENTS):
                carried = ends[m][p:p + 1, :] + segkeep[p:p + 1, :] * seg_decay * carried
                cl_ref[m, p + 1:p + 2, lanes] = carried
            cl_ref[m, SEGMENTS + 1:, lanes] = jnp.zeros((16 - SEGMENTS - 1, LANES), jnp.float32)
            end_ref[m:m + 1, lanes] = carried


def fix_kernel(acc_ref, qs_ref, cl_ref, hin_ref, amp_ref, logl_ref, mask_ref, out_ref):
    rows, width = acc_ref.shape
    seg_rows = rows // SEGMENTS
    copies = width // LANES
    widen = lambda part: jnp.concatenate([part] * copies, axis=1) if copies > 1 else part
    seg_index = lax.broadcasted_iota(jnp.int32, (SEGMENTS, width), 0).astype(jnp.float32)
    lag_index = lax.broadcasted_iota(jnp.int32, (seg_rows, width), 0).astype(jnp.float32) + 1.0
    opened = widen(mask_ref[3, 8:8 + SEGMENTS, :])
    starts = []
    powers = []
    for m in range(MODES):
        logl = logl_ref[m:m + 1, :]
        start = cl_ref[m, 0:SEGMENTS, :] + opened * jnp.exp(seg_index * (float(seg_rows) * logl)) * hin_ref[m:m + 1, :]
        starts.append(start)
        powers.append(amp_ref[m:m + 1, :] * jnp.exp(lag_index * logl))
    for p in range(SEGMENTS):
        lo = p * seg_rows
        corr = jnp.zeros((seg_rows, width), jnp.float32)
        for m in range(MODES):
            corr = corr + powers[m] * starts[m][p:p + 1, :]
        conv = acc_ref[lo:lo + seg_rows, :] + widen(mask_ref[2, lo:lo + seg_rows, :]) * corr
        out_ref[lo:lo + seg_rows, :] = (qs_ref[lo:lo + seg_rows, :] * conv).astype(out_ref.dtype)


def scan_kernel(count, spans, own_ref, fac_ref, q_ref, rim_ref, filt_ref, mask_ref, out_ref, qs_ref, sums, slots,
                send_sems, recv_sems, ext_ref):
    columns = q_ref.shape[1] // LANES
    groups = len(spans) + 1
    since = mask_ref[0]

    def filter_columns(group):
        for c in range(group * columns // groups, (group + 1) * columns // groups):
            lanes = slice(c * LANES, (c + 1) * LANES)
            qs_ref[:, lanes] = short_conv(q_ref[:, lanes], rim_ref[0, :, lanes], filt_ref[0, :, lanes], since, ext_ref)

    me = lax.axis_index("ctx")
    lane = lax.axis_index("tp")
    last = spans[-1] * 2 if spans else 1
    offsets = sorted(set(spans) | {1, 1 + last})
    barrier = pltpu.get_barrier_semaphore()
    for d in offsets:
        for other in (me - d, me + d):
            @pl.when((other >= 0) & (other < count))
            def _():
                pl.semaphore_signal(barrier, inc=1, device_id=(other, lane), device_id_type=pl.DeviceIdType.MESH)
    partners = 0
    for d in offsets:
        partners = partners + (me + count - d) // count + (2 * count - 1 - me - d) // count
    pl.semaphore_wait(barrier, partners)

    def transfer(src, slot, target):
        return pltpu.make_async_remote_copy(
            src_ref=src, dst_ref=slots.at[slot], send_sem=send_sems.at[slot], recv_sem=recv_sems.at[slot],
            device_id=(target, lane), device_id_type=pl.DeviceIdType.MESH)

    def exchange(src, sends):
        for slot, d in sends:
            @pl.when(me + d < count)
            def _():
                transfer(src, slot, me + d).start()

    def settle(src, sends):
        for slot, d in sends:
            @pl.when(me + d < count)
            def _():
                transfer(src, slot, me + d).wait_send()

    current = own_ref
    for r, d in enumerate(spans):
        exchange(current, [(r, d)])
        filter_columns(r)

        @pl.when(me - d >= 0)
        def _():
            transfer(current, r, me - d).wait_recv()
            sums[r] = current[...] + fac_ref[r] * slots[r]

        @pl.when(me - d < 0)
        def _():
            sums[r] = current[...]
        settle(current, [(r, d)])
        current = sums.at[r]
    near, far = len(spans), len(spans) + 1
    final = [(near, 1), (far, 1 + last)]
    exchange(current, final)
    filter_columns(len(spans))
    out_ref[...] = jnp.zeros(out_ref.shape, out_ref.dtype)

    @pl.when(me - 1 >= 0)
    def _():
        transfer(current, near, me - 1).wait_recv()
        out_ref[...] = slots[near]

    @pl.when(me - 1 - last >= 0)
    def _():
        transfer(current, far, me - 1 - last).wait_recv()
        out_ref[...] = out_ref[...] + fac_ref[len(spans)] * slots[far]
    settle(current, final)


def body(query_proj, key_proj, value_proj, short_filter, residues, decay_rate, skip_gain, doc_lengths):
    row_count, channels = query_proj.shape
    ctx_count = lax.axis_size("ctx")
    my_index = lax.axis_index("ctx")
    first_row = my_index * row_count
    seg_rows = row_count // SEGMENTS
    local_rows = jnp.arange(row_count, dtype=jnp.int32)
    positions = first_row + local_rows
    doc_starts = jnp.cumsum(doc_lengths) - doc_lengths
    row_start = jnp.max(
        jnp.where(doc_starts[None, :] <= positions[:, None], doc_starts[None, :], 0), axis=1
    )
    since = (positions - row_start).astype(jnp.float32)
    keep = (positions != row_start).astype(jnp.float32)
    seg_first = first_row + (local_rows // seg_rows) * seg_rows
    cont = (row_start < seg_first).astype(jnp.float32)
    seg_ids = jnp.arange(SEGMENTS, dtype=jnp.int32)
    seg_lo = first_row + seg_ids * seg_rows
    in_seg = (doc_starts[None, :] >= seg_lo[:, None]) & (doc_starts[None, :] < seg_lo[:, None] + seg_rows)
    segkeep = 1.0 - jnp.any(in_seg, axis=1).astype(jnp.float32)
    before = (doc_starts[None, :] >= first_row) & (doc_starts[None, :] < seg_lo[:, None])
    opened = 1.0 - jnp.any(before, axis=1).astype(jnp.float32)

    small = jnp.zeros((row_count,), jnp.float32).at[0:SEGMENTS].set(segkeep).at[8:8 + SEGMENTS].set(opened)
    masks = jnp.broadcast_to(jnp.stack([since, keep, cont, small])[:, :, None], (4, row_count, LANES))

    stacked = jnp.stack([query_proj, key_proj, value_proj])
    rim = from_behind(stacked[:, row_count - TAPS + 1:, :], "ctx", 1)
    log_decay = jnp.log1p(-decay_rate)
    lam = jnp.exp(log_decay)
    amp = residues * jnp.sqrt(decay_rate * (2.0 - decay_rate))
    tiles = channels // LANES
    col = lambda *lead: pl.BlockSpec(tuple(lead) + (LANES,), lambda c: (0,) * len(lead) + (c,))
    fixed = lambda *shape: pl.BlockSpec(shape, lambda c: (0,) * len(shape))
    f32 = jnp.float32
    cola = lambda *lead: pl.BlockSpec(tuple(lead) + (LANES_LOCAL,), lambda c: (0,) * len(lead) + (c,))
    acc, cl, own_state = pl.pallas_call(
        local_kernel,
        grid=(channels // LANES_LOCAL,),
        in_specs=[cola(row_count), cola(row_count), cola(3, TAPS - 1), cola(3, TAPS), cola(MODES), cola(MODES),
                  cola(1), fixed(4, row_count, LANES)],
        out_specs=[cola(row_count), cola(MODES, 16), cola(MODES)],
        out_shape=[jax.ShapeDtypeStruct((row_count, channels), f32),
                   jax.ShapeDtypeStruct((MODES, 16, channels), f32), jax.ShapeDtypeStruct((MODES, channels), f32)],
        scratch_shapes=[pltpu.VMEM((row_count + 8, LANES), f32), pltpu.VMEM((row_count, LANES), f32),
                        pltpu.VMEM((row_count, LANES), f32)],
        interpret=INTERPRET,
    )(key_proj, value_proj, rim, short_filter, amp, lam, skip_gain[None, :], masks)

    def starts_between(low_device, high_device):
        low_row = jnp.maximum(low_device, 0) * row_count
        high_row = (high_device + 1) * row_count
        return jnp.any((doc_starts >= low_row) & (doc_starts < high_row)).astype(jnp.float32)

    spans = []
    span = 1
    while 2 * span < ctx_count:
        spans.append(span)
        span *= 2
    factors = []
    for d in spans:
        open_path = 1.0 - starts_between(my_index - d + 1, my_index)
        factors.append(open_path * jnp.exp(float(d * row_count) * log_decay))
    open_path = 1.0 - starts_between(my_index - span, my_index - 1)
    factors.append(open_path * jnp.exp(float(span * row_count) * log_decay))
    factors = jnp.stack(factors)
    vmem = pl.BlockSpec(memory_space=pltpu.VMEM)
    incoming, q_short = pl.pallas_call(
        functools.partial(scan_kernel, ctx_count, tuple(spans)),
        out_shape=[jax.ShapeDtypeStruct((MODES, channels), f32), jax.ShapeDtypeStruct((row_count, channels), f32)],
        in_specs=[vmem] * 6,
        out_specs=[vmem, vmem],
        scratch_shapes=[
            pltpu.VMEM((len(spans), MODES, channels), f32),
            pltpu.VMEM((len(spans) + 2, MODES, channels), f32),
            pltpu.SemaphoreType.DMA((len(spans) + 2,)),
            pltpu.SemaphoreType.DMA((len(spans) + 2,)),
            pltpu.VMEM((row_count + 8, LANES), f32),
        ],
        compiler_params=pltpu.CompilerParams(collective_id=0, has_side_effects=True),
        interpret=INTERPRET,
    )(own_state, factors, query_proj, rim, short_filter, masks)

    wide = lambda *lead: pl.BlockSpec(tuple(lead) + (LANES_FIX,), lambda c: (0,) * len(lead) + (c,))
    return pl.pallas_call(
        fix_kernel,
        grid=(channels // LANES_FIX,),
        in_specs=[wide(row_count), wide(row_count), wide(MODES, 16), wide(MODES), wide(MODES), wide(MODES),
                  fixed(4, row_count, LANES)],
        out_specs=wide(row_count),
        out_shape=jax.ShapeDtypeStruct((row_count, channels), jnp.bfloat16),
        interpret=INTERPRET,
    )(acc, q_short, cl, incoming, amp, log_decay, masks)


def solution(mesh):
    in_specs = (
        P("ctx", "tp"),
        P("ctx", "tp"),
        P("ctx", "tp"),
        P(None, None, "tp"),
        P(None, "tp"),
        P(None, "tp"),
        P("tp"),
        P(),
    )
    out_specs = P("ctx", "tp")
    return jax.shard_map(body, mesh=mesh, in_specs=in_specs, out_specs=out_specs, check_vma=False)
```
